256 devices in a mesh: freq: 32 (over z, y), row: 2 (over x_lo), col: 4 (over x_hi, core).
Axes of the slice: x: 4 (x_hi: 2, x_lo: 2; x = x_hi * 2 + x_lo), y: 4, z: 8, core: 2. Of those that a mesh axis runs over, the one named last changes fastest.
Arguments:
- samples: int32 [2, 2048, 68608], P(None, ('row', 'col', 'freq')), may hold values from -7 to 7
- input_gains: float32 [2048], P(('row', 'col', 'freq')), may hold values from 0.3 to 3
- filter_taps: float32 [4, 1024], replicated, may hold values from 0.25 to 1
Outputs:
- vis_real: bfloat16 [128, 2048, 2048], P('freq', 'row', 'col')
- vis_imag: bfloat16 [128, 2048, 2048], P('freq', 'row', 'col')
The draws below stay inside these ranges and needn't reach their ends.
All inputs are finite; a program needn't handle non-finite values.
Results may differ from the reference program's by a relative error of at most 0.0065.
Values may be sent and summed in bfloat16 or wider, within the bound.
A program may use at most 64 MiB of HBM per device.

```python
import math
import jax
import jax.numpy as jnp
from jax import lax

INPUTS = 2048
NFFT = 1024
TAPS = 4
SPEC = 64
BAND = 128
NSAMP = 68608


def plant(entries, own_key, smallest, largest):
    spot = [jax.random.randint(jax.random.fold_in(own_key, axis), (), 0, length) for axis, length in enumerate(entries.shape)]
    main_axis = entries.shape.index(max(entries.shape))
    neighbour = spot[:main_axis] + [(spot[main_axis] + 1) % entries.shape[main_axis]] + spot[main_axis + 1:]
    return entries.at[tuple(spot)].set(smallest).at[tuple(neighbour)].set(largest)


def levels(stream_key, dims, pieces, low, high):
    loudness, own = 1.0, jax.random.fold_in(stream_key, 6)
    for dim, shards_of in pieces:
        heights = jnp.exp(jax.random.uniform(jax.random.fold_in(own, dim), (shards_of,), jnp.float32, low / len(pieces), high / len(pieces)))
        loudness = loudness * jnp.repeat(heights, dims[dim] // shards_of).reshape([-1 if axis == dim else 1 for axis in range(len(dims))])
    return loudness


def setup_inputs(seed: int = 0) -> dict:
    seeds = jax.random.split(jax.random.key(seed), 4)
    return {
        "samples": plant(jax.random.randint(seeds[0], (2, INPUTS, NSAMP), -7, 8), jax.random.fold_in(seeds[0], 1), -7, 7).astype(jnp.int32),
        "input_gains": jnp.clip(jnp.exp(math.log(3.0) - 2.3025851 * jax.random.uniform(seeds[1], (INPUTS,), jnp.float32) ** levels(seeds[1], (INPUTS,), ((0, 256),), -0.2, 0.2)), 0.3, 3.0),
        "filter_taps": jnp.clip(jax.random.uniform(seeds[2], (TAPS, NFFT), jnp.float32, 0.25, 1.0), 0.25, 1.0),
    }


def dft_table(channels):
    position = jnp.arange(NFFT, dtype=jnp.int32)
    channel = jnp.arange(channels, dtype=jnp.int32)
    phases = (position[:, None] * channel[None, :] % NFFT).astype(jnp.float32) * (2.0 * math.pi / NFFT)
    scaling = 0.5 / math.sqrt(NFFT)
    cosine = jnp.cos(phases) * scaling
    sine = jnp.sin(phases) * scaling
    real_rows = jnp.stack([cosine, -sine], axis=1)
    imag_rows = jnp.stack([sine, cosine], axis=1)
    return jnp.stack([real_rows, imag_rows], axis=0).astype(jnp.bfloat16)

def reference(samples, input_gains, filter_taps):
    table_values = dft_table(BAND).astype(jnp.float32)
    count = INPUTS // 64

    def one_block(block_index):
        start = (block_index * 64).astype(jnp.int32)
        segment = lax.dynamic_slice_in_dim(samples, start, 64, 1)
        block_gains = lax.dynamic_slice_in_dim(input_gains, start, 64, 0)
        voltage = segment.astype(jnp.float32) * 0.25 * block_gains[None, :, None]
        frames = voltage.reshape(2, 64, SPEC + TAPS - 1, NFFT)
        filtered = frames[:, :, 0:SPEC, :] * filter_taps[0]
        for tap_index in range(1, TAPS):
            filtered = filtered + frames[:, :, tap_index:tap_index + SPEC, :] * filter_taps[tap_index]
        filtered = filtered.astype(jnp.bfloat16)
        spectra = jnp.einsum('pimn,pnqk->kiqm', filtered.astype(jnp.float32), table_values)
        return spectra.reshape(BAND, 64, 2 * SPEC).astype(jnp.bfloat16)
    blocks = lax.map(one_block, jnp.arange(count, dtype=jnp.int32))
    spectra = jnp.transpose(blocks, (1, 0, 2, 3)).reshape(BAND, INPUTS, 2 * SPEC)

    def one_channel(channel_data):
        rotated = jnp.concatenate([-channel_data[:, SPEC:], channel_data[:, :SPEC]], axis=1)
        real_part = jnp.dot(channel_data, channel_data.T, preferred_element_type=jnp.float32) * (1.0 / SPEC)
        imag_part = jnp.dot(channel_data, rotated.T, preferred_element_type=jnp.float32) * (1.0 / SPEC)
        return (real_part.astype(jnp.bfloat16), imag_part.astype(jnp.bfloat16))
    vis_real, vis_imag = lax.map(one_channel, spectra)
    return (vis_real, vis_imag)
```

```python
import math

import numpy as np

import jax
import jax.numpy as jnp
from jax import lax
from jax.experimental import pallas as pl
from jax.experimental.pallas import tpu as pltpu
from jax.sharding import PartitionSpec as P

NFFT = 1024
TAPS = 4
SPEC = 64
CH_DEV = 4


def dft_table_np(channels):
    position = np.arange(NFFT, dtype=np.int64)
    channel = np.arange(channels, dtype=np.int64)
    phases = (position[:, None] * channel[None, :] % NFFT).astype(np.float64) * (2.0 * math.pi / NFFT)
    scaling = 0.5 / math.sqrt(NFFT)
    cosine = np.cos(phases) * scaling
    sine = np.sin(phases) * scaling
    real_rows = np.stack([cosine, -sine], axis=1)
    imag_rows = np.stack([sine, cosine], axis=1)
    table = np.stack([real_rows, imag_rows], axis=0).reshape(2, NFFT, 2 * channels)
    return jnp.asarray(table, dtype=jnp.bfloat16)


def pfb_dft_kernel(g_ref, taps_ref, s_ref, tab_ref, o_ref, acc_ref, f_ref):
    p = pl.program_id(0)
    inputs_here = s_ref.shape[1]
    scale = g_ref[...] * 0.25

    def frame(m, carry):
        total = None
        for t in range(TAPS):
            start = pl.multiple_of((m + t) * NFFT, NFFT)
            volts = s_ref[0, :, pl.ds(start, NFFT)].astype(jnp.float32) * scale
            term = volts * taps_ref[t : t + 1, :]
            total = term if total is None else total + term
        row = pl.multiple_of(m * inputs_here, inputs_here)
        f_ref[pl.ds(row, inputs_here), :] = total
        return carry

    lax.fori_loop(0, SPEC, frame, 0)
    prod = jnp.dot(
        f_ref[...].astype(jnp.bfloat16), tab_ref[0], preferred_element_type=jnp.float32
    )

    @pl.when(p == 0)
    def _():
        acc_ref[...] = prod

    @pl.when(p == 1)
    def _():
        o_ref[...] = (acc_ref[...] + prod).astype(o_ref.dtype)


def pfb_dft(samples, gains, taps, table):
    inputs_here, nsamp = samples.shape[1], samples.shape[2]
    width = table.shape[2]
    rows = SPEC * inputs_here
    return pl.pallas_call(
        pfb_dft_kernel,
        grid=(2,),
        out_shape=jax.ShapeDtypeStruct((rows, width), jnp.bfloat16),
        in_specs=[
            pl.BlockSpec((inputs_here, 1), lambda p: (0, 0)),
            pl.BlockSpec((TAPS, NFFT), lambda p: (0, 0)),
            pl.BlockSpec((1, inputs_here, nsamp), lambda p: (p, 0, 0)),
            pl.BlockSpec((1, NFFT, width), lambda p: (p, 0, 0)),
        ],
        out_specs=pl.BlockSpec((rows, width), lambda p: (0, 0)),
        scratch_shapes=[
            pltpu.VMEM((rows, width), jnp.float32),
            pltpu.VMEM((rows, NFFT), jnp.float32),
        ],
        compiler_params=pltpu.CompilerParams(vmem_limit_bytes=48 * 1024 * 1024),
    )(gains.reshape(inputs_here, 1), taps, samples, table)


def local(samples, input_gains, filter_taps):
    channels = CH_DEV * lax.axis_size("freq")
    inputs_here = samples.shape[1]
    table = dft_table_np(channels)
    flat = pfb_dft(samples, input_gains, filter_taps, table)
    spectra = flat.reshape(SPEC, inputs_here, 2, channels).transpose(3, 1, 2, 0)
    spectra = spectra.reshape(channels, inputs_here, 2 * SPEC)
    grouped = lax.all_to_all(spectra, "freq", split_axis=0, concat_axis=1, tiled=True)
    row_data = lax.all_gather(grouped, "col", axis=1, tiled=True)
    r = lax.axis_index("row")
    c = lax.axis_index("col")
    half = row_data.shape[1] // 2
    own_half = lax.dynamic_slice_in_dim(row_data, (c % 2) * half, half, 1)
    col_count = lax.axis_size("col")
    pairs = []
    for cc in range(col_count):
        rr = cc // 2
        pairs.append((rr * col_count + cc, (1 - rr) * col_count + cc))
    moved = lax.ppermute(own_half, ("row", "col"), pairs)
    column_data = jnp.where(c // 2 == r, own_half, moved)
    rotated = jnp.concatenate([-column_data[:, :, SPEC:], column_data[:, :, :SPEC]], axis=2)
    vis_real = (
        jnp.einsum("kim,kjm->kij", row_data, column_data, preferred_element_type=jnp.float32)
        * (1.0 / SPEC)
    ).astype(jnp.bfloat16)
    vis_imag = (
        jnp.einsum("kim,kjm->kij", row_data, rotated, preferred_element_type=jnp.float32)
        * (1.0 / SPEC)
    ).astype(jnp.bfloat16)
    return (vis_real, vis_imag)


def solution(mesh):
    placed = (P(None, ("row", "col", "freq"), None), P(("row", "col", "freq")), P())
    return jax.shard_map(
        local,
        mesh=mesh,
        in_specs=placed,
        out_specs=(P("freq", "row", "col"), P("freq", "row", "col")),
        check_vma=False,
    )
```

```python
import math

import numpy as np

import jax
import jax.numpy as jnp
from jax import lax
from jax.experimental import pallas as pl
from jax.experimental.pallas import tpu as pltpu
from jax.sharding import PartitionSpec as P

NFFT = 1024
TAPS = 4
SPEC = 64
CH_DEV = 4


def dft_table_np(channels):
    position = np.arange(NFFT, dtype=np.int64)
    channel = np.arange(channels, dtype=np.int64)
    phases = (position[:, None] * channel[None, :] % NFFT).astype(np.float64) * (2.0 * math.pi / NFFT)
    scaling = 0.5 / math.sqrt(NFFT)
    cosine = np.cos(phases) * scaling
    sine = np.sin(phases) * scaling
    real_rows = np.stack([cosine, -sine], axis=1)
    imag_rows = np.stack([sine, cosine], axis=1)
    table = np.stack([real_rows, imag_rows], axis=0).reshape(2, NFFT, 2 * channels)
    return jnp.asarray(table, dtype=jnp.bfloat16)


def pfb_dft_kernel(g_ref, taps_ref, s_ref, tab_ref, o_ref, acc_ref, f_ref):
    p = pl.program_id(0)
    inputs_here = s_ref.shape[1]
    scale = g_ref[...] * 0.25

    def frame(m, carry):
        total = None
        for t in range(TAPS):
            start = pl.multiple_of((m + t) * NFFT, NFFT)
            volts = s_ref[0, :, pl.ds(start, NFFT)].astype(jnp.float32) * scale
            term = volts * taps_ref[t : t + 1, :]
            total = term if total is None else total + term
        row = pl.multiple_of(m * inputs_here, inputs_here)
        f_ref[pl.ds(row, inputs_here), :] = total
        return carry

    lax.fori_loop(0, SPEC, frame, 0)
    prod = jnp.dot(
        f_ref[...].astype(jnp.bfloat16), tab_ref[0], preferred_element_type=jnp.float32
    )

    @pl.when(p == 0)
    def _():
        acc_ref[...] = prod

    @pl.when(p == 1)
    def _():
        o_ref[...] = (acc_ref[...] + prod).astype(o_ref.dtype)


def pfb_dft(samples, gains, taps, table):
    inputs_here, nsamp = samples.shape[1], samples.shape[2]
    width = table.shape[2]
    rows = SPEC * inputs_here
    return pl.pallas_call(
        pfb_dft_kernel,
        grid=(2,),
        out_shape=jax.ShapeDtypeStruct((rows, width), jnp.bfloat16),
        in_specs=[
            pl.BlockSpec((inputs_here, 1), lambda p: (0, 0)),
            pl.BlockSpec((TAPS, NFFT), lambda p: (0, 0)),
            pl.BlockSpec((1, inputs_here, nsamp), lambda p: (p, 0, 0)),
            pl.BlockSpec((1, NFFT, width), lambda p: (p, 0, 0)),
        ],
        out_specs=pl.BlockSpec((rows, width), lambda p: (0, 0)),
        scratch_shapes=[
            pltpu.VMEM((rows, width), jnp.float32),
            pltpu.VMEM((rows, NFFT), jnp.float32),
        ],
        compiler_params=pltpu.CompilerParams(vmem_limit_bytes=48 * 1024 * 1024),
    )(gains.reshape(inputs_here, 1), taps, samples, table)


MESH = pl.DeviceIdType.MESH


def turn_kernel(spec_ref, row_ref, col_ref, send1, recv1, own_sem, send2, recv2, recvx, local_sem):
    nf = spec_ref.shape[0]
    ncol = row_ref.shape[0]
    f = lax.axis_index("freq")
    r = lax.axis_index("row")
    c = lax.axis_index("col")
    cross_c = 2 * r + c // 2
    crossing = (c // 2) != r

    barrier = pltpu.get_barrier_semaphore()

    def greet_freq(d, carry):
        pl.semaphore_signal(barrier, inc=1, device_id=((f + d) % nf, r, c), device_id_type=MESH)
        return carry

    lax.fori_loop(1, nf, greet_freq, 0)
    for d in range(1, ncol):
        pl.semaphore_signal(barrier, inc=1, device_id=(f, r, (c + d) % ncol), device_id_type=MESH)
    pl.semaphore_signal(barrier, inc=1, device_id=(f, 1 - r, cross_c), device_id_type=MESH)

    @pl.when(crossing)
    def _():
        for e in range(2):
            pl.semaphore_signal(
                barrier, inc=1, device_id=(f, 1 - r, 2 * (c % 2) + e), device_id_type=MESH
            )

    pl.semaphore_wait(barrier, (nf - 1) + (ncol - 1) + 1 + 2 * crossing.astype(jnp.int32))

    own = pltpu.make_async_copy(spec_ref.at[f], row_ref.at[c, f], own_sem)
    own.start()

    def send_freq(d, carry):
        dest = (f + d) % nf
        pltpu.make_async_remote_copy(
            src_ref=spec_ref.at[dest],
            dst_ref=row_ref.at[c, f],
            send_sem=send1.at[d],
            recv_sem=recv1.at[f],
            device_id=(dest, r, c),
            device_id_type=MESH,
        ).start()
        return carry

    lax.fori_loop(1, nf, send_freq, 0)

    def recv_freq(d, carry):
        src = (f + nf - d) % nf
        pltpu.make_async_remote_copy(
            src_ref=spec_ref.at[src],
            dst_ref=row_ref.at[c, src],
            send_sem=send1.at[d],
            recv_sem=recv1.at[src],
            device_id=(src, r, c),
            device_id_type=MESH,
        ).wait_recv()
        return carry

    lax.fori_loop(1, nf, recv_freq, 0)
    own.wait()

    sends2 = []
    for d in range(1, ncol):
        cp = pltpu.make_async_remote_copy(
            src_ref=row_ref.at[c],
            dst_ref=row_ref.at[c],
            send_sem=send2.at[d],
            recv_sem=recv2.at[c],
            device_id=(f, r, (c + d) % ncol),
            device_id_type=MESH,
        )
        cp.start()
        sends2.append(cp)
    cross = pltpu.make_async_remote_copy(
        src_ref=row_ref.at[c],
        dst_ref=col_ref.at[c % 2],
        send_sem=send2.at[0],
        recv_sem=recvx.at[c % 2],
        device_id=(f, 1 - r, cross_c),
        device_id_type=MESH,
    )
    cross.start()

    for d in range(1, ncol):
        src = (c + ncol - d) % ncol
        pltpu.make_async_remote_copy(
            src_ref=row_ref.at[src],
            dst_ref=row_ref.at[src],
            send_sem=send2.at[d],
            recv_sem=recv2.at[src],
            device_id=(f, r, src),
            device_id_type=MESH,
        ).wait_recv()

    @pl.when(crossing)
    def _():
        for e in range(2):
            pltpu.make_async_remote_copy(
                src_ref=row_ref.at[e],
                dst_ref=col_ref.at[e],
                send_sem=send2.at[0],
                recv_sem=recvx.at[e],
                device_id=(f, 1 - r, 2 * (c % 2) + e),
                device_id_type=MESH,
            ).wait_recv()

    @pl.when(jnp.logical_not(crossing))
    def _():
        half = pltpu.make_async_copy(row_ref.at[pl.ds(2 * (c % 2), 2)], col_ref, local_sem)
        half.start()
        half.wait()

    def wait_send_freq(d, carry):
        dest = (f + d) % nf
        pltpu.make_async_remote_copy(
            src_ref=spec_ref.at[dest],
            dst_ref=row_ref.at[c, f],
            send_sem=send1.at[d],
            recv_sem=recv1.at[f],
            device_id=(dest, r, c),
            device_id_type=MESH,
        ).wait_send()
        return carry

    lax.fori_loop(1, nf, wait_send_freq, 0)
    for cp in sends2:
        cp.wait_send()
    cross.wait_send()


def corner_turn(spec):
    nf, rows, width = spec.shape
    ncol = lax.axis_size("col")
    vmem = pltpu.MemorySpace.VMEM
    return pl.pallas_call(
        turn_kernel,
        out_shape=(
            jax.ShapeDtypeStruct((ncol, nf, rows, width), spec.dtype),
            jax.ShapeDtypeStruct((2, nf, rows, width), spec.dtype),
        ),
        in_specs=[pl.BlockSpec(memory_space=vmem)],
        out_specs=(pl.BlockSpec(memory_space=vmem), pl.BlockSpec(memory_space=vmem)),
        scratch_shapes=[
            pltpu.SemaphoreType.DMA((nf,)),
            pltpu.SemaphoreType.DMA((nf,)),
            pltpu.SemaphoreType.DMA,
            pltpu.SemaphoreType.DMA((ncol,)),
            pltpu.SemaphoreType.DMA((ncol,)),
            pltpu.SemaphoreType.DMA((2,)),
            pltpu.SemaphoreType.DMA,
        ],
        compiler_params=pltpu.CompilerParams(collective_id=0, has_side_effects=True),
    )(spec)


def local(samples, input_gains, filter_taps):
    nf = lax.axis_size("freq")
    channels = CH_DEV * nf
    inputs_here = samples.shape[1]
    table = dft_table_np(channels)
    flat = pfb_dft(samples, input_gains, filter_taps, table)
    spec = flat.reshape(SPEC, inputs_here, 2, nf, CH_DEV).transpose(3, 4, 1, 2, 0)
    spec = spec.reshape(nf, CH_DEV * inputs_here, 2 * SPEC)
    row_blk, col_blk = corner_turn(spec)
    row_data = row_blk.reshape(-1, nf, CH_DEV, inputs_here, 2 * SPEC).transpose(2, 0, 1, 3, 4)
    row_data = row_data.reshape(CH_DEV, -1, 2 * SPEC)
    column_data = col_blk.reshape(2, nf, CH_DEV, inputs_here, 2 * SPEC).transpose(2, 0, 1, 3, 4)
    column_data = column_data.reshape(CH_DEV, -1, 2 * SPEC)
    rotated = jnp.concatenate([-column_data[:, :, SPEC:], column_data[:, :, :SPEC]], axis=2)
    vis_real = (
        jnp.einsum("kim,kjm->kij", row_data, column_data, preferred_element_type=jnp.float32)
        * (1.0 / SPEC)
    ).astype(jnp.bfloat16)
    vis_imag = (
        jnp.einsum("kim,kjm->kij", row_data, rotated, preferred_element_type=jnp.float32)
        * (1.0 / SPEC)
    ).astype(jnp.bfloat16)
    return (vis_real, vis_imag)


def solution(mesh):
    placed = (P(None, ("row", "col", "freq"), None), P(("row", "col", "freq")), P())
    return jax.shard_map(
        local,
        mesh=mesh,
        in_specs=placed,
        out_specs=(P("freq", "row", "col"), P("freq", "row", "col")),
        check_vma=False,
    )
```

```python
import math

import numpy as np

import jax
import jax.numpy as jnp
from jax import lax
from jax.experimental import pallas as pl
from jax.experimental.pallas import tpu as pltpu
from jax.sharding import PartitionSpec as P

NFFT = 1024
TAPS = 4
SPEC = 64
CH_DEV = 4


def dft_table_np(channels):
    position = np.arange(NFFT, dtype=np.int64)
    channel = np.arange(channels, dtype=np.int64)
    phases = (position[:, None] * channel[None, :] % NFFT).astype(np.float64) * (2.0 * math.pi / NFFT)
    scaling = 0.5 / math.sqrt(NFFT)
    cosine = np.cos(phases) * scaling
    sine = np.sin(phases) * scaling
    real_rows = np.stack([cosine, -sine], axis=1)
    imag_rows = np.stack([sine, cosine], axis=1)
    table = np.stack([real_rows, imag_rows], axis=0)
    table = table.transpose(2, 3, 0, 1).reshape(2 * channels, 2 * NFFT)
    return jnp.asarray(table, dtype=jnp.bfloat16)


LANES = 128


def pfb_dft_kernel(g_ref, taps_ref, s_hbm, tab_hbm, o_ref, sbuf, vbuf, tab_buf, f_ref, sems):
    inputs_here, nsamp = s_hbm.shape[1], s_hbm.shape[2]
    frames = nsamp // NFFT
    first = SPEC // 2 + TAPS - 1
    split = first * NFFT
    blocks = NFFT // LANES
    channels = tab_hbm.shape[0] // 2
    parts = []
    for p in range(2):
        head = pltpu.make_async_copy(
            s_hbm.at[p, :, pl.ds(0, split)], sbuf.at[p, :, pl.ds(0, split)], sems.at[2 * p]
        )
        tail = pltpu.make_async_copy(
            s_hbm.at[p, :, pl.ds(split, nsamp - split)],
            sbuf.at[p, :, pl.ds(split, nsamp - split)],
            sems.at[2 * p + 1],
        )
        head.start()
        tail.start()
        parts.append((head, tail))
    tab_cp = pltpu.make_async_copy(tab_hbm, tab_buf, sems.at[4])
    tab_cp.start()

    row = lax.broadcasted_iota(jnp.int32, (inputs_here, NFFT), 0)
    scale = jnp.zeros((inputs_here, NFFT), jnp.float32)
    for i in range(inputs_here):
        scale = jnp.where(row == i, g_ref[i] * 0.25, scale)

    def volts(p, lo, hi):
        def body(j, carry):
            start = pl.multiple_of(j * NFFT, NFFT)
            vbuf[p, j] = sbuf[p, :, pl.ds(start, NFFT)].astype(jnp.float32) * scale
            return carry

        lax.fori_loop(lo, hi, body, 0)

    def filt(p, lo, hi):
        def body(m, carry):
            total = vbuf[p, m] * taps_ref[0:1, :]
            for t in range(1, TAPS):
                total = total + vbuf[p, m + t] * taps_ref[t : t + 1, :]
            rows = pl.ds(pl.multiple_of(m * inputs_here, inputs_here), inputs_here)
            for b in range(blocks):
                f_ref[p * blocks + b, rows, :] = total[:, b * LANES : (b + 1) * LANES]
            return carry

        lax.fori_loop(lo, hi, body, 0)

    for p in range(2):
        head, tail = parts[p]
        head.wait()
        volts(p, 0, first)
        filt(p, 0, SPEC // 2)
        tail.wait()
        volts(p, first, frames)
        filt(p, SPEC // 2, SPEC)

    tab_cp.wait()
    for i in range(inputs_here):
        lhs = jnp.concatenate(
            [f_ref[b, pl.ds(i, SPEC, stride=inputs_here), :] for b in range(2 * blocks)], axis=1
        ).astype(jnp.bfloat16)
        prod = lax.dot_general(
            tab_buf[...], lhs, (((1,), (1,)), ((), ())), preferred_element_type=jnp.float32
        )
        val = jnp.concatenate([prod[:channels], prod[channels:]], axis=1)
        o_ref[pl.ds(i, channels, stride=inputs_here), :] = val


def pfb_dft(samples, gains, taps, table):
    inputs_here, nsamp = samples.shape[1], samples.shape[2]
    channels = table.shape[0] // 2
    frames = nsamp // NFFT
    vmem = pltpu.MemorySpace.VMEM
    return pl.pallas_call(
        pfb_dft_kernel,
        out_shape=jax.ShapeDtypeStruct((channels * inputs_here, 2 * SPEC), jnp.float32),
        in_specs=[
            pl.BlockSpec(memory_space=pltpu.MemorySpace.SMEM),
            pl.BlockSpec(memory_space=vmem),
            pl.BlockSpec(memory_space=pl.ANY),
            pl.BlockSpec(memory_space=pl.ANY),
        ],
        out_specs=pl.BlockSpec(memory_space=vmem),
        scratch_shapes=[
            pltpu.VMEM((2, inputs_here, nsamp), jnp.int32),
            pltpu.VMEM((2, frames, inputs_here, NFFT), jnp.float32),
            pltpu.VMEM(table.shape, jnp.bfloat16),
            pltpu.VMEM((2 * NFFT // LANES, SPEC * inputs_here, LANES), jnp.float32),
            pltpu.SemaphoreType.DMA((5,)),
        ],
        compiler_params=pltpu.CompilerParams(vmem_limit_bytes=40 * 1024 * 1024),
    )(gains, taps, samples, table)


MESH = pl.DeviceIdType.MESH


def turn_kernel(spec_ref, row_ref, col_ref, send1, recv1, own_sem, send2, recv2, recvx, local_sem):
    nf = spec_ref.shape[0]
    ncol = row_ref.shape[0]
    f = lax.axis_index("freq")
    r = lax.axis_index("row")
    c = lax.axis_index("col")
    cross_c = 2 * r + c // 2
    crossing = (c // 2) != r

    barrier = pltpu.get_barrier_semaphore()

    def greet_freq(d, carry):
        pl.semaphore_signal(barrier, inc=1, device_id=((f + d) % nf, r, c), device_id_type=MESH)
        return carry

    lax.fori_loop(1, nf, greet_freq, 0)
    for d in range(1, ncol):
        pl.semaphore_signal(barrier, inc=1, device_id=(f, r, (c + d) % ncol), device_id_type=MESH)
    pl.semaphore_signal(barrier, inc=1, device_id=(f, 1 - r, cross_c), device_id_type=MESH)

    @pl.when(crossing)
    def _():
        for e in range(2):
            pl.semaphore_signal(
                barrier, inc=1, device_id=(f, 1 - r, 2 * (c % 2) + e), device_id_type=MESH
            )

    pl.semaphore_wait(barrier, (nf - 1) + (ncol - 1) + 1 + 2 * crossing.astype(jnp.int32))

    own = pltpu.make_async_copy(spec_ref.at[f], row_ref.at[c, f], own_sem)
    own.start()

    def send_freq(d, carry):
        dest = (f + d) % nf
        pltpu.make_async_remote_copy(
            src_ref=spec_ref.at[dest],
            dst_ref=row_ref.at[c, f],
            send_sem=send1.at[d],
            recv_sem=recv1.at[f],
            device_id=(dest, r, c),
            device_id_type=MESH,
        ).start()
        return carry

    lax.fori_loop(1, nf, send_freq, 0)

    def recv_freq(d, carry):
        src = (f + nf - d) % nf
        pltpu.make_async_remote_copy(
            src_ref=spec_ref.at[src],
            dst_ref=row_ref.at[c, src],
            send_sem=send1.at[d],
            recv_sem=recv1.at[src],
            device_id=(src, r, c),
            device_id_type=MESH,
        ).wait_recv()
        return carry

    lax.fori_loop(1, nf, recv_freq, 0)
    own.wait()

    sends2 = []
    for d in range(1, ncol):
        cp = pltpu.make_async_remote_copy(
            src_ref=row_ref.at[c],
            dst_ref=row_ref.at[c],
            send_sem=send2.at[d],
            recv_sem=recv2.at[c],
            device_id=(f, r, (c + d) % ncol),
            device_id_type=MESH,
        )
        cp.start()
        sends2.append(cp)
    cross = pltpu.make_async_remote_copy(
        src_ref=row_ref.at[c],
        dst_ref=col_ref.at[c % 2],
        send_sem=send2.at[0],
        recv_sem=recvx.at[c % 2],
        device_id=(f, 1 - r, cross_c),
        device_id_type=MESH,
    )
    cross.start()

    for d in range(1, ncol):
        src = (c + ncol - d) % ncol
        pltpu.make_async_remote_copy(
            src_ref=row_ref.at[src],
            dst_ref=row_ref.at[src],
            send_sem=send2.at[d],
            recv_sem=recv2.at[src],
            device_id=(f, r, src),
            device_id_type=MESH,
        ).wait_recv()

    @pl.when(crossing)
    def _():
        for e in range(2):
            pltpu.make_async_remote_copy(
                src_ref=row_ref.at[e],
                dst_ref=col_ref.at[e],
                send_sem=send2.at[0],
                recv_sem=recvx.at[e],
                device_id=(f, 1 - r, 2 * (c % 2) + e),
                device_id_type=MESH,
            ).wait_recv()

    @pl.when(jnp.logical_not(crossing))
    def _():
        half = pltpu.make_async_copy(row_ref.at[pl.ds(2 * (c % 2), 2)], col_ref, local_sem)
        half.start()
        half.wait()

    def wait_send_freq(d, carry):
        dest = (f + d) % nf
        pltpu.make_async_remote_copy(
            src_ref=spec_ref.at[dest],
            dst_ref=row_ref.at[c, f],
            send_sem=send1.at[d],
            recv_sem=recv1.at[f],
            device_id=(dest, r, c),
            device_id_type=MESH,
        ).wait_send()
        return carry

    lax.fori_loop(1, nf, wait_send_freq, 0)
    for cp in sends2:
        cp.wait_send()
    cross.wait_send()


def corner_turn(spec):
    nf, rows, width = spec.shape
    ncol = lax.axis_size("col")
    vmem = pltpu.MemorySpace.VMEM
    return pl.pallas_call(
        turn_kernel,
        out_shape=(
            jax.ShapeDtypeStruct((ncol, nf, rows, width), spec.dtype),
            jax.ShapeDtypeStruct((2, nf, rows, width), spec.dtype),
        ),
        in_specs=[pl.BlockSpec(memory_space=vmem)],
        out_specs=(pl.BlockSpec(memory_space=vmem), pl.BlockSpec(memory_space=vmem)),
        scratch_shapes=[
            pltpu.SemaphoreType.DMA((nf,)),
            pltpu.SemaphoreType.DMA((nf,)),
            pltpu.SemaphoreType.DMA,
            pltpu.SemaphoreType.DMA((ncol,)),
            pltpu.SemaphoreType.DMA((ncol,)),
            pltpu.SemaphoreType.DMA((2,)),
            pltpu.SemaphoreType.DMA,
        ],
        compiler_params=pltpu.CompilerParams(collective_id=0, has_side_effects=True),
    )(spec)


def local(samples, input_gains, filter_taps):
    nf = lax.axis_size("freq")
    channels = CH_DEV * nf
    inputs_here = samples.shape[1]
    table = dft_table_np(channels)
    flat = pfb_dft(samples, input_gains, filter_taps, table)
    spec = flat.astype(jnp.bfloat16).reshape(nf, CH_DEV * inputs_here, 2 * SPEC)
    row_blk, col_blk = corner_turn(spec)
    row_data = row_blk.reshape(-1, nf, CH_DEV, inputs_here, 2 * SPEC).transpose(2, 0, 1, 3, 4)
    row_data = row_data.reshape(CH_DEV, -1, 2 * SPEC)
    column_data = col_blk.reshape(2, nf, CH_DEV, inputs_here, 2 * SPEC).transpose(2, 0, 1, 3, 4)
    column_data = column_data.reshape(CH_DEV, -1, 2 * SPEC)
    rotated = jnp.concatenate([-column_data[:, :, SPEC:], column_data[:, :, :SPEC]], axis=2)
    vis_real = (
        jnp.einsum("kim,kjm->kij", row_data, column_data, preferred_element_type=jnp.float32)
        * (1.0 / SPEC)
    ).astype(jnp.bfloat16)
    vis_imag = (
        jnp.einsum("kim,kjm->kij", row_data, rotated, preferred_element_type=jnp.float32)
        * (1.0 / SPEC)
    ).astype(jnp.bfloat16)
    return (vis_real, vis_imag)


def solution(mesh):
    placed = (P(None, ("row", "col", "freq"), None), P(("row", "col", "freq")), P())
    return jax.shard_map(
        local,
        mesh=mesh,
        in_specs=placed,
        out_specs=(P("freq", "row", "col"), P("freq", "row", "col")),
        check_vma=False,
    )
```

```python
import math

import numpy as np

import jax
import jax.numpy as jnp
from jax import lax
from jax.experimental import pallas as pl
from jax.experimental.pallas import tpu as pltpu
from jax.sharding import PartitionSpec as P

NFFT = 1024
TAPS = 4
SPEC = 64
CH_DEV = 4


def dft_table_np(channels):
    position = np.arange(NFFT, dtype=np.int64)
    channel = np.arange(channels, dtype=np.int64)
    phases = (position[:, None] * channel[None, :] % NFFT).astype(np.float64) * (2.0 * math.pi / NFFT)
    scaling = 0.5 / math.sqrt(NFFT)
    cosine = np.cos(phases) * scaling
    sine = np.sin(phases) * scaling
    real_rows = np.stack([cosine, -sine], axis=1)
    imag_rows = np.stack([sine, cosine], axis=1)
    table = np.stack([real_rows, imag_rows], axis=0)
    table = table.transpose(2, 3, 0, 1).reshape(2 * channels, 2 * NFFT)
    return jnp.asarray(table, dtype=jnp.bfloat16)


LANES = 128


def pfb_dft_kernel(g_ref, taps_ref, s_hbm, tab_hbm, o_ref, sbuf, vbuf, tab_buf, f_ref, sems):
    inputs_here, nsamp = s_hbm.shape[1], s_hbm.shape[2]
    frames = nsamp // NFFT
    first = SPEC // 2 + TAPS - 1
    split = first * NFFT
    blocks = NFFT // LANES
    channels = tab_hbm.shape[0] // 2
    parts = []
    for p in range(2):
        head = pltpu.make_async_copy(
            s_hbm.at[p, :, pl.ds(0, split)], sbuf.at[p, :, pl.ds(0, split)], sems.at[2 * p]
        )
        tail = pltpu.make_async_copy(
            s_hbm.at[p, :, pl.ds(split, nsamp - split)],
            sbuf.at[p, :, pl.ds(split, nsamp - split)],
            sems.at[2 * p + 1],
        )
        head.start()
        tail.start()
        parts.append((head, tail))
    tab_cp = pltpu.make_async_copy(tab_hbm, tab_buf, sems.at[4])
    tab_cp.start()

    row = lax.broadcasted_iota(jnp.int32, (inputs_here, NFFT), 0)
    scale = jnp.zeros((inputs_here, NFFT), jnp.float32)
    for i in range(inputs_here):
        scale = jnp.where(row == i, g_ref[i] * 0.25, scale)

    def volts(p, lo, hi):
        def body(j, carry):
            start = pl.multiple_of(j * NFFT, NFFT)
            vbuf[p, j] = sbuf[p, :, pl.ds(start, NFFT)].astype(jnp.float32) * scale
            return carry

        lax.fori_loop(lo, hi, body, 0)

    def filt(p, lo, hi):
        def body(m, carry):
            total = vbuf[p, m] * taps_ref[0:1, :]
            for t in range(1, TAPS):
                total = total + vbuf[p, m + t] * taps_ref[t : t + 1, :]
            rows = pl.ds(pl.multiple_of(m * inputs_here, inputs_here), inputs_here)
            for b in range(blocks):
                f_ref[p * blocks + b, rows, :] = total[:, b * LANES : (b + 1) * LANES]
            return carry

        lax.fori_loop(lo, hi, body, 0)

    for p in range(2):
        head, tail = parts[p]
        head.wait()
        volts(p, 0, first)
        filt(p, 0, SPEC // 2)
        tail.wait()
        volts(p, first, frames)
        filt(p, SPEC // 2, SPEC)

    tab_cp.wait()
    for i in range(inputs_here):
        lhs = jnp.concatenate(
            [f_ref[b, pl.ds(i, SPEC, stride=inputs_here), :] for b in range(2 * blocks)], axis=1
        ).astype(jnp.bfloat16)
        prod = lax.dot_general(
            tab_buf[...], lhs, (((1,), (1,)), ((), ())), preferred_element_type=jnp.float32
        )
        val = jnp.concatenate([prod[:channels], prod[channels:]], axis=1)
        o_ref[pl.ds(i, channels, stride=inputs_here), :] = val


def pfb_dft(samples, gains, taps, table):
    inputs_here, nsamp = samples.shape[1], samples.shape[2]
    channels = table.shape[0] // 2
    frames = nsamp // NFFT
    vmem = pltpu.MemorySpace.VMEM
    return pl.pallas_call(
        pfb_dft_kernel,
        out_shape=jax.ShapeDtypeStruct((channels * inputs_here, 2 * SPEC), jnp.float32),
        in_specs=[
            pl.BlockSpec(memory_space=pltpu.MemorySpace.SMEM),
            pl.BlockSpec(memory_space=vmem),
            pl.BlockSpec(memory_space=pl.ANY),
            pl.BlockSpec(memory_space=pl.ANY),
        ],
        out_specs=pl.BlockSpec(memory_space=vmem),
        scratch_shapes=[
            pltpu.VMEM((2, inputs_here, nsamp), jnp.int32),
            pltpu.VMEM((2, frames, inputs_here, NFFT), jnp.float32),
            pltpu.VMEM(table.shape, jnp.bfloat16),
            pltpu.VMEM((2 * NFFT // LANES, SPEC * inputs_here, LANES), jnp.float32),
            pltpu.SemaphoreType.DMA((5,)),
        ],
        compiler_params=pltpu.CompilerParams(vmem_limit_bytes=40 * 1024 * 1024),
    )(gains, taps, samples, table)


MESH = pl.DeviceIdType.MESH


def turn_kernel(
    spec_ref, row_ref, col_ref, send1, recv1, own_sem, sends, recva, recvb, recvc, recvd, local_sem
):
    nf = spec_ref.shape[0]
    f = lax.axis_index("freq")
    r = lax.axis_index("row")
    c = lax.axis_index("col")
    k = c % 2
    h = c // 2
    sib = c + 1 - 2 * k
    cross_c = 2 * r + h
    crossing = h != r
    relay_target = jnp.logical_or(c == 1, c == 2)
    fan_target = jnp.logical_not(relay_target)
    relay_dest = 2 - k
    relay_src = 2 * r + 2 - c

    barrier = pltpu.get_barrier_semaphore()

    def greet_freq(d, carry):
        pl.semaphore_signal(barrier, inc=1, device_id=((f + d) % nf, r, c), device_id_type=MESH)
        return carry

    lax.fori_loop(1, nf, greet_freq, 0)
    pl.semaphore_signal(barrier, inc=1, device_id=(f, r, sib), device_id_type=MESH)
    pl.semaphore_signal(barrier, inc=1, device_id=(f, 1 - r, cross_c), device_id_type=MESH)

    @pl.when(crossing)
    def _():
        for e in range(2):
            pl.semaphore_signal(barrier, inc=1, device_id=(f, 1 - r, 2 * k + e), device_id_type=MESH)
        pl.semaphore_signal(barrier, inc=1, device_id=(f, 1 - r, relay_dest), device_id_type=MESH)

    @pl.when(relay_target)
    def _():
        pl.semaphore_signal(barrier, inc=1, device_id=(f, 1 - r, relay_src), device_id_type=MESH)

    expected = (nf - 1) + 2 + 3 * crossing.astype(jnp.int32) + relay_target.astype(jnp.int32)
    pl.semaphore_wait(barrier, expected)

    own = pltpu.make_async_copy(spec_ref.at[f], row_ref.at[c, f], own_sem)
    own.start()

    def freq_copy(d):
        dest = (f + d) % nf
        return pltpu.make_async_remote_copy(
            src_ref=spec_ref.at[dest],
            dst_ref=row_ref.at[c, f],
            send_sem=send1.at[d],
            recv_sem=recv1.at[f],
            device_id=(dest, r, c),
            device_id_type=MESH,
        )

    def send_freq(d, carry):
        freq_copy(d).start()
        return carry

    lax.fori_loop(1, nf, send_freq, 0)

    def recv_freq(d, carry):
        src = (f + nf - d) % nf
        pltpu.make_async_remote_copy(
            src_ref=spec_ref.at[src],
            dst_ref=row_ref.at[c, src],
            send_sem=send1.at[d],
            recv_sem=recv1.at[src],
            device_id=(src, r, c),
            device_id_type=MESH,
        ).wait_recv()
        return carry

    lax.fori_loop(1, nf, recv_freq, 0)
    own.wait()

    to_sib = pltpu.make_async_remote_copy(
        src_ref=row_ref.at[c],
        dst_ref=row_ref.at[c],
        send_sem=sends.at[0],
        recv_sem=recva,
        device_id=(f, r, sib),
        device_id_type=MESH,
    )
    to_sib.start()
    to_cross = pltpu.make_async_remote_copy(
        src_ref=row_ref.at[c],
        dst_ref=col_ref.at[k],
        send_sem=sends.at[1],
        recv_sem=recvb.at[k],
        device_id=(f, 1 - r, cross_c),
        device_id_type=MESH,
    )
    to_cross.start()

    def relay_copy(e):
        return pltpu.make_async_remote_copy(
            src_ref=col_ref.at[e],
            dst_ref=row_ref.at[2 * k + e],
            send_sem=sends.at[2 + e],
            recv_sem=recvc.at[e],
            device_id=(f, 1 - r, relay_dest),
            device_id_type=MESH,
        )

    def fan_copy(e, base):
        return pltpu.make_async_remote_copy(
            src_ref=row_ref.at[base + e],
            dst_ref=row_ref.at[base + e],
            send_sem=sends.at[4 + e],
            recv_sem=recvd.at[e],
            device_id=(f, r, sib),
            device_id_type=MESH,
        )

    @pl.when(crossing)
    def _():
        for e in range(2):
            pltpu.make_async_remote_copy(
                src_ref=row_ref.at[e],
                dst_ref=col_ref.at[e],
                send_sem=sends.at[1],
                recv_sem=recvb.at[e],
                device_id=(f, 1 - r, 2 * k + e),
                device_id_type=MESH,
            ).wait_recv()
            relay_copy(e).start()

    @pl.when(relay_target)
    def _():
        for e in range(2):
            pltpu.make_async_remote_copy(
                src_ref=col_ref.at[e],
                dst_ref=row_ref.at[2 * (2 - c) + e],
                send_sem=sends.at[2 + e],
                recv_sem=recvc.at[e],
                device_id=(f, 1 - r, relay_src),
                device_id_type=MESH,
            ).wait_recv()
            fan_copy(e, 2 * (2 - c)).start()

    @pl.when(fan_target)
    def _():
        for e in range(2):
            fan_copy(e, 2 * (2 - sib)).wait_recv()

    pltpu.make_async_remote_copy(
        src_ref=row_ref.at[sib],
        dst_ref=row_ref.at[sib],
        send_sem=sends.at[0],
        recv_sem=recva,
        device_id=(f, r, sib),
        device_id_type=MESH,
    ).wait_recv()

    @pl.when(jnp.logical_not(crossing))
    def _():
        half = pltpu.make_async_copy(row_ref.at[pl.ds(2 * k, 2)], col_ref, local_sem)
        half.start()
        half.wait()

    def wait_send_freq(d, carry):
        freq_copy(d).wait_send()
        return carry

    lax.fori_loop(1, nf, wait_send_freq, 0)
    to_sib.wait_send()
    to_cross.wait_send()

    @pl.when(crossing)
    def _():
        for e in range(2):
            relay_copy(e).wait_send()

    @pl.when(relay_target)
    def _():
        for e in range(2):
            fan_copy(e, 2 * (2 - c)).wait_send()


def corner_turn(spec):
    nf, rows, width = spec.shape
    ncol = lax.axis_size("col")
    vmem = pltpu.MemorySpace.VMEM
    return pl.pallas_call(
        turn_kernel,
        out_shape=(
            jax.ShapeDtypeStruct((ncol, nf, rows, width), spec.dtype),
            jax.ShapeDtypeStruct((2, nf, rows, width), spec.dtype),
        ),
        in_specs=[pl.BlockSpec(memory_space=vmem)],
        out_specs=(pl.BlockSpec(memory_space=vmem), pl.BlockSpec(memory_space=vmem)),
        scratch_shapes=[
            pltpu.SemaphoreType.DMA((nf,)),
            pltpu.SemaphoreType.DMA((nf,)),
            pltpu.SemaphoreType.DMA,
            pltpu.SemaphoreType.DMA((6,)),
            pltpu.SemaphoreType.DMA,
            pltpu.SemaphoreType.DMA((2,)),
            pltpu.SemaphoreType.DMA((2,)),
            pltpu.SemaphoreType.DMA((2,)),
            pltpu.SemaphoreType.DMA,
        ],
        compiler_params=pltpu.CompilerParams(collective_id=0, has_side_effects=True),
    )(spec)


def local(samples, input_gains, filter_taps):
    nf = lax.axis_size("freq")
    channels = CH_DEV * nf
    inputs_here = samples.shape[1]
    table = dft_table_np(channels)
    flat = pfb_dft(samples, input_gains, filter_taps, table)
    spec = flat.astype(jnp.bfloat16).reshape(nf, CH_DEV * inputs_here, 2 * SPEC)
    row_blk, col_blk = corner_turn(spec)
    row_data = row_blk.reshape(-1, nf, CH_DEV, inputs_here, 2 * SPEC).transpose(2, 0, 1, 3, 4)
    row_data = row_data.reshape(CH_DEV, -1, 2 * SPEC)
    column_data = col_blk.reshape(2, nf, CH_DEV, inputs_here, 2 * SPEC).transpose(2, 0, 1, 3, 4)
    column_data = column_data.reshape(CH_DEV, -1, 2 * SPEC)
    rotated = jnp.concatenate([-column_data[:, :, SPEC:], column_data[:, :, :SPEC]], axis=2)
    vis_real = (
        jnp.einsum("kim,kjm->kij", row_data, column_data, preferred_element_type=jnp.float32)
        * (1.0 / SPEC)
    ).astype(jnp.bfloat16)
    vis_imag = (
        jnp.einsum("kim,kjm->kij", row_data, rotated, preferred_element_type=jnp.float32)
        * (1.0 / SPEC)
    ).astype(jnp.bfloat16)
    return (vis_real, vis_imag)


def solution(mesh):
    placed = (P(None, ("row", "col", "freq"), None), P(("row", "col", "freq")), P())
    return jax.shard_map(
        local,
        mesh=mesh,
        in_specs=placed,
        out_specs=(P("freq", "row", "col"), P("freq", "row", "col")),
        check_vma=False,
    )
```

```python
import math

import numpy as np

import jax
import jax.numpy as jnp
from jax import lax
from jax.experimental import pallas as pl
from jax.experimental.pallas import tpu as pltpu
from jax.sharding import PartitionSpec as P

NFFT = 1024
TAPS = 4
SPEC = 64
CH_DEV = 4


def dft_table_np(channels):
    position = np.arange(NFFT, dtype=np.int64)
    channel = np.arange(channels, dtype=np.int64)
    phases = (position[:, None] * channel[None, :] % NFFT).astype(np.float64) * (2.0 * math.pi / NFFT)
    scaling = 0.5 / math.sqrt(NFFT)
    cosine = np.cos(phases) * scaling
    sine = np.sin(phases) * scaling
    real_rows = np.stack([cosine, -sine], axis=1)
    imag_rows = np.stack([sine, cosine], axis=1)
    table = np.stack([real_rows, imag_rows], axis=0)
    table = table.transpose(2, 3, 0, 1).reshape(2 * channels, 2 * NFFT)
    return jnp.asarray(table, dtype=jnp.bfloat16)


LANES = 128


def pfb_dft_kernel(g_ref, taps_ref, s_hbm, tab_hbm, o_ref, sbuf, vbuf, tab_buf, f_ref, sems):
    inputs_here, nsamp = s_hbm.shape[1], s_hbm.shape[2]
    frames = nsamp // NFFT
    first = SPEC // 2 + TAPS - 1
    split = first * NFFT
    blocks = NFFT // LANES
    channels = tab_hbm.shape[0] // 2
    parts = []
    for p in range(2):
        head = pltpu.make_async_copy(
            s_hbm.at[p, :, pl.ds(0, split)], sbuf.at[p, :, pl.ds(0, split)], sems.at[2 * p]
        )
        tail = pltpu.make_async_copy(
            s_hbm.at[p, :, pl.ds(split, nsamp - split)],
            sbuf.at[p, :, pl.ds(split, nsamp - split)],
            sems.at[2 * p + 1],
        )
        head.start()
        tail.start()
        parts.append((head, tail))
    tab_cp = pltpu.make_async_copy(tab_hbm, tab_buf, sems.at[4])
    tab_cp.start()

    row = lax.broadcasted_iota(jnp.int32, (inputs_here, NFFT), 0)
    scale = jnp.zeros((inputs_here, NFFT), jnp.float32)
    for i in range(inputs_here):
        scale = jnp.where(row == i, g_ref[i] * 0.25, scale)

    def volts(p, lo, hi):
        def body(j, carry):
            start = pl.multiple_of(j * NFFT, NFFT)
            vbuf[p, j] = sbuf[p, :, pl.ds(start, NFFT)].astype(jnp.float32) * scale
            return carry

        lax.fori_loop(lo, hi, body, 0)

    def filt(p, lo, hi):
        def body(m, carry):
            total = vbuf[p, m] * taps_ref[0:1, :]
            for t in range(1, TAPS):
                total = total + vbuf[p, m + t] * taps_ref[t : t + 1, :]
            rows = pl.ds(pl.multiple_of(m * inputs_here, inputs_here), inputs_here)
            for b in range(blocks):
                f_ref[p * blocks + b, rows, :] = total[:, b * LANES : (b + 1) * LANES]
            return carry

        lax.fori_loop(lo, hi, body, 0)

    for p in range(2):
        head, tail = parts[p]
        head.wait()
        volts(p, 0, first)
        filt(p, 0, SPEC // 2)
        tail.wait()
        volts(p, first, frames)
        filt(p, SPEC // 2, SPEC)

    tab_cp.wait()
    for i in range(inputs_here):
        lhs = jnp.concatenate(
            [f_ref[b, pl.ds(i, SPEC, stride=inputs_here), :] for b in range(2 * blocks)], axis=1
        ).astype(jnp.bfloat16)
        prod = lax.dot_general(
            tab_buf[...], lhs, (((1,), (1,)), ((), ())), preferred_element_type=jnp.float32
        )
        val = jnp.concatenate([prod[:channels], prod[channels:]], axis=1)
        o_ref[pl.ds(i, channels, stride=inputs_here), :] = val


def pfb_dft(samples, gains, taps, table):
    inputs_here, nsamp = samples.shape[1], samples.shape[2]
    channels = table.shape[0] // 2
    frames = nsamp // NFFT
    vmem = pltpu.MemorySpace.VMEM
    return pl.pallas_call(
        pfb_dft_kernel,
        out_shape=jax.ShapeDtypeStruct((channels * inputs_here, 2 * SPEC), jnp.float32),
        in_specs=[
            pl.BlockSpec(memory_space=pltpu.MemorySpace.SMEM),
            pl.BlockSpec(memory_space=vmem),
            pl.BlockSpec(memory_space=pl.ANY),
            pl.BlockSpec(memory_space=pl.ANY),
        ],
        out_specs=pl.BlockSpec(memory_space=vmem),
        scratch_shapes=[
            pltpu.VMEM((2, inputs_here, nsamp), jnp.int32),
            pltpu.VMEM((2, frames, inputs_here, NFFT), jnp.float32),
            pltpu.VMEM(table.shape, jnp.bfloat16),
            pltpu.VMEM((2 * NFFT // LANES, SPEC * inputs_here, LANES), jnp.float32),
            pltpu.SemaphoreType.DMA((5,)),
        ],
        compiler_params=pltpu.CompilerParams(vmem_limit_bytes=40 * 1024 * 1024),
    )(gains, taps, samples, table)


MESH = pl.DeviceIdType.MESH
PIECES = 4


def turn_kernel(
    spec_ref, row_ref, col_ref, send1, recv1, own_sem, senda, sendb, sendc, sendd,
    recva, recvb, recvc, recvd, local_sem,
):
    nf = spec_ref.shape[0]
    f = lax.axis_index("freq")
    r = lax.axis_index("row")
    c = lax.axis_index("col")
    k = c % 2
    h = c // 2
    sib = c + 1 - 2 * k
    cross_c = 2 * r + h
    crossing = h != r
    relay_target = jnp.logical_or(c == 1, c == 2)
    fan_target = jnp.logical_not(relay_target)
    relay_dest = 2 - k
    relay_src = 2 * r + 2 - c

    barrier = pltpu.get_barrier_semaphore()

    def greet_freq(d, carry):
        pl.semaphore_signal(barrier, inc=1, device_id=((f + d) % nf, r, c), device_id_type=MESH)
        return carry

    lax.fori_loop(1, nf, greet_freq, 0)
    pl.semaphore_signal(barrier, inc=1, device_id=(f, r, sib), device_id_type=MESH)
    pl.semaphore_signal(barrier, inc=1, device_id=(f, 1 - r, cross_c), device_id_type=MESH)

    @pl.when(crossing)
    def _():
        for e in range(2):
            pl.semaphore_signal(barrier, inc=1, device_id=(f, 1 - r, 2 * k + e), device_id_type=MESH)
        pl.semaphore_signal(barrier, inc=1, device_id=(f, 1 - r, relay_dest), device_id_type=MESH)

    @pl.when(relay_target)
    def _():
        pl.semaphore_signal(barrier, inc=1, device_id=(f, 1 - r, relay_src), device_id_type=MESH)

    expected = (nf - 1) + 2 + 3 * crossing.astype(jnp.int32) + relay_target.astype(jnp.int32)
    pl.semaphore_wait(barrier, expected)

    own = pltpu.make_async_copy(spec_ref.at[f], row_ref.at[c, f], own_sem)
    own.start()

    def freq_copy(d):
        dest = (f + d) % nf
        return pltpu.make_async_remote_copy(
            src_ref=spec_ref.at[dest],
            dst_ref=row_ref.at[c, f],
            send_sem=send1.at[d],
            recv_sem=recv1.at[f],
            device_id=(dest, r, c),
            device_id_type=MESH,
        )

    def send_freq(d, carry):
        freq_copy(d).start()
        return carry

    lax.fori_loop(1, nf, send_freq, 0)

    size = nf // PIECES

    def piece(q):
        return pl.ds(q * size, size)

    def sib_copy(q, slot):
        return pltpu.make_async_remote_copy(
            src_ref=row_ref.at[slot, piece(q)],
            dst_ref=row_ref.at[slot, piece(q)],
            send_sem=senda.at[q],
            recv_sem=recva.at[q],
            device_id=(f, r, sib),
            device_id_type=MESH,
        )

    def cross_copy(q, e, dev):
        return pltpu.make_async_remote_copy(
            src_ref=row_ref.at[c, piece(q)],
            dst_ref=col_ref.at[e, piece(q)],
            send_sem=sendb.at[q],
            recv_sem=recvb.at[e * PIECES + q],
            device_id=dev,
            device_id_type=MESH,
        )

    def relay_copy(q, e, slot, dev):
        return pltpu.make_async_remote_copy(
            src_ref=col_ref.at[e, piece(q)],
            dst_ref=row_ref.at[slot, piece(q)],
            send_sem=sendc.at[e * PIECES + q],
            recv_sem=recvc.at[e * PIECES + q],
            device_id=dev,
            device_id_type=MESH,
        )

    def fan_copy(q, e, base):
        return pltpu.make_async_remote_copy(
            src_ref=row_ref.at[base + e, piece(q)],
            dst_ref=row_ref.at[base + e, piece(q)],
            send_sem=sendd.at[e * PIECES + q],
            recv_sem=recvd.at[e * PIECES + q],
            device_id=(f, r, sib),
            device_id_type=MESH,
        )

    for q in range(PIECES):

        def recv_freq(j, carry):
            src = q * size + j

            @pl.when(src != f)
            def _():
                pltpu.make_async_remote_copy(
                    src_ref=spec_ref.at[src],
                    dst_ref=row_ref.at[c, src],
                    send_sem=send1.at[0],
                    recv_sem=recv1.at[src],
                    device_id=(src, r, c),
                    device_id_type=MESH,
                ).wait_recv()

            @pl.when(src == f)
            def _():
                own.wait()

            return carry

        lax.fori_loop(0, size, recv_freq, 0)
        sib_copy(q, c).start()
        cross_copy(q, k, (f, 1 - r, cross_c)).start()

        @pl.when(crossing)
        def _():
            for e in range(2):
                cross_copy(q, e, (f, 1 - r, 2 * k + e)).wait_recv()
                relay_copy(q, e, 2 * k + e, (f, 1 - r, relay_dest)).start()

        @pl.when(relay_target)
        def _():
            for e in range(2):
                relay_copy(q, e, 2 * (2 - c) + e, (f, 1 - r, relay_src)).wait_recv()
                fan_copy(q, e, 2 * (2 - c)).start()

    @pl.when(fan_target)
    def _():
        for q in range(PIECES):
            for e in range(2):
                fan_copy(q, e, 2 * (2 - sib)).wait_recv()

    for q in range(PIECES):
        sib_copy(q, sib).wait_recv()

    @pl.when(jnp.logical_not(crossing))
    def _():
        half = pltpu.make_async_copy(row_ref.at[pl.ds(2 * k, 2)], col_ref, local_sem)
        half.start()
        half.wait()

    def wait_send_freq(d, carry):
        freq_copy(d).wait_send()
        return carry

    lax.fori_loop(1, nf, wait_send_freq, 0)
    for q in range(PIECES):
        sib_copy(q, c).wait_send()
        cross_copy(q, k, (f, 1 - r, cross_c)).wait_send()

    @pl.when(crossing)
    def _():
        for q in range(PIECES):
            for e in range(2):
                relay_copy(q, e, 2 * k + e, (f, 1 - r, relay_dest)).wait_send()

    @pl.when(relay_target)
    def _():
        for q in range(PIECES):
            for e in range(2):
                fan_copy(q, e, 2 * (2 - c)).wait_send()


def corner_turn(spec):
    nf, rows, width = spec.shape
    ncol = lax.axis_size("col")
    vmem = pltpu.MemorySpace.VMEM
    return pl.pallas_call(
        turn_kernel,
        out_shape=(
            jax.ShapeDtypeStruct((ncol, nf, rows, width), spec.dtype),
            jax.ShapeDtypeStruct((2, nf, rows, width), spec.dtype),
        ),
        in_specs=[pl.BlockSpec(memory_space=vmem)],
        out_specs=(pl.BlockSpec(memory_space=vmem), pl.BlockSpec(memory_space=vmem)),
        scratch_shapes=[
            pltpu.SemaphoreType.DMA((nf,)),
            pltpu.SemaphoreType.DMA((nf,)),
            pltpu.SemaphoreType.DMA,
            pltpu.SemaphoreType.DMA((PIECES,)),
            pltpu.SemaphoreType.DMA((PIECES,)),
            pltpu.SemaphoreType.DMA((2 * PIECES,)),
            pltpu.SemaphoreType.DMA((2 * PIECES,)),
            pltpu.SemaphoreType.DMA((PIECES,)),
            pltpu.SemaphoreType.DMA((2 * PIECES,)),
            pltpu.SemaphoreType.DMA((2 * PIECES,)),
            pltpu.SemaphoreType.DMA((2 * PIECES,)),
            pltpu.SemaphoreType.DMA,
        ],
        compiler_params=pltpu.CompilerParams(collective_id=0, has_side_effects=True),
    )(spec)


def local(samples, input_gains, filter_taps):
    nf = lax.axis_size("freq")
    channels = CH_DEV * nf
    inputs_here = samples.shape[1]
    table = dft_table_np(channels)
    flat = pfb_dft(samples, input_gains, filter_taps, table)
    spec = flat.astype(jnp.bfloat16).reshape(nf, CH_DEV * inputs_here, 2 * SPEC)
    row_blk, col_blk = corner_turn(spec)
    row_data = row_blk.reshape(-1, nf, CH_DEV, inputs_here, 2 * SPEC).transpose(2, 0, 1, 3, 4)
    row_data = row_data.reshape(CH_DEV, -1, 2 * SPEC)
    column_data = col_blk.reshape(2, nf, CH_DEV, inputs_here, 2 * SPEC).transpose(2, 0, 1, 3, 4)
    column_data = column_data.reshape(CH_DEV, -1, 2 * SPEC)
    rotated = jnp.concatenate([-column_data[:, :, SPEC:], column_data[:, :, :SPEC]], axis=2)
    vis_real = (
        jnp.einsum("kim,kjm->kij", row_data, column_data, preferred_element_type=jnp.float32)
        * (1.0 / SPEC)
    ).astype(jnp.bfloat16)
    vis_imag = (
        jnp.einsum("kim,kjm->kij", row_data, rotated, preferred_element_type=jnp.float32)
        * (1.0 / SPEC)
    ).astype(jnp.bfloat16)
    return (vis_real, vis_imag)


def solution(mesh):
    placed = (P(None, ("row", "col", "freq"), None), P(("row", "col", "freq")), P())
    return jax.shard_map(
        local,
        mesh=mesh,
        in_specs=placed,
        out_specs=(P("freq", "row", "col"), P("freq", "row", "col")),
        check_vma=False,
    )
```

```python
import math

import numpy as np

import jax
import jax.numpy as jnp
from jax import lax
from jax.experimental import pallas as pl
from jax.experimental.pallas import tpu as pltpu
from jax.sharding import PartitionSpec as P

NFFT = 1024
TAPS = 4
SPEC = 64
CH_DEV = 4
FREQ_Y = 4


def dft_table_np(channels):
    position = np.arange(NFFT, dtype=np.int64)
    channel = np.arange(channels, dtype=np.int64)
    phases = (position[:, None] * channel[None, :] % NFFT).astype(np.float64) * (2.0 * math.pi / NFFT)
    scaling = 0.5 / math.sqrt(NFFT)
    cosine = np.cos(phases) * scaling
    sine = np.sin(phases) * scaling
    real_rows = np.stack([cosine, -sine], axis=1)
    imag_rows = np.stack([sine, cosine], axis=1)
    table = np.stack([real_rows, imag_rows], axis=0)
    groups = channels // CH_DEV
    order = np.arange(channels).reshape(groups // FREQ_Y, FREQ_Y, CH_DEV).transpose(1, 0, 2).reshape(-1)
    table = table[:, :, :, order]
    table = table.transpose(2, 3, 0, 1).reshape(2 * channels, 2 * NFFT)
    return jnp.asarray(table, dtype=jnp.bfloat16)


LANES = 128


def pfb_dft_kernel(g_ref, taps_ref, s_hbm, tab_hbm, o_ref, sbuf, vbuf, tab_buf, f_ref, sems):
    inputs_here, nsamp = s_hbm.shape[1], s_hbm.shape[2]
    frames = nsamp // NFFT
    first = SPEC // 2 + TAPS - 1
    split = first * NFFT
    blocks = NFFT // LANES
    channels = tab_hbm.shape[0] // 2
    parts = []
    for p in range(2):
        head = pltpu.make_async_copy(
            s_hbm.at[p, :, pl.ds(0, split)], sbuf.at[p, :, pl.ds(0, split)], sems.at[2 * p]
        )
        tail = pltpu.make_async_copy(
            s_hbm.at[p, :, pl.ds(split, nsamp - split)],
            sbuf.at[p, :, pl.ds(split, nsamp - split)],
            sems.at[2 * p + 1],
        )
        head.start()
        tail.start()
        parts.append((head, tail))
    tab_cp = pltpu.make_async_copy(tab_hbm, tab_buf, sems.at[4])
    tab_cp.start()

    row = lax.broadcasted_iota(jnp.int32, (inputs_here, NFFT), 0)
    scale = jnp.zeros((inputs_here, NFFT), jnp.float32)
    for i in range(inputs_here):
        scale = jnp.where(row == i, g_ref[i] * 0.25, scale)

    def volts(p, lo, hi):
        def body(j, carry):
            start = pl.multiple_of(j * NFFT, NFFT)
            vbuf[p, j] = sbuf[p, :, pl.ds(start, NFFT)].astype(jnp.float32) * scale
            return carry

        lax.fori_loop(lo, hi, body, 0)

    def filt(p, lo, hi):
        def body(m, carry):
            total = vbuf[p, m] * taps_ref[0:1, :]
            for t in range(1, TAPS):
                total = total + vbuf[p, m + t] * taps_ref[t : t + 1, :]
            rows = pl.ds(pl.multiple_of(m * inputs_here, inputs_here), inputs_here)
            for b in range(blocks):
                f_ref[p * blocks + b, rows, :] = total[:, b * LANES : (b + 1) * LANES]
            return carry

        lax.fori_loop(lo, hi, body, 0)

    for p in range(2):
        head, tail = parts[p]
        head.wait()
        volts(p, 0, first)
        filt(p, 0, SPEC // 2)
        tail.wait()
        volts(p, first, frames)
        filt(p, SPEC // 2, SPEC)

    tab_cp.wait()
    for i in range(inputs_here):
        lhs = jnp.concatenate(
            [f_ref[b, pl.ds(i, SPEC, stride=inputs_here), :] for b in range(2 * blocks)], axis=1
        ).astype(jnp.bfloat16)
        prod = lax.dot_general(
            tab_buf[...], lhs, (((1,), (1,)), ((), ())), preferred_element_type=jnp.float32
        )
        val = jnp.concatenate([prod[:channels], prod[channels:]], axis=1)
        o_ref[pl.ds(i, channels, stride=inputs_here), :] = val


def pfb_dft(samples, gains, taps, table):
    inputs_here, nsamp = samples.shape[1], samples.shape[2]
    channels = table.shape[0] // 2
    frames = nsamp // NFFT
    vmem = pltpu.MemorySpace.VMEM
    return pl.pallas_call(
        pfb_dft_kernel,
        out_shape=jax.ShapeDtypeStruct((channels * inputs_here, 2 * SPEC), jnp.float32),
        in_specs=[
            pl.BlockSpec(memory_space=pltpu.MemorySpace.SMEM),
            pl.BlockSpec(memory_space=vmem),
            pl.BlockSpec(memory_space=pl.ANY),
            pl.BlockSpec(memory_space=pl.ANY),
        ],
        out_specs=pl.BlockSpec(memory_space=vmem),
        scratch_shapes=[
            pltpu.VMEM((2, inputs_here, nsamp), jnp.int32),
            pltpu.VMEM((2, frames, inputs_here, NFFT), jnp.float32),
            pltpu.VMEM(table.shape, jnp.bfloat16),
            pltpu.VMEM((2 * NFFT // LANES, SPEC * inputs_here, LANES), jnp.float32),
            pltpu.SemaphoreType.DMA((5,)),
        ],
        compiler_params=pltpu.CompilerParams(vmem_limit_bytes=40 * 1024 * 1024),
    )(gains, taps, samples, table)


MESH = pl.DeviceIdType.MESH


def turn_kernel(
    spec_ref, row_ref, col_ref, mid_ref, send1, recv1, send2, recv2, own_sem, sends,
    recva, recvb, recvc, recvd, local_sem,
):
    nf = spec_ref.shape[0] * spec_ref.shape[1]
    f = lax.axis_index("freq")
    r = lax.axis_index("row")
    c = lax.axis_index("col")
    k = c % 2
    h = c // 2
    sib = c + 1 - 2 * k
    cross_c = 2 * r + h
    crossing = h != r
    relay_target = jnp.logical_or(c == 1, c == 2)
    fan_target = jnp.logical_not(relay_target)
    relay_dest = 2 - k
    relay_src = 2 * r + 2 - c

    ny = FREQ_Y
    nz = nf // ny
    z = f // ny
    y = f % ny

    barrier = pltpu.get_barrier_semaphore()
    for d in range(1, ny):
        pl.semaphore_signal(barrier, inc=1, device_id=(z * ny + (y + d) % ny, r, c), device_id_type=MESH)

    def greet_z(d, carry):
        pl.semaphore_signal(barrier, inc=1, device_id=(((z + d) % nz) * ny + y, r, c), device_id_type=MESH)
        return carry

    lax.fori_loop(1, nz, greet_z, 0)
    pl.semaphore_signal(barrier, inc=1, device_id=(f, r, sib), device_id_type=MESH)
    pl.semaphore_signal(barrier, inc=1, device_id=(f, 1 - r, cross_c), device_id_type=MESH)

    @pl.when(crossing)
    def _():
        for e in range(2):
            pl.semaphore_signal(barrier, inc=1, device_id=(f, 1 - r, 2 * k + e), device_id_type=MESH)
        pl.semaphore_signal(barrier, inc=1, device_id=(f, 1 - r, relay_dest), device_id_type=MESH)

    @pl.when(relay_target)
    def _():
        pl.semaphore_signal(barrier, inc=1, device_id=(f, 1 - r, relay_src), device_id_type=MESH)

    expected = (ny - 1) + (nz - 1) + 2 + 3 * crossing.astype(jnp.int32) + relay_target.astype(jnp.int32)
    pl.semaphore_wait(barrier, expected)

    own_y = pltpu.make_async_copy(spec_ref.at[y], mid_ref.at[y], own_sem.at[0])
    own_y.start()

    def y_copy(d):
        dest = (y + d) % ny
        return pltpu.make_async_remote_copy(
            src_ref=spec_ref.at[dest],
            dst_ref=mid_ref.at[y],
            send_sem=send1.at[d],
            recv_sem=recv1.at[y],
            device_id=(z * ny + dest, r, c),
            device_id_type=MESH,
        )

    for d in range(1, ny):
        y_copy(d).start()
    for d in range(1, ny):
        src = (y + ny - d) % ny
        pltpu.make_async_remote_copy(
            src_ref=spec_ref.at[src],
            dst_ref=mid_ref.at[src],
            send_sem=send1.at[d],
            recv_sem=recv1.at[src],
            device_id=(z * ny + src, r, c),
            device_id_type=MESH,
        ).wait_recv()
    own_y.wait()

    own_z = pltpu.make_async_copy(mid_ref.at[:, z], row_ref.at[c, pl.ds(z * ny, ny)], own_sem.at[1])
    own_z.start()

    def z_copy(d):
        dest = (z + d) % nz
        return pltpu.make_async_remote_copy(
            src_ref=mid_ref.at[:, dest],
            dst_ref=row_ref.at[c, pl.ds(z * ny, ny)],
            send_sem=send2.at[d],
            recv_sem=recv2.at[z],
            device_id=(dest * ny + y, r, c),
            device_id_type=MESH,
        )

    def send_z(d, carry):
        z_copy(d).start()
        return carry

    lax.fori_loop(1, nz, send_z, 0)

    def recv_z(d, carry):
        src = (z + nz - d) % nz
        pltpu.make_async_remote_copy(
            src_ref=mid_ref.at[:, src],
            dst_ref=row_ref.at[c, pl.ds(src * ny, ny)],
            send_sem=send2.at[d],
            recv_sem=recv2.at[src],
            device_id=(src * ny + y, r, c),
            device_id_type=MESH,
        ).wait_recv()
        return carry

    lax.fori_loop(1, nz, recv_z, 0)
    own_z.wait()

    to_sib = pltpu.make_async_remote_copy(
        src_ref=row_ref.at[c],
        dst_ref=row_ref.at[c],
        send_sem=sends.at[0],
        recv_sem=recva,
        device_id=(f, r, sib),
        device_id_type=MESH,
    )
    to_sib.start()
    to_cross = pltpu.make_async_remote_copy(
        src_ref=row_ref.at[c],
        dst_ref=col_ref.at[k],
        send_sem=sends.at[1],
        recv_sem=recvb.at[k],
        device_id=(f, 1 - r, cross_c),
        device_id_type=MESH,
    )
    to_cross.start()

    def relay_copy(e):
        return pltpu.make_async_remote_copy(
            src_ref=col_ref.at[e],
            dst_ref=row_ref.at[2 * k + e],
            send_sem=sends.at[2 + e],
            recv_sem=recvc.at[e],
            device_id=(f, 1 - r, relay_dest),
            device_id_type=MESH,
        )

    def fan_copy(e, base):
        return pltpu.make_async_remote_copy(
            src_ref=row_ref.at[base + e],
            dst_ref=row_ref.at[base + e],
            send_sem=sends.at[4 + e],
            recv_sem=recvd.at[e],
            device_id=(f, r, sib),
            device_id_type=MESH,
        )

    @pl.when(crossing)
    def _():
        for e in range(2):
            pltpu.make_async_remote_copy(
                src_ref=row_ref.at[e],
                dst_ref=col_ref.at[e],
                send_sem=sends.at[1],
                recv_sem=recvb.at[e],
                device_id=(f, 1 - r, 2 * k + e),
                device_id_type=MESH,
            ).wait_recv()
            relay_copy(e).start()

    @pl.when(relay_target)
    def _():
        for e in range(2):
            pltpu.make_async_remote_copy(
                src_ref=col_ref.at[e],
                dst_ref=row_ref.at[2 * (2 - c) + e],
                send_sem=sends.at[2 + e],
                recv_sem=recvc.at[e],
                device_id=(f, 1 - r, relay_src),
                device_id_type=MESH,
            ).wait_recv()
            fan_copy(e, 2 * (2 - c)).start()

    @pl.when(fan_target)
    def _():
        for e in range(2):
            fan_copy(e, 2 * (2 - sib)).wait_recv()

    pltpu.make_async_remote_copy(
        src_ref=row_ref.at[sib],
        dst_ref=row_ref.at[sib],
        send_sem=sends.at[0],
        recv_sem=recva,
        device_id=(f, r, sib),
        device_id_type=MESH,
    ).wait_recv()

    @pl.when(jnp.logical_not(crossing))
    def _():
        half = pltpu.make_async_copy(row_ref.at[pl.ds(2 * k, 2)], col_ref, local_sem)
        half.start()
        half.wait()

    for d in range(1, ny):
        y_copy(d).wait_send()

    def wait_send_z(d, carry):
        z_copy(d).wait_send()
        return carry

    lax.fori_loop(1, nz, wait_send_z, 0)
    to_sib.wait_send()
    to_cross.wait_send()

    @pl.when(crossing)
    def _():
        for e in range(2):
            relay_copy(e).wait_send()

    @pl.when(relay_target)
    def _():
        for e in range(2):
            fan_copy(e, 2 * (2 - c)).wait_send()


def corner_turn(spec):
    ny, nz, rows, width = spec.shape
    nf = ny * nz
    ncol = lax.axis_size("col")
    vmem = pltpu.MemorySpace.VMEM
    return pl.pallas_call(
        turn_kernel,
        out_shape=(
            jax.ShapeDtypeStruct((ncol, nf, rows, width), spec.dtype),
            jax.ShapeDtypeStruct((2, nf, rows, width), spec.dtype),
        ),
        in_specs=[pl.BlockSpec(memory_space=vmem)],
        out_specs=(pl.BlockSpec(memory_space=vmem), pl.BlockSpec(memory_space=vmem)),
        scratch_shapes=[
            pltpu.VMEM((FREQ_Y, nf // FREQ_Y, rows, width), spec.dtype),
            pltpu.SemaphoreType.DMA((FREQ_Y,)),
            pltpu.SemaphoreType.DMA((FREQ_Y,)),
            pltpu.SemaphoreType.DMA((nf // FREQ_Y,)),
            pltpu.SemaphoreType.DMA((nf // FREQ_Y,)),
            pltpu.SemaphoreType.DMA((2,)),
            pltpu.SemaphoreType.DMA((6,)),
            pltpu.SemaphoreType.DMA,
            pltpu.SemaphoreType.DMA((2,)),
            pltpu.SemaphoreType.DMA((2,)),
            pltpu.SemaphoreType.DMA((2,)),
            pltpu.SemaphoreType.DMA,
        ],
        compiler_params=pltpu.CompilerParams(collective_id=0, has_side_effects=True),
    )(spec)


def local(samples, input_gains, filter_taps):
    nf = lax.axis_size("freq")
    channels = CH_DEV * nf
    inputs_here = samples.shape[1]
    table = dft_table_np(channels)
    flat = pfb_dft(samples, input_gains, filter_taps, table)
    spec = flat.astype(jnp.bfloat16).reshape(nf, CH_DEV * inputs_here, 2 * SPEC)
    row_blk, col_blk = corner_turn(spec.reshape(FREQ_Y, nf // FREQ_Y, *spec.shape[1:]))
    row_data = row_blk.reshape(-1, nf, CH_DEV, inputs_here, 2 * SPEC).transpose(2, 0, 1, 3, 4)
    row_data = row_data.reshape(CH_DEV, -1, 2 * SPEC)
    column_data = col_blk.reshape(2, nf, CH_DEV, inputs_here, 2 * SPEC).transpose(2, 0, 1, 3, 4)
    column_data = column_data.reshape(CH_DEV, -1, 2 * SPEC)
    rotated = jnp.concatenate([-column_data[:, :, SPEC:], column_data[:, :, :SPEC]], axis=2)
    vis_real = (
        jnp.einsum("kim,kjm->kij", row_data, column_data, preferred_element_type=jnp.float32)
        * (1.0 / SPEC)
    ).astype(jnp.bfloat16)
    vis_imag = (
        jnp.einsum("kim,kjm->kij", row_data, rotated, preferred_element_type=jnp.float32)
        * (1.0 / SPEC)
    ).astype(jnp.bfloat16)
    return (vis_real, vis_imag)


def solution(mesh):
    placed = (P(None, ("row", "col", "freq"), None), P(("row", "col", "freq")), P())
    return jax.shard_map(
        local,
        mesh=mesh,
        in_specs=placed,
        out_specs=(P("freq", "row", "col"), P("freq", "row", "col")),
        check_vma=False,
    )
```

```python
import math

import numpy as np

import jax
import jax.numpy as jnp
from jax import lax
from jax.experimental import pallas as pl
from jax.experimental.pallas import tpu as pltpu
from jax.sharding import PartitionSpec as P

NFFT = 1024
TAPS = 4
SPEC = 64
CH_DEV = 4


def dft_table_np(channels):
    position = np.arange(NFFT, dtype=np.int64)
    channel = np.arange(channels, dtype=np.int64)
    phases = (position[:, None] * channel[None, :] % NFFT).astype(np.float64) * (2.0 * math.pi / NFFT)
    scaling = 0.5 / math.sqrt(NFFT)
    cosine = np.cos(phases) * scaling
    sine = np.sin(phases) * scaling
    real_rows = np.stack([cosine, -sine], axis=1)
    imag_rows = np.stack([sine, cosine], axis=1)
    table = np.stack([real_rows, imag_rows], axis=0)
    table = table.transpose(2, 3, 0, 1).reshape(2 * channels, 2 * NFFT)
    return jnp.asarray(table, dtype=jnp.bfloat16)


LANES = 128


def pfb_dft_kernel(g_hbm, taps_hbm, s_hbm, tab_hbm, o_ref, g_ref, taps_ref, sbuf, vbuf, tab_buf, f_ref, sems):
    inputs_here, nsamp = s_hbm.shape[1], s_hbm.shape[2]
    frames = nsamp // NFFT
    first = SPEC // 2 + TAPS - 1
    split = first * NFFT
    blocks = NFFT // LANES
    channels = tab_hbm.shape[0] // 2
    parts = []
    for p in range(2):
        head = pltpu.make_async_copy(
            s_hbm.at[p, :, pl.ds(0, split)], sbuf.at[p, :, pl.ds(0, split)], sems.at[2 * p]
        )
        tail = pltpu.make_async_copy(
            s_hbm.at[p, :, pl.ds(split, nsamp - split)],
            sbuf.at[p, :, pl.ds(split, nsamp - split)],
            sems.at[2 * p + 1],
        )
        head.start()
        tail.start()
        parts.append((head, tail))
    tab_cp = pltpu.make_async_copy(tab_hbm, tab_buf, sems.at[4])
    tab_cp.start()
    g_cp = pltpu.make_async_copy(g_hbm, g_ref, sems.at[5])
    g_cp.start()
    taps_cp = pltpu.make_async_copy(taps_hbm, taps_ref, sems.at[6])
    taps_cp.start()
    g_cp.wait()
    taps_cp.wait()

    row = lax.broadcasted_iota(jnp.int32, (inputs_here, NFFT), 0)
    scale = jnp.zeros((inputs_here, NFFT), jnp.float32)
    for i in range(inputs_here):
        scale = jnp.where(row == i, g_ref[i] * 0.25, scale)

    def volts(p, lo, hi):
        def body(j, carry):
            start = pl.multiple_of(j * NFFT, NFFT)
            vbuf[p, j] = sbuf[p, :, pl.ds(start, NFFT)].astype(jnp.float32) * scale
            return carry

        lax.fori_loop(lo, hi, body, 0)

    def filt(p, lo, hi):
        def body(m, carry):
            total = vbuf[p, m] * taps_ref[0:1, :]
            for t in range(1, TAPS):
                total = total + vbuf[p, m + t] * taps_ref[t : t + 1, :]
            rows = pl.ds(pl.multiple_of(m * inputs_here, inputs_here), inputs_here)
            for b in range(blocks):
                f_ref[p * blocks + b, rows, :] = total[:, b * LANES : (b + 1) * LANES]
            return carry

        lax.fori_loop(lo, hi, body, 0)

    for p in range(2):
        head, tail = parts[p]
        head.wait()
        volts(p, 0, first)
        filt(p, 0, SPEC // 2)
        tail.wait()
        volts(p, first, frames)
        filt(p, SPEC // 2, SPEC)

    tab_cp.wait()
    for i in range(inputs_here):
        lhs = jnp.concatenate(
            [f_ref[b, pl.ds(i, SPEC, stride=inputs_here), :] for b in range(2 * blocks)], axis=1
        ).astype(jnp.bfloat16)
        prod = lax.dot_general(
            tab_buf[...], lhs, (((1,), (1,)), ((), ())), preferred_element_type=jnp.float32
        )
        val = jnp.concatenate([prod[:channels], prod[channels:]], axis=1)
        o_ref[pl.ds(i, channels, stride=inputs_here), :] = val


def pfb_dft(samples, gains, taps, table):
    inputs_here, nsamp = samples.shape[1], samples.shape[2]
    channels = table.shape[0] // 2
    frames = nsamp // NFFT
    vmem = pltpu.MemorySpace.VMEM
    return pl.pallas_call(
        pfb_dft_kernel,
        out_shape=jax.ShapeDtypeStruct((channels * inputs_here, 2 * SPEC), jnp.float32),
        in_specs=[pl.BlockSpec(memory_space=pl.ANY)] * 4,
        out_specs=pl.BlockSpec(memory_space=vmem),
        scratch_shapes=[
            pltpu.SMEM((inputs_here,), jnp.float32),
            pltpu.VMEM((TAPS, NFFT), jnp.float32),
            pltpu.VMEM((2, inputs_here, nsamp), jnp.int32),
            pltpu.VMEM((2, frames, inputs_here, NFFT), jnp.float32),
            pltpu.VMEM(table.shape, jnp.bfloat16),
            pltpu.VMEM((2 * NFFT // LANES, SPEC * inputs_here, LANES), jnp.float32),
            pltpu.SemaphoreType.DMA((7,)),
        ],
        compiler_params=pltpu.CompilerParams(vmem_limit_bytes=63 * 1024 * 1024),
    )(gains, taps, samples, table)


MESH = pl.DeviceIdType.MESH


def turn_kernel(
    spec_ref, row_ref, col_ref, send1, recv1, own_sem, sends, recva, recvb, recvc, recvd, local_sem
):
    nf = spec_ref.shape[0]
    f = lax.axis_index("freq")
    r = lax.axis_index("row")
    c = lax.axis_index("col")
    k = c % 2
    h = c // 2
    sib = c + 1 - 2 * k
    cross_c = 2 * r + h
    crossing = h != r
    relay_target = jnp.logical_or(c == 1, c == 2)
    fan_target = jnp.logical_not(relay_target)
    relay_dest = 2 - k
    relay_src = 2 * r + 2 - c

    barrier = pltpu.get_barrier_semaphore()

    def greet_freq(d, carry):
        pl.semaphore_signal(barrier, inc=1, device_id=((f + d) % nf, r, c), device_id_type=MESH)
        return carry

    lax.fori_loop(1, nf, greet_freq, 0)
    pl.semaphore_signal(barrier, inc=1, device_id=(f, r, sib), device_id_type=MESH)
    pl.semaphore_signal(barrier, inc=1, device_id=(f, 1 - r, cross_c), device_id_type=MESH)

    @pl.when(crossing)
    def _():
        for e in range(2):
            pl.semaphore_signal(barrier, inc=1, device_id=(f, 1 - r, 2 * k + e), device_id_type=MESH)
        pl.semaphore_signal(barrier, inc=1, device_id=(f, 1 - r, relay_dest), device_id_type=MESH)

    @pl.when(relay_target)
    def _():
        pl.semaphore_signal(barrier, inc=1, device_id=(f, 1 - r, relay_src), device_id_type=MESH)

    expected = (nf - 1) + 2 + 3 * crossing.astype(jnp.int32) + relay_target.astype(jnp.int32)
    pl.semaphore_wait(barrier, expected)

    own = pltpu.make_async_copy(spec_ref.at[f], row_ref.at[c, f], own_sem)
    own.start()

    def freq_copy(d):
        dest = (f + d) % nf
        return pltpu.make_async_remote_copy(
            src_ref=spec_ref.at[dest],
            dst_ref=row_ref.at[c, f],
            send_sem=send1.at[d],
            recv_sem=recv1.at[f],
            device_id=(dest, r, c),
            device_id_type=MESH,
        )

    def send_freq(d, carry):
        freq_copy(d).start()
        return carry

    lax.fori_loop(1, nf, send_freq, 0)

    def recv_freq(d, carry):
        src = (f + nf - d) % nf
        pltpu.make_async_remote_copy(
            src_ref=spec_ref.at[src],
            dst_ref=row_ref.at[c, src],
            send_sem=send1.at[d],
            recv_sem=recv1.at[src],
            device_id=(src, r, c),
            device_id_type=MESH,
        ).wait_recv()
        return carry

    lax.fori_loop(1, nf, recv_freq, 0)
    own.wait()

    to_sib = pltpu.make_async_remote_copy(
        src_ref=row_ref.at[c],
        dst_ref=row_ref.at[c],
        send_sem=sends.at[0],
        recv_sem=recva,
        device_id=(f, r, sib),
        device_id_type=MESH,
    )
    to_sib.start()
    to_cross = pltpu.make_async_remote_copy(
        src_ref=row_ref.at[c],
        dst_ref=col_ref.at[k],
        send_sem=sends.at[1],
        recv_sem=recvb.at[k],
        device_id=(f, 1 - r, cross_c),
        device_id_type=MESH,
    )
    to_cross.start()

    def relay_copy(e):
        return pltpu.make_async_remote_copy(
            src_ref=col_ref.at[e],
            dst_ref=row_ref.at[2 * k + e],
            send_sem=sends.at[2 + e],
            recv_sem=recvc.at[e],
            device_id=(f, 1 - r, relay_dest),
            device_id_type=MESH,
        )

    def fan_copy(e, base):
        return pltpu.make_async_remote_copy(
            src_ref=row_ref.at[base + e],
            dst_ref=row_ref.at[base + e],
            send_sem=sends.at[4 + e],
            recv_sem=recvd.at[e],
            device_id=(f, r, sib),
            device_id_type=MESH,
        )

    @pl.when(crossing)
    def _():
        for e in range(2):
            pltpu.make_async_remote_copy(
                src_ref=row_ref.at[e],
                dst_ref=col_ref.at[e],
                send_sem=sends.at[1],
                recv_sem=recvb.at[e],
                device_id=(f, 1 - r, 2 * k + e),
                device_id_type=MESH,
            ).wait_recv()
            relay_copy(e).start()

    @pl.when(relay_target)
    def _():
        for e in range(2):
            pltpu.make_async_remote_copy(
                src_ref=col_ref.at[e],
                dst_ref=row_ref.at[2 * (2 - c) + e],
                send_sem=sends.at[2 + e],
                recv_sem=recvc.at[e],
                device_id=(f, 1 - r, relay_src),
                device_id_type=MESH,
            ).wait_recv()
            fan_copy(e, 2 * (2 - c)).start()

    @pl.when(fan_target)
    def _():
        for e in range(2):
            fan_copy(e, 2 * (2 - sib)).wait_recv()

    pltpu.make_async_remote_copy(
        src_ref=row_ref.at[sib],
        dst_ref=row_ref.at[sib],
        send_sem=sends.at[0],
        recv_sem=recva,
        device_id=(f, r, sib),
        device_id_type=MESH,
    ).wait_recv()

    @pl.when(jnp.logical_not(crossing))
    def _():
        half = pltpu.make_async_copy(row_ref.at[pl.ds(2 * k, 2)], col_ref, local_sem)
        half.start()
        half.wait()

    def wait_send_freq(d, carry):
        freq_copy(d).wait_send()
        return carry

    lax.fori_loop(1, nf, wait_send_freq, 0)
    to_sib.wait_send()
    to_cross.wait_send()

    @pl.when(crossing)
    def _():
        for e in range(2):
            relay_copy(e).wait_send()

    @pl.when(relay_target)
    def _():
        for e in range(2):
            fan_copy(e, 2 * (2 - c)).wait_send()


def corner_turn(spec):
    nf, rows, width = spec.shape
    ncol = lax.axis_size("col")
    vmem = pltpu.MemorySpace.VMEM
    return pl.pallas_call(
        turn_kernel,
        out_shape=(
            jax.ShapeDtypeStruct((ncol, nf, rows, width), spec.dtype),
            jax.ShapeDtypeStruct((2, nf, rows, width), spec.dtype),
        ),
        in_specs=[pl.BlockSpec(memory_space=vmem)],
        out_specs=(pl.BlockSpec(memory_space=vmem), pl.BlockSpec(memory_space=vmem)),
        scratch_shapes=[
            pltpu.SemaphoreType.DMA((nf,)),
            pltpu.SemaphoreType.DMA((nf,)),
            pltpu.SemaphoreType.DMA,
            pltpu.SemaphoreType.DMA((6,)),
            pltpu.SemaphoreType.DMA,
            pltpu.SemaphoreType.DMA((2,)),
            pltpu.SemaphoreType.DMA((2,)),
            pltpu.SemaphoreType.DMA((2,)),
            pltpu.SemaphoreType.DMA,
        ],
        compiler_params=pltpu.CompilerParams(collective_id=0, has_side_effects=True),
    )(spec)


def local(samples, input_gains, filter_taps):
    nf = lax.axis_size("freq")
    channels = CH_DEV * nf
    inputs_here = samples.shape[1]
    table = dft_table_np(channels)
    flat = pfb_dft(samples, input_gains, filter_taps, table)
    spec = flat.astype(jnp.bfloat16).reshape(nf, CH_DEV * inputs_here, 2 * SPEC)
    row_blk, col_blk = corner_turn(spec)
    row_data = row_blk.reshape(-1, nf, CH_DEV, inputs_here, 2 * SPEC).transpose(2, 0, 1, 3, 4)
    row_data = row_data.reshape(CH_DEV, -1, 2 * SPEC)
    column_data = col_blk.reshape(2, nf, CH_DEV, inputs_here, 2 * SPEC).transpose(2, 0, 1, 3, 4)
    column_data = column_data.reshape(CH_DEV, -1, 2 * SPEC)
    rotated = jnp.concatenate([-column_data[:, :, SPEC:], column_data[:, :, :SPEC]], axis=2)
    vis_real = (
        jnp.einsum("kim,kjm->kij", row_data, column_data, preferred_element_type=jnp.float32)
        * (1.0 / SPEC)
    ).astype(jnp.bfloat16)
    vis_imag = (
        jnp.einsum("kim,kjm->kij", row_data, rotated, preferred_element_type=jnp.float32)
        * (1.0 / SPEC)
    ).astype(jnp.bfloat16)
    return (vis_real, vis_imag)


def solution(mesh):
    placed = (P(None, ("row", "col", "freq"), None), P(("row", "col", "freq")), P())
    return jax.shard_map(
        local,
        mesh=mesh,
        in_specs=placed,
        out_specs=(P("freq", "row", "col"), P("freq", "row", "col")),
        check_vma=False,
    )
```

```python
import math

import numpy as np

import jax
import jax.numpy as jnp
from jax import lax
from jax.experimental import pallas as pl
from jax.experimental.pallas import tpu as pltpu
from jax.sharding import PartitionSpec as P

NFFT = 1024
TAPS = 4
SPEC = 64
CH_DEV = 4


def dft_table_np(channels):
    position = np.arange(NFFT, dtype=np.int64)
    channel = np.arange(channels, dtype=np.int64)
    phases = (position[:, None] * channel[None, :] % NFFT).astype(np.float64) * (2.0 * math.pi / NFFT)
    scaling = 0.5 / math.sqrt(NFFT)
    cosine = np.cos(phases) * scaling
    sine = np.sin(phases) * scaling
    real_rows = np.stack([cosine, -sine], axis=1)
    imag_rows = np.stack([sine, cosine], axis=1)
    table = np.stack([real_rows, imag_rows], axis=0)
    table = table.transpose(2, 3, 0, 1).reshape(2 * channels, 2 * NFFT)
    return jnp.asarray(table, dtype=jnp.bfloat16)


LANES = 128


def pfb_dft_body(g_hbm, taps_hbm, s_hbm, tab_hbm, o_ref, g_ref, taps_ref, sbuf, vbuf, tab_buf, f_ref, sems, after_start):
    inputs_here, nsamp = s_hbm.shape[1], s_hbm.shape[2]
    frames = nsamp // NFFT
    first = SPEC // 2 + TAPS - 1
    split = first * NFFT
    blocks = NFFT // LANES
    channels = tab_hbm.shape[0] // 2
    parts = []
    for p in range(2):
        head = pltpu.make_async_copy(
            s_hbm.at[p, :, pl.ds(0, split)], sbuf.at[p, :, pl.ds(0, split)], sems.at[2 * p]
        )
        tail = pltpu.make_async_copy(
            s_hbm.at[p, :, pl.ds(split, nsamp - split)],
            sbuf.at[p, :, pl.ds(split, nsamp - split)],
            sems.at[2 * p + 1],
        )
        head.start()
        tail.start()
        parts.append((head, tail))
    tab_cp = pltpu.make_async_copy(tab_hbm, tab_buf, sems.at[4])
    tab_cp.start()
    g_cp = pltpu.make_async_copy(g_hbm, g_ref, sems.at[5])
    g_cp.start()
    taps_cp = pltpu.make_async_copy(taps_hbm, taps_ref, sems.at[6])
    taps_cp.start()
    after_start()
    g_cp.wait()
    taps_cp.wait()

    row = lax.broadcasted_iota(jnp.int32, (inputs_here, NFFT), 0)
    scale = jnp.zeros((inputs_here, NFFT), jnp.float32)
    for i in range(inputs_here):
        scale = jnp.where(row == i, g_ref[i] * 0.25, scale)

    def volts(p, lo, hi):
        def body(j, carry):
            start = pl.multiple_of(j * NFFT, NFFT)
            vbuf[p, j] = sbuf[p, :, pl.ds(start, NFFT)].astype(jnp.float32) * scale
            return carry

        lax.fori_loop(lo, hi, body, 0)

    def filt(p, lo, hi):
        def body(m, carry):
            total = vbuf[p, m] * taps_ref[0:1, :]
            for t in range(1, TAPS):
                total = total + vbuf[p, m + t] * taps_ref[t : t + 1, :]
            rows = pl.ds(pl.multiple_of(m * inputs_here, inputs_here), inputs_here)
            for b in range(blocks):
                f_ref[p * blocks + b, rows, :] = total[:, b * LANES : (b + 1) * LANES]
            return carry

        lax.fori_loop(lo, hi, body, 0)

    for p in range(2):
        head, tail = parts[p]
        head.wait()
        volts(p, 0, first)
        filt(p, 0, SPEC // 2)
        tail.wait()
        volts(p, first, frames)
        filt(p, SPEC // 2, SPEC)

    tab_cp.wait()
    for i in range(inputs_here):
        lhs = jnp.concatenate(
            [f_ref[b, pl.ds(i, SPEC, stride=inputs_here), :] for b in range(2 * blocks)], axis=1
        ).astype(jnp.bfloat16)
        prod = lax.dot_general(
            tab_buf[...], lhs, (((1,), (1,)), ((), ())), preferred_element_type=jnp.float32
        )
        val = jnp.concatenate([prod[:channels], prod[channels:]], axis=1)
        o_ref[pl.ds(i, channels, stride=inputs_here), :] = val


MESH = pl.DeviceIdType.MESH


def fused_kernel(
    g_hbm, taps_hbm, s_hbm, tab_hbm, row_ref, col_ref,
    g_ref, taps_ref, sbuf, vbuf, tab_buf, f_ref, o_scr, spec_ref, pfb_sems,
    send1, recv1, own_sem, sends, recva, recvb, recvc, recvd, local_sem,
):
    nf = spec_ref.shape[0]
    f = lax.axis_index("freq")
    r = lax.axis_index("row")
    c = lax.axis_index("col")
    k = c % 2
    h = c // 2
    sib = c + 1 - 2 * k
    cross_c = 2 * r + h
    crossing = h != r
    relay_target = jnp.logical_or(c == 1, c == 2)
    fan_target = jnp.logical_not(relay_target)
    relay_dest = 2 - k
    relay_src = 2 * r + 2 - c

    def greet_all():
        barrier = pltpu.get_barrier_semaphore()

        def greet_freq(d, carry):
            pl.semaphore_signal(barrier, inc=1, device_id=((f + d) % nf, r, c), device_id_type=MESH)
            return carry

        lax.fori_loop(1, nf, greet_freq, 0)
        pl.semaphore_signal(barrier, inc=1, device_id=(f, r, sib), device_id_type=MESH)
        pl.semaphore_signal(barrier, inc=1, device_id=(f, 1 - r, cross_c), device_id_type=MESH)

        @pl.when(crossing)
        def _():
            for e in range(2):
                pl.semaphore_signal(barrier, inc=1, device_id=(f, 1 - r, 2 * k + e), device_id_type=MESH)
            pl.semaphore_signal(barrier, inc=1, device_id=(f, 1 - r, relay_dest), device_id_type=MESH)

        @pl.when(relay_target)
        def _():
            pl.semaphore_signal(barrier, inc=1, device_id=(f, 1 - r, relay_src), device_id_type=MESH)


    barrier = pltpu.get_barrier_semaphore()
    pfb_dft_body(
        g_hbm, taps_hbm, s_hbm, tab_hbm, o_scr, g_ref, taps_ref, sbuf, vbuf, tab_buf, f_ref,
        pfb_sems, greet_all,
    )
    spec_ref[...] = o_scr[...].astype(spec_ref.dtype).reshape(spec_ref.shape)

    expected = (nf - 1) + 2 + 3 * crossing.astype(jnp.int32) + relay_target.astype(jnp.int32)
    pl.semaphore_wait(barrier, expected)

    own = pltpu.make_async_copy(spec_ref.at[f], row_ref.at[c, f], own_sem)
    own.start()

    def freq_copy(d):
        dest = (f + d) % nf
        return pltpu.make_async_remote_copy(
            src_ref=spec_ref.at[dest],
            dst_ref=row_ref.at[c, f],
            send_sem=send1.at[d],
            recv_sem=recv1.at[f],
            device_id=(dest, r, c),
            device_id_type=MESH,
        )

    def send_freq(d, carry):
        freq_copy(d).start()
        return carry

    lax.fori_loop(1, nf, send_freq, 0)

    def recv_freq(d, carry):
        src = (f + nf - d) % nf
        pltpu.make_async_remote_copy(
            src_ref=spec_ref.at[src],
            dst_ref=row_ref.at[c, src],
            send_sem=send1.at[d],
            recv_sem=recv1.at[src],
            device_id=(src, r, c),
            device_id_type=MESH,
        ).wait_recv()
        return carry

    lax.fori_loop(1, nf, recv_freq, 0)
    own.wait()

    to_sib = pltpu.make_async_remote_copy(
        src_ref=row_ref.at[c],
        dst_ref=row_ref.at[c],
        send_sem=sends.at[0],
        recv_sem=recva,
        device_id=(f, r, sib),
        device_id_type=MESH,
    )
    to_sib.start()
    to_cross = pltpu.make_async_remote_copy(
        src_ref=row_ref.at[c],
        dst_ref=col_ref.at[k],
        send_sem=sends.at[1],
        recv_sem=recvb.at[k],
        device_id=(f, 1 - r, cross_c),
        device_id_type=MESH,
    )
    to_cross.start()

    def relay_copy(e):
        return pltpu.make_async_remote_copy(
            src_ref=col_ref.at[e],
            dst_ref=row_ref.at[2 * k + e],
            send_sem=sends.at[2 + e],
            recv_sem=recvc.at[e],
            device_id=(f, 1 - r, relay_dest),
            device_id_type=MESH,
        )

    def fan_copy(e, base):
        return pltpu.make_async_remote_copy(
            src_ref=row_ref.at[base + e],
            dst_ref=row_ref.at[base + e],
            send_sem=sends.at[4 + e],
            recv_sem=recvd.at[e],
            device_id=(f, r, sib),
            device_id_type=MESH,
        )

    @pl.when(crossing)
    def _():
        for e in range(2):
            pltpu.make_async_remote_copy(
                src_ref=row_ref.at[e],
                dst_ref=col_ref.at[e],
                send_sem=sends.at[1],
                recv_sem=recvb.at[e],
                device_id=(f, 1 - r, 2 * k + e),
                device_id_type=MESH,
            ).wait_recv()
            relay_copy(e).start()

    @pl.when(relay_target)
    def _():
        for e in range(2):
            pltpu.make_async_remote_copy(
                src_ref=col_ref.at[e],
                dst_ref=row_ref.at[2 * (2 - c) + e],
                send_sem=sends.at[2 + e],
                recv_sem=recvc.at[e],
                device_id=(f, 1 - r, relay_src),
                device_id_type=MESH,
            ).wait_recv()
            fan_copy(e, 2 * (2 - c)).start()

    @pl.when(fan_target)
    def _():
        for e in range(2):
            fan_copy(e, 2 * (2 - sib)).wait_recv()

    pltpu.make_async_remote_copy(
        src_ref=row_ref.at[sib],
        dst_ref=row_ref.at[sib],
        send_sem=sends.at[0],
        recv_sem=recva,
        device_id=(f, r, sib),
        device_id_type=MESH,
    ).wait_recv()

    @pl.when(jnp.logical_not(crossing))
    def _():
        half = pltpu.make_async_copy(row_ref.at[pl.ds(2 * k, 2)], col_ref, local_sem)
        half.start()
        half.wait()

    def wait_send_freq(d, carry):
        freq_copy(d).wait_send()
        return carry

    lax.fori_loop(1, nf, wait_send_freq, 0)
    to_sib.wait_send()
    to_cross.wait_send()

    @pl.when(crossing)
    def _():
        for e in range(2):
            relay_copy(e).wait_send()

    @pl.when(relay_target)
    def _():
        for e in range(2):
            fan_copy(e, 2 * (2 - c)).wait_send()


def fused_call(samples, gains, taps, table):
    inputs_here, nsamp = samples.shape[1], samples.shape[2]
    channels = table.shape[0] // 2
    frames = nsamp // NFFT
    nf = channels // CH_DEV
    rows = CH_DEV * inputs_here
    width = 2 * SPEC
    ncol = lax.axis_size("col")
    vmem = pltpu.MemorySpace.VMEM
    return pl.pallas_call(
        fused_kernel,
        out_shape=(
            jax.ShapeDtypeStruct((ncol, nf, rows, width), jnp.bfloat16),
            jax.ShapeDtypeStruct((2, nf, rows, width), jnp.bfloat16),
        ),
        in_specs=[pl.BlockSpec(memory_space=pl.ANY)] * 4,
        out_specs=(pl.BlockSpec(memory_space=vmem), pl.BlockSpec(memory_space=vmem)),
        scratch_shapes=[
            pltpu.SMEM((inputs_here,), jnp.float32),
            pltpu.VMEM((TAPS, NFFT), jnp.float32),
            pltpu.VMEM((2, inputs_here, nsamp), jnp.int32),
            pltpu.VMEM((2, frames, inputs_here, NFFT), jnp.float32),
            pltpu.VMEM(table.shape, jnp.bfloat16),
            pltpu.VMEM((2 * NFFT // LANES, SPEC * inputs_here, LANES), jnp.float32),
            pltpu.VMEM((channels * inputs_here, width), jnp.float32),
            pltpu.VMEM((nf, rows, width), jnp.bfloat16),
            pltpu.SemaphoreType.DMA((7,)),
            pltpu.SemaphoreType.DMA((nf,)),
            pltpu.SemaphoreType.DMA((nf,)),
            pltpu.SemaphoreType.DMA,
            pltpu.SemaphoreType.DMA((6,)),
            pltpu.SemaphoreType.DMA,
            pltpu.SemaphoreType.DMA((2,)),
            pltpu.SemaphoreType.DMA((2,)),
            pltpu.SemaphoreType.DMA((2,)),
            pltpu.SemaphoreType.DMA,
        ],
        compiler_params=pltpu.CompilerParams(
            collective_id=0, has_side_effects=True, vmem_limit_bytes=63 * 1024 * 1024
        ),
    )(gains, taps, samples, table)


def local(samples, input_gains, filter_taps):
    nf = lax.axis_size("freq")
    channels = CH_DEV * nf
    inputs_here = samples.shape[1]
    table = dft_table_np(channels)
    row_blk, col_blk = fused_call(samples, input_gains, filter_taps, table)
    row_data = row_blk.reshape(-1, nf, CH_DEV, inputs_here, 2 * SPEC).transpose(2, 0, 1, 3, 4)
    row_data = row_data.reshape(CH_DEV, -1, 2 * SPEC)
    column_data = col_blk.reshape(2, nf, CH_DEV, inputs_here, 2 * SPEC).transpose(2, 0, 1, 3, 4)
    column_data = column_data.reshape(CH_DEV, -1, 2 * SPEC)
    rotated = jnp.concatenate([-column_data[:, :, SPEC:], column_data[:, :, :SPEC]], axis=2)
    vis_real = (
        jnp.einsum("kim,kjm->kij", row_data, column_data, preferred_element_type=jnp.float32)
        * (1.0 / SPEC)
    ).astype(jnp.bfloat16)
    vis_imag = (
        jnp.einsum("kim,kjm->kij", row_data, rotated, preferred_element_type=jnp.float32)
        * (1.0 / SPEC)
    ).astype(jnp.bfloat16)
    return (vis_real, vis_imag)


def solution(mesh):
    placed = (P(None, ("row", "col", "freq"), None), P(("row", "col", "freq")), P())
    return jax.shard_map(
        local,
        mesh=mesh,
        in_specs=placed,
        out_specs=(P("freq", "row", "col"), P("freq", "row", "col")),
        check_vma=False,
    )
```

```python
import math

import numpy as np

import jax
import jax.numpy as jnp
from jax import lax
from jax.experimental import pallas as pl
from jax.experimental.pallas import tpu as pltpu
from jax.sharding import PartitionSpec as P

NFFT = 1024
TAPS = 4
SPEC = 64
CH_DEV = 4


def dft_table_np(channels):
    position = np.arange(NFFT, dtype=np.int64)
    channel = np.arange(channels, dtype=np.int64)
    phases = (position[:, None] * channel[None, :] % NFFT).astype(np.float64) * (2.0 * math.pi / NFFT)
    scaling = 0.5 / math.sqrt(NFFT)
    cosine = np.cos(phases) * scaling
    sine = np.sin(phases) * scaling
    real_rows = np.stack([cosine, -sine], axis=1)
    imag_rows = np.stack([sine, cosine], axis=1)
    table = np.stack([real_rows, imag_rows], axis=0)
    table = table.transpose(2, 3, 0, 1).reshape(2 * channels, 2 * NFFT)
    return jnp.asarray(table, dtype=jnp.bfloat16)


LANES = 128


def pfb_dft_body(g_hbm, taps_hbm, s_hbm, tab_hbm, o_ref, g_ref, taps_ref, sbuf, vbuf, tab_buf, f_ref, sems, after_start):
    inputs_here, nsamp = s_hbm.shape[1], s_hbm.shape[2]
    frames = nsamp // NFFT
    first = SPEC // 2 + TAPS - 1
    split = first * NFFT
    blocks = NFFT // LANES
    channels = tab_hbm.shape[0] // 2
    parts = []
    for p in range(2):
        head = pltpu.make_async_copy(
            s_hbm.at[p, :, pl.ds(0, split)], sbuf.at[p, :, pl.ds(0, split)], sems.at[2 * p]
        )
        tail = pltpu.make_async_copy(
            s_hbm.at[p, :, pl.ds(split, nsamp - split)],
            sbuf.at[p, :, pl.ds(split, nsamp - split)],
            sems.at[2 * p + 1],
        )
        head.start()
        tail.start()
        parts.append((head, tail))
    tab_cp = pltpu.make_async_copy(tab_hbm, tab_buf, sems.at[4])
    tab_cp.start()
    g_cp = pltpu.make_async_copy(g_hbm, g_ref, sems.at[5])
    g_cp.start()
    taps_cp = pltpu.make_async_copy(taps_hbm, taps_ref, sems.at[6])
    taps_cp.start()
    after_start()
    g_cp.wait()
    taps_cp.wait()

    row = lax.broadcasted_iota(jnp.int32, (inputs_here, NFFT), 0)
    scale = jnp.zeros((inputs_here, NFFT), jnp.float32)
    for i in range(inputs_here):
        scale = jnp.where(row == i, g_ref[i] * 0.25, scale)

    def volts(p, lo, hi):
        def body(j, carry):
            start = pl.multiple_of(j * NFFT, NFFT)
            vbuf[p, j] = sbuf[p, :, pl.ds(start, NFFT)].astype(jnp.float32) * scale
            return carry

        lax.fori_loop(lo, hi, body, 0)

    def filt(p, lo, hi):
        def body(m, carry):
            total = vbuf[p, m] * taps_ref[0:1, :]
            for t in range(1, TAPS):
                total = total + vbuf[p, m + t] * taps_ref[t : t + 1, :]
            rows = pl.ds(pl.multiple_of(m * inputs_here, inputs_here), inputs_here)
            for b in range(blocks):
                f_ref[p * blocks + b, rows, :] = total[:, b * LANES : (b + 1) * LANES]
            return carry

        lax.fori_loop(lo, hi, body, 0)

    for p in range(2):
        head, tail = parts[p]
        head.wait()
        volts(p, 0, first)
        filt(p, 0, SPEC // 2)
        tail.wait()
        volts(p, first, frames)
        filt(p, SPEC // 2, SPEC)

    tab_cp.wait()
    for i in range(inputs_here):
        lhs = jnp.concatenate(
            [f_ref[b, pl.ds(i, SPEC, stride=inputs_here), :] for b in range(2 * blocks)], axis=1
        ).astype(jnp.bfloat16)
        prod = lax.dot_general(
            tab_buf[...], lhs, (((1,), (1,)), ((), ())), preferred_element_type=jnp.float32
        )
        val = jnp.concatenate([prod[:channels], prod[channels:]], axis=1)
        o_ref[pl.ds(i, channels, stride=inputs_here), :] = val


MESH = pl.DeviceIdType.MESH


def fused_kernel(
    g_hbm, taps_hbm, s_hbm, tab_hbm, row_ref, col_ref,
    g_ref, taps_ref, sbuf, vbuf, tab_buf, f_ref, o_scr, spec_ref, pfb_sems,
    send1, recv1, own_sem, sends, recva, recvb, recvc, recvd, local_sem,
):
    nf = spec_ref.shape[0]
    f = lax.axis_index("freq")
    r = lax.axis_index("row")
    c = lax.axis_index("col")
    k = c % 2
    h = c // 2
    sib = c + 1 - 2 * k
    cross_c = 2 * r + h
    crossing = h != r
    relay_target = jnp.logical_or(c == 1, c == 2)
    fan_target = jnp.logical_not(relay_target)
    relay_dest = 2 - k
    relay_src = 2 * r + 2 - c

    def greet_all():
        barrier = pltpu.get_barrier_semaphore()

        def greet_freq(d, carry):
            pl.semaphore_signal(barrier, inc=1, device_id=((f + d) % nf, r, c), device_id_type=MESH)
            return carry

        lax.fori_loop(1, nf, greet_freq, 0)
        pl.semaphore_signal(barrier, inc=1, device_id=(f, r, sib), device_id_type=MESH)
        pl.semaphore_signal(barrier, inc=1, device_id=(f, 1 - r, cross_c), device_id_type=MESH)

        @pl.when(crossing)
        def _():
            for e in range(2):
                pl.semaphore_signal(barrier, inc=1, device_id=(f, 1 - r, 2 * k + e), device_id_type=MESH)
            pl.semaphore_signal(barrier, inc=1, device_id=(f, 1 - r, relay_dest), device_id_type=MESH)

        @pl.when(relay_target)
        def _():
            pl.semaphore_signal(barrier, inc=1, device_id=(f, 1 - r, relay_src), device_id_type=MESH)


    barrier = pltpu.get_barrier_semaphore()
    pfb_dft_body(
        g_hbm, taps_hbm, s_hbm, tab_hbm, o_scr, g_ref, taps_ref, sbuf, vbuf, tab_buf, f_ref,
        pfb_sems, greet_all,
    )
    spec_ref[...] = o_scr[...].astype(spec_ref.dtype).reshape(spec_ref.shape)

    expected = (nf - 1) + 2 + 3 * crossing.astype(jnp.int32) + relay_target.astype(jnp.int32)
    pl.semaphore_wait(barrier, expected)

    own = pltpu.make_async_copy(spec_ref.at[f], row_ref.at[c, f], own_sem)
    own.start()

    def freq_copy(d):
        dest = (f + d) % nf
        return pltpu.make_async_remote_copy(
            src_ref=spec_ref.at[dest],
            dst_ref=row_ref.at[c, f],
            send_sem=send1.at[d],
            recv_sem=recv1.at[f],
            device_id=(dest, r, c),
            device_id_type=MESH,
        )

    def send_freq(d, carry):
        freq_copy(d).start()
        return carry

    lax.fori_loop(1, nf, send_freq, 0)

    def recv_freq(d, carry):
        src = (f + nf - d) % nf
        pltpu.make_async_remote_copy(
            src_ref=spec_ref.at[src],
            dst_ref=row_ref.at[c, src],
            send_sem=send1.at[d],
            recv_sem=recv1.at[src],
            device_id=(src, r, c),
            device_id_type=MESH,
        ).wait_recv()
        return carry

    lax.fori_loop(1, nf, recv_freq, 0)
    own.wait()

    to_sib = pltpu.make_async_remote_copy(
        src_ref=row_ref.at[c],
        dst_ref=row_ref.at[c],
        send_sem=sends.at[0],
        recv_sem=recva,
        device_id=(f, r, sib),
        device_id_type=MESH,
    )
    to_sib.start()
    to_cross = pltpu.make_async_remote_copy(
        src_ref=row_ref.at[c],
        dst_ref=col_ref.at[k],
        send_sem=sends.at[1],
        recv_sem=recvb.at[k],
        device_id=(f, 1 - r, cross_c),
        device_id_type=MESH,
    )
    to_cross.start()

    def relay_copy(e):
        return pltpu.make_async_remote_copy(
            src_ref=col_ref.at[e],
            dst_ref=row_ref.at[2 * k + e],
            send_sem=sends.at[2 + e],
            recv_sem=recvc.at[e],
            device_id=(f, 1 - r, relay_dest),
            device_id_type=MESH,
        )

    def fan_copy(e, base):
        return pltpu.make_async_remote_copy(
            src_ref=row_ref.at[base + e],
            dst_ref=row_ref.at[base + e],
            send_sem=sends.at[4 + e],
            recv_sem=recvd.at[e],
            device_id=(f, r, sib),
            device_id_type=MESH,
        )

    @pl.when(crossing)
    def _():
        for e in range(2):
            pltpu.make_async_remote_copy(
                src_ref=row_ref.at[e],
                dst_ref=col_ref.at[e],
                send_sem=sends.at[1],
                recv_sem=recvb.at[e],
                device_id=(f, 1 - r, 2 * k + e),
                device_id_type=MESH,
            ).wait_recv()
            relay_copy(e).start()

    @pl.when(relay_target)
    def _():
        for e in range(2):
            pltpu.make_async_remote_copy(
                src_ref=col_ref.at[e],
                dst_ref=row_ref.at[2 * (2 - c) + e],
                send_sem=sends.at[2 + e],
                recv_sem=recvc.at[e],
                device_id=(f, 1 - r, relay_src),
                device_id_type=MESH,
            ).wait_recv()
            fan_copy(e, 2 * (2 - c)).start()

    @pl.when(fan_target)
    def _():
        for e in range(2):
            fan_copy(e, 2 * (2 - sib)).wait_recv()

    pltpu.make_async_remote_copy(
        src_ref=row_ref.at[sib],
        dst_ref=row_ref.at[sib],
        send_sem=sends.at[0],
        recv_sem=recva,
        device_id=(f, r, sib),
        device_id_type=MESH,
    ).wait_recv()

    @pl.when(jnp.logical_not(crossing))
    def _():
        half = pltpu.make_async_copy(row_ref.at[pl.ds(2 * k, 2)], col_ref, local_sem)
        half.start()
        half.wait()

    def wait_send_freq(d, carry):
        freq_copy(d).wait_send()
        return carry

    lax.fori_loop(1, nf, wait_send_freq, 0)
    to_sib.wait_send()
    to_cross.wait_send()

    @pl.when(crossing)
    def _():
        for e in range(2):
            relay_copy(e).wait_send()

    @pl.when(relay_target)
    def _():
        for e in range(2):
            fan_copy(e, 2 * (2 - c)).wait_send()


def fused_call(samples, gains, taps, table):
    inputs_here, nsamp = samples.shape[1], samples.shape[2]
    channels = table.shape[0] // 2
    frames = nsamp // NFFT
    nf = channels // CH_DEV
    rows = CH_DEV * inputs_here
    width = 2 * SPEC
    ncol = lax.axis_size("col")
    vmem = pltpu.MemorySpace.VMEM
    return pl.pallas_call(
        fused_kernel,
        out_shape=(
            jax.ShapeDtypeStruct((ncol, nf, rows, width), jnp.bfloat16),
            jax.ShapeDtypeStruct((2, nf, rows, width), jnp.bfloat16),
        ),
        in_specs=[pl.BlockSpec(memory_space=pl.ANY)] * 4,
        out_specs=(pl.BlockSpec(memory_space=vmem), pl.BlockSpec(memory_space=vmem)),
        scratch_shapes=[
            pltpu.SMEM((inputs_here,), jnp.float32),
            pltpu.VMEM((TAPS, NFFT), jnp.float32),
            pltpu.VMEM((2, inputs_here, nsamp), jnp.int32),
            pltpu.VMEM((2, frames, inputs_here, NFFT), jnp.float32),
            pltpu.VMEM(table.shape, jnp.bfloat16),
            pltpu.VMEM((2 * NFFT // LANES, SPEC * inputs_here, LANES), jnp.float32),
            pltpu.VMEM((channels * inputs_here, width), jnp.float32),
            pltpu.VMEM((nf, rows, width), jnp.bfloat16),
            pltpu.SemaphoreType.DMA((7,)),
            pltpu.SemaphoreType.DMA((nf,)),
            pltpu.SemaphoreType.DMA((nf,)),
            pltpu.SemaphoreType.DMA,
            pltpu.SemaphoreType.DMA((6,)),
            pltpu.SemaphoreType.DMA,
            pltpu.SemaphoreType.DMA((2,)),
            pltpu.SemaphoreType.DMA((2,)),
            pltpu.SemaphoreType.DMA((2,)),
            pltpu.SemaphoreType.DMA,
        ],
        compiler_params=pltpu.CompilerParams(
            collective_id=0, has_side_effects=True, vmem_limit_bytes=63 * 1024 * 1024
        ),
    )(gains, taps, samples, table)


def local(samples, input_gains, filter_taps):
    nf = lax.axis_size("freq")
    channels = CH_DEV * nf
    inputs_here = samples.shape[1]
    table = dft_table_np(channels)
    row_blk, col_blk = fused_call(samples, input_gains, filter_taps, table)
    return visibilities(row_blk, col_blk)


def vis_kernel(row_ref, col_ref, vr_ref, vi_ref, a_scr, b_scr):
    kk = pl.program_id(0)
    groups = row_ref.shape[2] // CH_DEV

    @pl.when(kk == 0)
    def _():
        rows = row_ref[...].astype(jnp.float32)
        cols = col_ref[...].astype(jnp.float32)
        for j in range(CH_DEV):
            a = rows[:, :, j * groups : (j + 1) * groups, :]
            a_scr[j] = a.reshape(-1, a.shape[-1]).astype(a_scr.dtype)
            b = cols[:, :, j * groups : (j + 1) * groups, :]
            b = b.reshape(-1, b.shape[-1])
            b_scr[j, 0] = b.astype(b_scr.dtype)
            b_scr[j, 1] = jnp.concatenate([-b[:, SPEC:], b[:, :SPEC]], axis=1).astype(b_scr.dtype)

    a = a_scr[kk]
    dims = (((1,), (1,)), ((), ()))
    vr = lax.dot_general(a, b_scr[kk, 0], dims, preferred_element_type=jnp.float32)
    vr_ref[0] = (vr * (1.0 / SPEC)).astype(vr_ref.dtype)
    vi = lax.dot_general(a, b_scr[kk, 1], dims, preferred_element_type=jnp.float32)
    vi_ref[0] = (vi * (1.0 / SPEC)).astype(vi_ref.dtype)


def visibilities(row_blk, col_blk):
    nrow = row_blk.shape[0] * row_blk.shape[1] * row_blk.shape[2] // CH_DEV
    ncolumn = col_blk.shape[0] * col_blk.shape[1] * col_blk.shape[2] // CH_DEV
    width = row_blk.shape[3]
    out = jax.ShapeDtypeStruct((CH_DEV, nrow, ncolumn), jnp.bfloat16)
    return pl.pallas_call(
        vis_kernel,
        grid=(CH_DEV,),
        out_shape=(out, out),
        in_specs=[
            pl.BlockSpec(row_blk.shape, lambda k: (0, 0, 0, 0)),
            pl.BlockSpec(col_blk.shape, lambda k: (0, 0, 0, 0)),
        ],
        out_specs=(
            pl.BlockSpec((1, nrow, ncolumn), lambda k: (k, 0, 0)),
            pl.BlockSpec((1, nrow, ncolumn), lambda k: (k, 0, 0)),
        ),
        scratch_shapes=[
            pltpu.VMEM((CH_DEV, nrow, width), jnp.bfloat16),
            pltpu.VMEM((CH_DEV, 2, ncolumn, width), jnp.bfloat16),
        ],
        compiler_params=pltpu.CompilerParams(vmem_limit_bytes=48 * 1024 * 1024),
    )(row_blk, col_blk)


def solution(mesh):
    placed = (P(None, ("row", "col", "freq"), None), P(("row", "col", "freq")), P())
    return jax.shard_map(
        local,
        mesh=mesh,
        in_specs=placed,
        out_specs=(P("freq", "row", "col"), P("freq", "row", "col")),
        check_vma=False,
    )
```

```python
import math

import numpy as np

import jax
import jax.numpy as jnp
from jax import lax
from jax.experimental import pallas as pl
from jax.experimental.pallas import tpu as pltpu
from jax.sharding import PartitionSpec as P

NFFT = 1024
TAPS = 4
SPEC = 64
CH_DEV = 4


def dft_table_np(channels):
    position = np.arange(NFFT, dtype=np.int64)
    channel = np.arange(channels, dtype=np.int64)
    phases = (position[:, None] * channel[None, :] % NFFT).astype(np.float64) * (2.0 * math.pi / NFFT)
    scaling = 0.5 / math.sqrt(NFFT)
    cosine = np.cos(phases) * scaling
    sine = np.sin(phases) * scaling
    real_rows = np.stack([cosine, -sine], axis=1)
    imag_rows = np.stack([sine, cosine], axis=1)
    table = np.stack([real_rows, imag_rows], axis=0)
    table = table.transpose(2, 3, 0, 1).reshape(2 * channels, 2 * NFFT)
    return jnp.asarray(table, dtype=jnp.bfloat16)


LANES = 128


def pfb_dft_body(g_hbm, taps_hbm, s_hbm, tab_hbm, o_ref, g_ref, taps_ref, sbuf, vbuf, tab_buf, f_ref, sems, after_start):
    inputs_here, nsamp = s_hbm.shape[1], s_hbm.shape[2]
    frames = nsamp // NFFT
    first = SPEC // 2 + TAPS - 1
    split = first * NFFT
    blocks = NFFT // LANES
    channels = tab_hbm.shape[0] // 2
    parts = []
    for p in range(2):
        head = pltpu.make_async_copy(
            s_hbm.at[p, :, pl.ds(0, split)], sbuf.at[p, :, pl.ds(0, split)], sems.at[2 * p]
        )
        tail = pltpu.make_async_copy(
            s_hbm.at[p, :, pl.ds(split, nsamp - split)],
            sbuf.at[p, :, pl.ds(split, nsamp - split)],
            sems.at[2 * p + 1],
        )
        head.start()
        tail.start()
        parts.append((head, tail))
    tab_cp = pltpu.make_async_copy(tab_hbm, tab_buf, sems.at[4])
    tab_cp.start()
    g_cp = pltpu.make_async_copy(g_hbm, g_ref, sems.at[5])
    g_cp.start()
    taps_cp = pltpu.make_async_copy(taps_hbm, taps_ref, sems.at[6])
    taps_cp.start()
    after_start()
    g_cp.wait()
    taps_cp.wait()

    row = lax.broadcasted_iota(jnp.int32, (inputs_here, NFFT), 0)
    scale = jnp.zeros((inputs_here, NFFT), jnp.float32)
    for i in range(inputs_here):
        scale = jnp.where(row == i, g_ref[i] * 0.25, scale)

    def volts(p, lo, hi):
        def body(j, carry):
            start = pl.multiple_of(j * NFFT, NFFT)
            vbuf[p, j] = sbuf[p, :, pl.ds(start, NFFT)].astype(jnp.float32) * scale
            return carry

        lax.fori_loop(lo, hi, body, 0)

    def filt(p, lo, hi):
        def body(m, carry):
            total = vbuf[p, m] * taps_ref[0:1, :]
            for t in range(1, TAPS):
                total = total + vbuf[p, m + t] * taps_ref[t : t + 1, :]
            rows = pl.ds(pl.multiple_of(m * inputs_here, inputs_here), inputs_here)
            for b in range(blocks):
                f_ref[p * blocks + b, rows, :] = total[:, b * LANES : (b + 1) * LANES]
            return carry

        lax.fori_loop(lo, hi, body, 0)

    for p in range(2):
        head, tail = parts[p]
        head.wait()
        volts(p, 0, first)
        filt(p, 0, SPEC // 2)
        tail.wait()
        volts(p, first, frames)
        filt(p, SPEC // 2, SPEC)

    tab_cp.wait()
    for i in range(inputs_here):
        lhs = jnp.concatenate(
            [f_ref[b, pl.ds(i, SPEC, stride=inputs_here), :] for b in range(2 * blocks)], axis=1
        ).astype(jnp.bfloat16)
        prod = lax.dot_general(
            tab_buf[...], lhs, (((1,), (1,)), ((), ())), preferred_element_type=jnp.float32
        )
        val = jnp.concatenate([prod[:channels], prod[channels:]], axis=1)
        o_ref[pl.ds(i, channels, stride=inputs_here), :] = val


MESH = pl.DeviceIdType.MESH


def fused_kernel(
    g_hbm, taps_hbm, s_hbm, tab_hbm, row_ref, col_ref,
    g_ref, taps_ref, sbuf, vbuf, tab_buf, f_ref, o_scr, spec_ref, pfb_sems,
    send1, recv1, own_sem, sends, recva, recvb, recvc, recvd, local_sem,
):
    nf = spec_ref.shape[0]
    f = lax.axis_index("freq")
    r = lax.axis_index("row")
    c = lax.axis_index("col")
    k = c % 2
    h = c // 2
    sib = c + 1 - 2 * k
    cross_c = 2 * r + h
    crossing = h != r
    relay_target = jnp.logical_or(c == 1, c == 2)
    fan_target = jnp.logical_not(relay_target)
    relay_dest = 2 - k
    relay_src = 2 * r + 2 - c

    def greet_all():
        barrier = pltpu.get_barrier_semaphore()

        def greet_freq(d, carry):
            pl.semaphore_signal(barrier, inc=1, device_id=((f + d) % nf, r, c), device_id_type=MESH)
            return carry

        lax.fori_loop(1, nf, greet_freq, 0)
        pl.semaphore_signal(barrier, inc=1, device_id=(f, r, sib), device_id_type=MESH)
        pl.semaphore_signal(barrier, inc=1, device_id=(f, 1 - r, cross_c), device_id_type=MESH)

        @pl.when(crossing)
        def _():
            for e in range(2):
                pl.semaphore_signal(barrier, inc=1, device_id=(f, 1 - r, 2 * k + e), device_id_type=MESH)
            pl.semaphore_signal(barrier, inc=1, device_id=(f, 1 - r, relay_dest), device_id_type=MESH)

        @pl.when(relay_target)
        def _():
            pl.semaphore_signal(barrier, inc=1, device_id=(f, 1 - r, relay_src), device_id_type=MESH)


    barrier = pltpu.get_barrier_semaphore()
    pfb_dft_body(
        g_hbm, taps_hbm, s_hbm, tab_hbm, o_scr, g_ref, taps_ref, sbuf, vbuf, tab_buf, f_ref,
        pfb_sems, greet_all,
    )
    spec_ref[...] = o_scr[...].astype(spec_ref.dtype).reshape(spec_ref.shape)

    expected = (nf - 1) + 2 + 3 * crossing.astype(jnp.int32) + relay_target.astype(jnp.int32)
    pl.semaphore_wait(barrier, expected)

    own = pltpu.make_async_copy(spec_ref.at[f], row_ref.at[c, f], own_sem)
    own.start()

    def freq_copy(d):
        dest = (f + d) % nf
        return pltpu.make_async_remote_copy(
            src_ref=spec_ref.at[dest],
            dst_ref=row_ref.at[c, f],
            send_sem=send1.at[d],
            recv_sem=recv1.at[f],
            device_id=(dest, r, c),
            device_id_type=MESH,
        )

    def send_freq(d, carry):
        freq_copy(d).start()
        return carry

    lax.fori_loop(1, nf, send_freq, 0)

    def recv_freq(d, carry):
        src = (f + nf - d) % nf
        pltpu.make_async_remote_copy(
            src_ref=spec_ref.at[src],
            dst_ref=row_ref.at[c, src],
            send_sem=send1.at[d],
            recv_sem=recv1.at[src],
            device_id=(src, r, c),
            device_id_type=MESH,
        ).wait_recv()
        return carry

    lax.fori_loop(1, nf, recv_freq, 0)
    own.wait()

    to_sib = pltpu.make_async_remote_copy(
        src_ref=row_ref.at[c],
        dst_ref=row_ref.at[c],
        send_sem=sends.at[0],
        recv_sem=recva,
        device_id=(f, r, sib),
        device_id_type=MESH,
    )
    to_sib.start()
    to_cross = pltpu.make_async_remote_copy(
        src_ref=row_ref.at[c],
        dst_ref=col_ref.at[k],
        send_sem=sends.at[1],
        recv_sem=recvb.at[k],
        device_id=(f, 1 - r, cross_c),
        device_id_type=MESH,
    )
    to_cross.start()

    def relay_copy(e):
        return pltpu.make_async_remote_copy(
            src_ref=col_ref.at[e],
            dst_ref=row_ref.at[2 * k + e],
            send_sem=sends.at[2 + e],
            recv_sem=recvc.at[e],
            device_id=(f, 1 - r, relay_dest),
            device_id_type=MESH,
        )

    def fan_copy(e, base):
        return pltpu.make_async_remote_copy(
            src_ref=row_ref.at[base + e],
            dst_ref=row_ref.at[base + e],
            send_sem=sends.at[4 + e],
            recv_sem=recvd.at[e],
            device_id=(f, r, sib),
            device_id_type=MESH,
        )

    @pl.when(crossing)
    def _():
        for e in range(2):
            pltpu.make_async_remote_copy(
                src_ref=row_ref.at[e],
                dst_ref=col_ref.at[e],
                send_sem=sends.at[1],
                recv_sem=recvb.at[e],
                device_id=(f, 1 - r, 2 * k + e),
                device_id_type=MESH,
            ).wait_recv()
            relay_copy(e).start()

    @pl.when(relay_target)
    def _():
        for e in range(2):
            pltpu.make_async_remote_copy(
                src_ref=col_ref.at[e],
                dst_ref=row_ref.at[2 * (2 - c) + e],
                send_sem=sends.at[2 + e],
                recv_sem=recvc.at[e],
                device_id=(f, 1 - r, relay_src),
                device_id_type=MESH,
            ).wait_recv()
            fan_copy(e, 2 * (2 - c)).start()

    @pl.when(fan_target)
    def _():
        for e in range(2):
            fan_copy(e, 2 * (2 - sib)).wait_recv()

    pltpu.make_async_remote_copy(
        src_ref=row_ref.at[sib],
        dst_ref=row_ref.at[sib],
        send_sem=sends.at[0],
        recv_sem=recva,
        device_id=(f, r, sib),
        device_id_type=MESH,
    ).wait_recv()

    @pl.when(jnp.logical_not(crossing))
    def _():
        half = pltpu.make_async_copy(row_ref.at[pl.ds(2 * k, 2)], col_ref, local_sem)
        half.start()
        half.wait()

    def wait_send_freq(d, carry):
        freq_copy(d).wait_send()
        return carry

    lax.fori_loop(1, nf, wait_send_freq, 0)
    to_sib.wait_send()
    to_cross.wait_send()

    @pl.when(crossing)
    def _():
        for e in range(2):
            relay_copy(e).wait_send()

    @pl.when(relay_target)
    def _():
        for e in range(2):
            fan_copy(e, 2 * (2 - c)).wait_send()


def fused_call(samples, gains, taps, table):
    inputs_here, nsamp = samples.shape[1], samples.shape[2]
    channels = table.shape[0] // 2
    frames = nsamp // NFFT
    nf = channels // CH_DEV
    rows = CH_DEV * inputs_here
    width = 2 * SPEC
    ncol = lax.axis_size("col")
    vmem = pltpu.MemorySpace.VMEM
    return pl.pallas_call(
        fused_kernel,
        out_shape=(
            jax.ShapeDtypeStruct((ncol, nf, rows, width), jnp.bfloat16),
            jax.ShapeDtypeStruct((2, nf, rows, width), jnp.bfloat16),
        ),
        in_specs=[pl.BlockSpec(memory_space=pl.ANY)] * 4,
        out_specs=(pl.BlockSpec(memory_space=vmem), pl.BlockSpec(memory_space=vmem)),
        scratch_shapes=[
            pltpu.SMEM((inputs_here,), jnp.float32),
            pltpu.VMEM((TAPS, NFFT), jnp.float32),
            pltpu.VMEM((2, inputs_here, nsamp), jnp.int32),
            pltpu.VMEM((2, frames, inputs_here, NFFT), jnp.float32),
            pltpu.VMEM(table.shape, jnp.bfloat16),
            pltpu.VMEM((2 * NFFT // LANES, SPEC * inputs_here, LANES), jnp.float32),
            pltpu.VMEM((channels * inputs_here, width), jnp.float32),
            pltpu.VMEM((nf, rows, width), jnp.bfloat16),
            pltpu.SemaphoreType.DMA((7,)),
            pltpu.SemaphoreType.DMA((nf,)),
            pltpu.SemaphoreType.DMA((nf,)),
            pltpu.SemaphoreType.DMA,
            pltpu.SemaphoreType.DMA((6,)),
            pltpu.SemaphoreType.DMA,
            pltpu.SemaphoreType.DMA((2,)),
            pltpu.SemaphoreType.DMA((2,)),
            pltpu.SemaphoreType.DMA((2,)),
            pltpu.SemaphoreType.DMA,
        ],
        compiler_params=pltpu.CompilerParams(
            collective_id=0, has_side_effects=True, vmem_limit_bytes=63 * 1024 * 1024
        ),
    )(gains, taps, samples, table)


def local(samples, input_gains, filter_taps):
    nf = lax.axis_size("freq")
    channels = CH_DEV * nf
    inputs_here = samples.shape[1]
    table = dft_table_np(channels)
    row_blk, col_blk = fused_call(samples, input_gains, filter_taps, table)
    return visibilities(row_blk, col_blk)


def vis_kernel(row_ref, col_ref, vr_ref, vi_ref, a_scr, b_scr):
    kk = pl.program_id(0)
    groups = row_ref.shape[2] // CH_DEV

    @pl.when(kk == 0)
    def _():
        rows = row_ref[...].astype(jnp.float32)
        cols = col_ref[...].astype(jnp.float32)
        for j in range(CH_DEV):
            a = rows[:, :, j * groups : (j + 1) * groups, :]
            a_scr[j] = a.reshape(-1, a.shape[-1]).astype(a_scr.dtype)
            b = cols[:, :, j * groups : (j + 1) * groups, :]
            b = b.reshape(-1, b.shape[-1])
            b_scr[j, 0] = b.astype(b_scr.dtype)
            b_scr[j, 1] = jnp.concatenate([-b[:, SPEC:], b[:, :SPEC]], axis=1).astype(b_scr.dtype)

    a = a_scr[kk]
    dims = (((1,), (1,)), ((), ()))
    vr = lax.dot_general(a, b_scr[kk, 0], dims, preferred_element_type=jnp.float32)
    vr_ref[0] = (vr * (1.0 / SPEC)).astype(vr_ref.dtype)
    vi = lax.dot_general(a, b_scr[kk, 1], dims, preferred_element_type=jnp.float32)
    vi_ref[0] = (vi * (1.0 / SPEC)).astype(vi_ref.dtype)


def visibilities(row_blk, col_blk):
    nrow = row_blk.shape[0] * row_blk.shape[1] * row_blk.shape[2] // CH_DEV
    ncolumn = col_blk.shape[0] * col_blk.shape[1] * col_blk.shape[2] // CH_DEV
    width = row_blk.shape[3]
    out = jax.ShapeDtypeStruct((CH_DEV, nrow, ncolumn), jnp.bfloat16)
    return pl.pallas_call(
        vis_kernel,
        grid=(CH_DEV,),
        out_shape=(out, out),
        in_specs=[
            pl.BlockSpec(row_blk.shape, lambda k: (0, 0, 0, 0)),
            pl.BlockSpec(col_blk.shape, lambda k: (0, 0, 0, 0)),
        ],
        out_specs=(
            pl.BlockSpec((1, nrow, ncolumn), lambda k: (k, 0, 0)),
            pl.BlockSpec((1, nrow, ncolumn), lambda k: (k, 0, 0)),
        ),
        scratch_shapes=[
            pltpu.VMEM((CH_DEV, nrow, width), jnp.bfloat16),
            pltpu.VMEM((CH_DEV, 2, ncolumn, width), jnp.bfloat16),
        ],
        compiler_params=pltpu.CompilerParams(vmem_limit_bytes=63 * 1024 * 1024),
    )(row_blk, col_blk)


def solution(mesh):
    placed = (P(None, ("row", "col", "freq"), None), P(("row", "col", "freq")), P())
    return jax.shard_map(
        local,
        mesh=mesh,
        in_specs=placed,
        out_specs=(P("freq", "row", "col"), P("freq", "row", "col")),
        check_vma=False,
    )
```

```python
import math

import numpy as np

import jax
import jax.numpy as jnp
from jax import lax
from jax.experimental import pallas as pl
from jax.experimental.pallas import tpu as pltpu
from jax.sharding import PartitionSpec as P

NFFT = 1024
TAPS = 4
SPEC = 64
CH_DEV = 4


def dft_table_np(channels):
    position = np.arange(NFFT, dtype=np.int64)
    channel = np.arange(channels, dtype=np.int64)
    phases = (position[:, None] * channel[None, :] % NFFT).astype(np.float64) * (2.0 * math.pi / NFFT)
    scaling = 0.5 / math.sqrt(NFFT)
    cosine = np.cos(phases) * scaling
    sine = np.sin(phases) * scaling
    real_rows = np.stack([cosine, -sine], axis=1)
    imag_rows = np.stack([sine, cosine], axis=1)
    table = np.stack([real_rows, imag_rows], axis=0)
    table = table.transpose(2, 3, 0, 1).reshape(2 * channels, 2 * NFFT)
    return jnp.asarray(table, dtype=jnp.bfloat16)


LANES = 128


def pfb_dft_body(g_hbm, taps_hbm, s_hbm, tab_hbm, o_ref, g_ref, taps_ref, sbuf, vbuf, tab_buf, f_ref, sems, after_start):
    inputs_here, nsamp = s_hbm.shape[1], s_hbm.shape[2]
    frames = nsamp // NFFT
    first = SPEC // 2 + TAPS - 1
    split = first * NFFT
    blocks = NFFT // LANES
    channels = tab_hbm.shape[0] // 2
    parts = []
    for p in range(2):
        head = pltpu.make_async_copy(
            s_hbm.at[p, :, pl.ds(0, split)], sbuf.at[p, :, pl.ds(0, split)], sems.at[2 * p]
        )
        tail = pltpu.make_async_copy(
            s_hbm.at[p, :, pl.ds(split, nsamp - split)],
            sbuf.at[p, :, pl.ds(split, nsamp - split)],
            sems.at[2 * p + 1],
        )
        head.start()
        tail.start()
        parts.append((head, tail))
    tab_cp = pltpu.make_async_copy(tab_hbm, tab_buf, sems.at[4])
    tab_cp.start()
    g_cp = pltpu.make_async_copy(g_hbm, g_ref, sems.at[5])
    g_cp.start()
    taps_cp = pltpu.make_async_copy(taps_hbm, taps_ref, sems.at[6])
    taps_cp.start()
    after_start()
    g_cp.wait()
    taps_cp.wait()

    row = lax.broadcasted_iota(jnp.int32, (inputs_here, NFFT), 0)
    scale = jnp.zeros((inputs_here, NFFT), jnp.float32)
    for i in range(inputs_here):
        scale = jnp.where(row == i, g_ref[i] * 0.25, scale)

    def volts(p, lo, hi):
        def body(j, carry):
            start = pl.multiple_of(j * NFFT, NFFT)
            vbuf[p, j] = sbuf[p, :, pl.ds(start, NFFT)].astype(jnp.float32) * scale
            return carry

        lax.fori_loop(lo, hi, body, 0)

    def filt(p, lo, hi):
        def body(m, carry):
            total = vbuf[p, m] * taps_ref[0:1, :]
            for t in range(1, TAPS):
                total = total + vbuf[p, m + t] * taps_ref[t : t + 1, :]
            rows = pl.ds(pl.multiple_of(m * inputs_here, inputs_here), inputs_here)
            for b in range(blocks):
                f_ref[p * blocks + b, rows, :] = total[:, b * LANES : (b + 1) * LANES]
            return carry

        lax.fori_loop(lo, hi, body, 0)

    for p in range(2):
        head, tail = parts[p]
        head.wait()
        volts(p, 0, first)
        filt(p, 0, SPEC // 2)
        tail.wait()
        volts(p, first, frames)
        filt(p, SPEC // 2, SPEC)

    tab_cp.wait()
    for i in range(inputs_here):
        lhs = jnp.concatenate(
            [f_ref[b, pl.ds(i, SPEC, stride=inputs_here), :] for b in range(2 * blocks)], axis=1
        ).astype(jnp.bfloat16)
        prod = lax.dot_general(
            tab_buf[...], lhs, (((1,), (1,)), ((), ())), preferred_element_type=jnp.float32
        )
        val = jnp.concatenate([prod[:channels], prod[channels:]], axis=1)
        o_ref[pl.ds(i, channels, stride=inputs_here), :] = val


MESH = pl.DeviceIdType.MESH


def fused_kernel(
    g_hbm, taps_hbm, s_hbm, tab_hbm, row_ref, col_ref,
    g_ref, taps_ref, sbuf, vbuf, tab_buf, f_ref, o_scr, spec_ref, relay_buf, pfb_sems,
    send1, recv1, own_sem, sends, recva, recvb, recvc, recvd, recve, recvf, local_sem,
):
    nf = spec_ref.shape[0]
    f = lax.axis_index("freq")
    r = lax.axis_index("row")
    c = lax.axis_index("col")
    k = c % 2
    h = c // 2
    sib = c + 1 - 2 * k
    cross_c = 2 * r + h
    crossing = h != r
    relay_target = jnp.logical_or(c == 1, c == 2)
    fan_target = jnp.logical_not(relay_target)
    relay_dest = 2 - k
    relay_src = 2 * r + 2 - c
    side_source = k == 1
    side_relay = jnp.logical_not(crossing)
    side_target = fan_target
    side_dest = 2 * (1 - r) + h
    side_from = 2 * k + 1
    side_to = 3 - 3 * k
    side_target_src = 2 * (1 - r) + 1 - h
    base = 2 * (1 - h)

    def greet_all():
        barrier = pltpu.get_barrier_semaphore()

        def greet_freq(d, carry):
            pl.semaphore_signal(barrier, inc=1, device_id=((f + d) % nf, r, c), device_id_type=MESH)
            return carry

        lax.fori_loop(1, nf, greet_freq, 0)
        pl.semaphore_signal(barrier, inc=1, device_id=(f, r, sib), device_id_type=MESH)
        pl.semaphore_signal(barrier, inc=1, device_id=(f, 1 - r, cross_c), device_id_type=MESH)

        @pl.when(crossing)
        def _():
            for e in range(2):
                pl.semaphore_signal(barrier, inc=1, device_id=(f, 1 - r, 2 * k + e), device_id_type=MESH)
            pl.semaphore_signal(barrier, inc=1, device_id=(f, 1 - r, relay_dest), device_id_type=MESH)

        @pl.when(relay_target)
        def _():
            pl.semaphore_signal(barrier, inc=1, device_id=(f, 1 - r, relay_src), device_id_type=MESH)

        @pl.when(side_source)
        def _():
            pl.semaphore_signal(barrier, inc=1, device_id=(f, 1 - r, side_dest), device_id_type=MESH)

        @pl.when(side_relay)
        def _():
            pl.semaphore_signal(barrier, inc=1, device_id=(f, 1 - r, side_from), device_id_type=MESH)
            pl.semaphore_signal(barrier, inc=1, device_id=(f, 1 - r, side_to), device_id_type=MESH)

        @pl.when(side_target)
        def _():
            pl.semaphore_signal(barrier, inc=1, device_id=(f, 1 - r, side_target_src), device_id_type=MESH)


    barrier = pltpu.get_barrier_semaphore()
    pfb_dft_body(
        g_hbm, taps_hbm, s_hbm, tab_hbm, o_scr, g_ref, taps_ref, sbuf, vbuf, tab_buf, f_ref,
        pfb_sems, greet_all,
    )
    spec_ref[...] = o_scr[...].astype(spec_ref.dtype).reshape(spec_ref.shape)

    expected = (
        (nf - 1) + 2 + 3 * crossing.astype(jnp.int32) + relay_target.astype(jnp.int32)
        + side_source.astype(jnp.int32) + 2 * side_relay.astype(jnp.int32)
        + side_target.astype(jnp.int32)
    )
    pl.semaphore_wait(barrier, expected)

    own = pltpu.make_async_copy(spec_ref.at[f], row_ref.at[c, f], own_sem)
    own.start()

    def freq_copy(d):
        dest = (f + d) % nf
        return pltpu.make_async_remote_copy(
            src_ref=spec_ref.at[dest],
            dst_ref=row_ref.at[c, f],
            send_sem=send1.at[d],
            recv_sem=recv1.at[f],
            device_id=(dest, r, c),
            device_id_type=MESH,
        )

    def send_freq(d, carry):
        freq_copy(d).start()
        return carry

    lax.fori_loop(1, nf, send_freq, 0)

    def recv_freq(d, carry):
        src = (f + nf - d) % nf
        pltpu.make_async_remote_copy(
            src_ref=spec_ref.at[src],
            dst_ref=row_ref.at[c, src],
            send_sem=send1.at[d],
            recv_sem=recv1.at[src],
            device_id=(src, r, c),
            device_id_type=MESH,
        ).wait_recv()
        return carry

    lax.fori_loop(1, nf, recv_freq, 0)
    own.wait()

    to_sib = pltpu.make_async_remote_copy(
        src_ref=row_ref.at[c],
        dst_ref=row_ref.at[c],
        send_sem=sends.at[0],
        recv_sem=recva,
        device_id=(f, r, sib),
        device_id_type=MESH,
    )
    to_sib.start()
    to_cross = pltpu.make_async_remote_copy(
        src_ref=row_ref.at[c],
        dst_ref=col_ref.at[k],
        send_sem=sends.at[1],
        recv_sem=recvb.at[k],
        device_id=(f, 1 - r, cross_c),
        device_id_type=MESH,
    )
    to_cross.start()

    def side_copy():
        return pltpu.make_async_remote_copy(
            src_ref=row_ref.at[c],
            dst_ref=relay_buf,
            send_sem=sends.at[2],
            recv_sem=recve,
            device_id=(f, 1 - r, side_dest),
            device_id_type=MESH,
        )

    def relay_copy():
        return pltpu.make_async_remote_copy(
            src_ref=col_ref.at[0],
            dst_ref=row_ref.at[2 * k],
            send_sem=sends.at[3],
            recv_sem=recvc,
            device_id=(f, 1 - r, relay_dest),
            device_id_type=MESH,
        )

    def side_relay_copy():
        return pltpu.make_async_remote_copy(
            src_ref=relay_buf,
            dst_ref=row_ref.at[2 * k + 1],
            send_sem=sends.at[4],
            recv_sem=recvf,
            device_id=(f, 1 - r, side_to),
            device_id_type=MESH,
        )

    def fan_copy(slot):
        return pltpu.make_async_remote_copy(
            src_ref=row_ref.at[slot],
            dst_ref=row_ref.at[slot],
            send_sem=sends.at[5],
            recv_sem=recvd,
            device_id=(f, r, sib),
            device_id_type=MESH,
        )

    mine = jnp.where(relay_target, 0, 1)

    @pl.when(side_source)
    def _():
        side_copy().start()

    @pl.when(crossing)
    def _():
        pltpu.make_async_remote_copy(
            src_ref=row_ref.at[0],
            dst_ref=col_ref.at[0],
            send_sem=sends.at[1],
            recv_sem=recvb.at[0],
            device_id=(f, 1 - r, 2 * k),
            device_id_type=MESH,
        ).wait_recv()
        relay_copy().start()

    @pl.when(side_relay)
    def _():
        pltpu.make_async_remote_copy(
            src_ref=row_ref.at[c],
            dst_ref=relay_buf,
            send_sem=sends.at[2],
            recv_sem=recve,
            device_id=(f, 1 - r, side_from),
            device_id_type=MESH,
        ).wait_recv()
        side_relay_copy().start()

    @pl.when(relay_target)
    def _():
        pltpu.make_async_remote_copy(
            src_ref=col_ref.at[0],
            dst_ref=row_ref.at[base],
            send_sem=sends.at[3],
            recv_sem=recvc,
            device_id=(f, 1 - r, relay_src),
            device_id_type=MESH,
        ).wait_recv()

    @pl.when(side_target)
    def _():
        pltpu.make_async_remote_copy(
            src_ref=relay_buf,
            dst_ref=row_ref.at[base + 1],
            send_sem=sends.at[4],
            recv_sem=recvf,
            device_id=(f, 1 - r, side_target_src),
            device_id_type=MESH,
        ).wait_recv()

    fan_copy(base + mine).start()
    fan_copy(base + 1 - mine).wait_recv()

    pltpu.make_async_remote_copy(
        src_ref=row_ref.at[sib],
        dst_ref=row_ref.at[sib],
        send_sem=sends.at[0],
        recv_sem=recva,
        device_id=(f, r, sib),
        device_id_type=MESH,
    ).wait_recv()

    @pl.when(crossing)
    def _():
        pltpu.make_async_remote_copy(
            src_ref=row_ref.at[1],
            dst_ref=col_ref.at[1],
            send_sem=sends.at[1],
            recv_sem=recvb.at[1],
            device_id=(f, 1 - r, 2 * k + 1),
            device_id_type=MESH,
        ).wait_recv()

    @pl.when(jnp.logical_not(crossing))
    def _():
        half = pltpu.make_async_copy(row_ref.at[pl.ds(2 * k, 2)], col_ref, local_sem)
        half.start()
        half.wait()

    def wait_send_freq(d, carry):
        freq_copy(d).wait_send()
        return carry

    lax.fori_loop(1, nf, wait_send_freq, 0)
    to_sib.wait_send()
    to_cross.wait_send()
    fan_copy(base + mine).wait_send()

    @pl.when(side_source)
    def _():
        side_copy().wait_send()

    @pl.when(crossing)
    def _():
        relay_copy().wait_send()

    @pl.when(side_relay)
    def _():
        side_relay_copy().wait_send()


def fused_call(samples, gains, taps, table):
    inputs_here, nsamp = samples.shape[1], samples.shape[2]
    channels = table.shape[0] // 2
    frames = nsamp // NFFT
    nf = channels // CH_DEV
    rows = CH_DEV * inputs_here
    width = 2 * SPEC
    ncol = lax.axis_size("col")
    vmem = pltpu.MemorySpace.VMEM
    return pl.pallas_call(
        fused_kernel,
        out_shape=(
            jax.ShapeDtypeStruct((ncol, nf, rows, width), jnp.bfloat16),
            jax.ShapeDtypeStruct((2, nf, rows, width), jnp.bfloat16),
        ),
        in_specs=[pl.BlockSpec(memory_space=pl.ANY)] * 4,
        out_specs=(pl.BlockSpec(memory_space=vmem), pl.BlockSpec(memory_space=vmem)),
        scratch_shapes=[
            pltpu.SMEM((inputs_here,), jnp.float32),
            pltpu.VMEM((TAPS, NFFT), jnp.float32),
            pltpu.VMEM((2, inputs_here, nsamp), jnp.int32),
            pltpu.VMEM((2, frames, inputs_here, NFFT), jnp.float32),
            pltpu.VMEM(table.shape, jnp.bfloat16),
            pltpu.VMEM((2 * NFFT // LANES, SPEC * inputs_here, LANES), jnp.float32),
            pltpu.VMEM((channels * inputs_here, width), jnp.float32),
            pltpu.VMEM((nf, rows, width), jnp.bfloat16),
            pltpu.VMEM((nf, rows, width), jnp.bfloat16),
            pltpu.SemaphoreType.DMA((7,)),
            pltpu.SemaphoreType.DMA((nf,)),
            pltpu.SemaphoreType.DMA((nf,)),
            pltpu.SemaphoreType.DMA,
            pltpu.SemaphoreType.DMA((6,)),
            pltpu.SemaphoreType.DMA,
            pltpu.SemaphoreType.DMA((2,)),
            pltpu.SemaphoreType.DMA,
            pltpu.SemaphoreType.DMA,
            pltpu.SemaphoreType.DMA,
            pltpu.SemaphoreType.DMA,
            pltpu.SemaphoreType.DMA,
        ],
        compiler_params=pltpu.CompilerParams(
            collective_id=0, has_side_effects=True, vmem_limit_bytes=63 * 1024 * 1024
        ),
    )(gains, taps, samples, table)


def local(samples, input_gains, filter_taps):
    nf = lax.axis_size("freq")
    channels = CH_DEV * nf
    inputs_here = samples.shape[1]
    table = dft_table_np(channels)
    row_blk, col_blk = fused_call(samples, input_gains, filter_taps, table)
    return visibilities(row_blk, col_blk)


def vis_kernel(row_ref, col_ref, vr_ref, vi_ref, a_scr, b_scr):
    kk = pl.program_id(0)
    groups = row_ref.shape[2] // CH_DEV

    @pl.when(kk == 0)
    def _():
        rows = row_ref[...].astype(jnp.float32)
        cols = col_ref[...].astype(jnp.float32)
        for j in range(CH_DEV):
            a = rows[:, :, j * groups : (j + 1) * groups, :]
            a_scr[j] = a.reshape(-1, a.shape[-1]).astype(a_scr.dtype)
            b = cols[:, :, j * groups : (j + 1) * groups, :]
            b = b.reshape(-1, b.shape[-1])
            b_scr[j, 0] = b.astype(b_scr.dtype)
            b_scr[j, 1] = jnp.concatenate([-b[:, SPEC:], b[:, :SPEC]], axis=1).astype(b_scr.dtype)

    a = a_scr[kk]
    dims = (((1,), (1,)), ((), ()))
    vr = lax.dot_general(a, b_scr[kk, 0], dims, preferred_element_type=jnp.float32)
    vr_ref[0] = (vr * (1.0 / SPEC)).astype(vr_ref.dtype)
    vi = lax.dot_general(a, b_scr[kk, 1], dims, preferred_element_type=jnp.float32)
    vi_ref[0] = (vi * (1.0 / SPEC)).astype(vi_ref.dtype)


def visibilities(row_blk, col_blk):
    nrow = row_blk.shape[0] * row_blk.shape[1] * row_blk.shape[2] // CH_DEV
    ncolumn = col_blk.shape[0] * col_blk.shape[1] * col_blk.shape[2] // CH_DEV
    width = row_blk.shape[3]
    out = jax.ShapeDtypeStruct((CH_DEV, nrow, ncolumn), jnp.bfloat16)
    return pl.pallas_call(
        vis_kernel,
        grid=(CH_DEV,),
        out_shape=(out, out),
        in_specs=[
            pl.BlockSpec(row_blk.shape, lambda k: (0, 0, 0, 0)),
            pl.BlockSpec(col_blk.shape, lambda k: (0, 0, 0, 0)),
        ],
        out_specs=(
            pl.BlockSpec((1, nrow, ncolumn), lambda k: (k, 0, 0)),
            pl.BlockSpec((1, nrow, ncolumn), lambda k: (k, 0, 0)),
        ),
        scratch_shapes=[
            pltpu.VMEM((CH_DEV, nrow, width), jnp.bfloat16),
            pltpu.VMEM((CH_DEV, 2, ncolumn, width), jnp.bfloat16),
        ],
        compiler_params=pltpu.CompilerParams(vmem_limit_bytes=63 * 1024 * 1024),
    )(row_blk, col_blk)


def solution(mesh):
    placed = (P(None, ("row", "col", "freq"), None), P(("row", "col", "freq")), P())
    return jax.shard_map(
        local,
        mesh=mesh,
        in_specs=placed,
        out_specs=(P("freq", "row", "col"), P("freq", "row", "col")),
        check_vma=False,
    )
```

```python
import math

import numpy as np

import jax
import jax.numpy as jnp
from jax import lax
from jax.experimental import pallas as pl
from jax.experimental.pallas import tpu as pltpu
from jax.sharding import PartitionSpec as P

NFFT = 1024
TAPS = 4
SPEC = 64
CH_DEV = 4


def dft_table_np(channels):
    position = np.arange(NFFT, dtype=np.int64)
    channel = np.arange(channels, dtype=np.int64)
    phases = (position[:, None] * channel[None, :] % NFFT).astype(np.float64) * (2.0 * math.pi / NFFT)
    scaling = 0.5 / math.sqrt(NFFT)
    cosine = np.cos(phases) * scaling
    sine = np.sin(phases) * scaling
    real_rows = np.stack([cosine, -sine], axis=1)
    imag_rows = np.stack([sine, cosine], axis=1)
    table = np.stack([real_rows, imag_rows], axis=0)
    table = table.transpose(2, 3, 0, 1).reshape(2 * channels, 2 * NFFT)
    return jnp.asarray(table, dtype=jnp.bfloat16)


LANES = 128


def pfb_dft_body(g_hbm, taps_hbm, s_hbm, tab_hbm, o_ref, g_ref, taps_ref, sbuf, vbuf, tab_buf, f_ref, sems, after_start):
    inputs_here, nsamp = s_hbm.shape[1], s_hbm.shape[2]
    frames = nsamp // NFFT
    first = SPEC // 2 + TAPS - 1
    split = first * NFFT
    blocks = NFFT // LANES
    channels = tab_hbm.shape[0] // 2
    parts = []
    for p in range(2):
        head = pltpu.make_async_copy(
            s_hbm.at[p, :, pl.ds(0, split)], sbuf.at[p, :, pl.ds(0, split)], sems.at[2 * p]
        )
        tail = pltpu.make_async_copy(
            s_hbm.at[p, :, pl.ds(split, nsamp - split)],
            sbuf.at[p, :, pl.ds(split, nsamp - split)],
            sems.at[2 * p + 1],
        )
        head.start()
        tail.start()
        parts.append((head, tail))
    tab_cp = pltpu.make_async_copy(tab_hbm, tab_buf, sems.at[4])
    tab_cp.start()
    g_cp = pltpu.make_async_copy(g_hbm, g_ref, sems.at[5])
    g_cp.start()
    taps_cp = pltpu.make_async_copy(taps_hbm, taps_ref, sems.at[6])
    taps_cp.start()
    after_start()
    g_cp.wait()
    taps_cp.wait()

    row = lax.broadcasted_iota(jnp.int32, (inputs_here, NFFT), 0)
    scale = jnp.zeros((inputs_here, NFFT), jnp.float32)
    for i in range(inputs_here):
        scale = jnp.where(row == i, g_ref[i] * 0.25, scale)

    def volts(p, lo, hi):
        def body(j, carry):
            start = pl.multiple_of(j * NFFT, NFFT)
            vbuf[p, j] = sbuf[p, :, pl.ds(start, NFFT)].astype(jnp.float32) * scale
            return carry

        lax.fori_loop(lo, hi, body, 0)

    def filt(p, lo, hi):
        def body(m, carry):
            total = vbuf[p, m] * taps_ref[0:1, :]
            for t in range(1, TAPS):
                total = total + vbuf[p, m + t] * taps_ref[t : t + 1, :]
            rows = pl.ds(pl.multiple_of(m * inputs_here, inputs_here), inputs_here)
            for b in range(blocks):
                f_ref[p * blocks + b, rows, :] = total[:, b * LANES : (b + 1) * LANES]
            return carry

        lax.fori_loop(lo, hi, body, 0)

    for p in range(2):
        head, tail = parts[p]
        head.wait()
        volts(p, 0, first)
        filt(p, 0, SPEC // 2)
        tail.wait()
        volts(p, first, frames)
        filt(p, SPEC // 2, SPEC)

    tab_cp.wait()
    for i in range(inputs_here):
        lhs = jnp.concatenate(
            [f_ref[b, pl.ds(i, SPEC, stride=inputs_here), :] for b in range(2 * blocks)], axis=1
        ).astype(jnp.bfloat16)
        prod = lax.dot_general(
            tab_buf[...], lhs, (((1,), (1,)), ((), ())), preferred_element_type=jnp.float32
        )
        val = jnp.concatenate([prod[:channels], prod[channels:]], axis=1)
        o_ref[pl.ds(i, channels, stride=inputs_here), :] = val


MESH = pl.DeviceIdType.MESH


def fused_kernel(
    g_hbm, taps_hbm, s_hbm, tab_hbm, row_ref, col_ref,
    g_ref, taps_ref, sbuf, vbuf, tab_buf, f_ref, o_scr, spec_ref, relay_buf, pfb_sems,
    send1, recv1, own_sem, sends, recva, recvb, recvc, recvd, recve, recvf, local_sem,
):
    nf = spec_ref.shape[0]
    f = lax.axis_index("freq")
    r = lax.axis_index("row")
    c = lax.axis_index("col")
    k = c % 2
    h = c // 2
    sib = c + 1 - 2 * k
    cross_c = 2 * r + h
    crossing = h != r
    relay_target = jnp.logical_or(c == 1, c == 2)
    fan_target = jnp.logical_not(relay_target)
    relay_dest = 2 - k
    relay_src = 2 * r + 2 - c
    side_source = k == 1
    side_relay = jnp.logical_not(crossing)
    side_target = fan_target
    side_dest = 2 * (1 - r) + h
    side_from = 2 * k + 1
    side_to = 3 - 3 * k
    side_target_src = 2 * (1 - r) + 1 - h
    base = 2 * (1 - h)

    def greet_all():
        barrier = pltpu.get_barrier_semaphore()

        def greet_freq(d, carry):
            pl.semaphore_signal(barrier, inc=1, device_id=((f + d) % nf, r, c), device_id_type=MESH)
            return carry

        lax.fori_loop(1, nf, greet_freq, 0)
        pl.semaphore_signal(barrier, inc=1, device_id=(f, r, sib), device_id_type=MESH)
        pl.semaphore_signal(barrier, inc=1, device_id=(f, 1 - r, cross_c), device_id_type=MESH)

        @pl.when(crossing)
        def _():
            for e in range(2):
                pl.semaphore_signal(barrier, inc=1, device_id=(f, 1 - r, 2 * k + e), device_id_type=MESH)
            pl.semaphore_signal(barrier, inc=1, device_id=(f, 1 - r, relay_dest), device_id_type=MESH)

        @pl.when(relay_target)
        def _():
            pl.semaphore_signal(barrier, inc=1, device_id=(f, 1 - r, relay_src), device_id_type=MESH)

        @pl.when(side_source)
        def _():
            pl.semaphore_signal(barrier, inc=1, device_id=(f, 1 - r, side_dest), device_id_type=MESH)

        @pl.when(side_relay)
        def _():
            pl.semaphore_signal(barrier, inc=1, device_id=(f, 1 - r, side_from), device_id_type=MESH)
            pl.semaphore_signal(barrier, inc=1, device_id=(f, 1 - r, side_to), device_id_type=MESH)

        @pl.when(side_target)
        def _():
            pl.semaphore_signal(barrier, inc=1, device_id=(f, 1 - r, side_target_src), device_id_type=MESH)


    barrier = pltpu.get_barrier_semaphore()
    pfb_dft_body(
        g_hbm, taps_hbm, s_hbm, tab_hbm, o_scr, g_ref, taps_ref, sbuf, vbuf, tab_buf, f_ref,
        pfb_sems, greet_all,
    )
    spec_ref[...] = o_scr[...].astype(spec_ref.dtype).reshape(spec_ref.shape)

    expected = (
        (nf - 1) + 2 + 3 * crossing.astype(jnp.int32) + relay_target.astype(jnp.int32)
        + side_source.astype(jnp.int32) + 2 * side_relay.astype(jnp.int32)
        + side_target.astype(jnp.int32)
    )
    pl.semaphore_wait(barrier, expected)

    own = pltpu.make_async_copy(spec_ref.at[f], row_ref.at[c, f], own_sem)
    own.start()

    def freq_copy(d):
        dest = (f + d) % nf
        return pltpu.make_async_remote_copy(
            src_ref=spec_ref.at[dest],
            dst_ref=row_ref.at[c, f],
            send_sem=send1.at[d],
            recv_sem=recv1.at[f],
            device_id=(dest, r, c),
            device_id_type=MESH,
        )

    def send_freq(d, carry):
        freq_copy(d).start()
        return carry

    lax.fori_loop(1, nf, send_freq, 0)

    def recv_freq(d, carry):
        src = (f + nf - d) % nf
        pltpu.make_async_remote_copy(
            src_ref=spec_ref.at[src],
            dst_ref=row_ref.at[c, src],
            send_sem=send1.at[d],
            recv_sem=recv1.at[src],
            device_id=(src, r, c),
            device_id_type=MESH,
        ).wait_recv()
        return carry

    lax.fori_loop(1, nf, recv_freq, 0)
    own.wait()

    to_sib = pltpu.make_async_remote_copy(
        src_ref=row_ref.at[c],
        dst_ref=row_ref.at[c],
        send_sem=sends.at[0],
        recv_sem=recva,
        device_id=(f, r, sib),
        device_id_type=MESH,
    )
    to_sib.start()
    to_cross = pltpu.make_async_remote_copy(
        src_ref=row_ref.at[c],
        dst_ref=col_ref.at[k],
        send_sem=sends.at[1],
        recv_sem=recvb.at[k],
        device_id=(f, 1 - r, cross_c),
        device_id_type=MESH,
    )
    to_cross.start()

    def side_copy():
        return pltpu.make_async_remote_copy(
            src_ref=row_ref.at[c],
            dst_ref=relay_buf,
            send_sem=sends.at[2],
            recv_sem=recve,
            device_id=(f, 1 - r, side_dest),
            device_id_type=MESH,
        )

    def relay_copy():
        return pltpu.make_async_remote_copy(
            src_ref=col_ref.at[0],
            dst_ref=row_ref.at[2 * k],
            send_sem=sends.at[3],
            recv_sem=recvc,
            device_id=(f, 1 - r, relay_dest),
            device_id_type=MESH,
        )

    def side_relay_copy():
        return pltpu.make_async_remote_copy(
            src_ref=relay_buf,
            dst_ref=row_ref.at[2 * k + 1],
            send_sem=sends.at[4],
            recv_sem=recvf,
            device_id=(f, 1 - r, side_to),
            device_id_type=MESH,
        )

    def fan_copy(slot):
        return pltpu.make_async_remote_copy(
            src_ref=row_ref.at[slot],
            dst_ref=row_ref.at[slot],
            send_sem=sends.at[5],
            recv_sem=recvd,
            device_id=(f, r, sib),
            device_id_type=MESH,
        )

    mine = jnp.where(relay_target, 0, 1)

    @pl.when(side_source)
    def _():
        side_copy().start()

    @pl.when(crossing)
    def _():
        pltpu.make_async_remote_copy(
            src_ref=row_ref.at[0],
            dst_ref=col_ref.at[0],
            send_sem=sends.at[1],
            recv_sem=recvb.at[0],
            device_id=(f, 1 - r, 2 * k),
            device_id_type=MESH,
        ).wait_recv()
        relay_copy().start()

    @pl.when(side_relay)
    def _():
        pltpu.make_async_remote_copy(
            src_ref=row_ref.at[c],
            dst_ref=relay_buf,
            send_sem=sends.at[2],
            recv_sem=recve,
            device_id=(f, 1 - r, side_from),
            device_id_type=MESH,
        ).wait_recv()
        side_relay_copy().start()

    @pl.when(relay_target)
    def _():
        pltpu.make_async_remote_copy(
            src_ref=col_ref.at[0],
            dst_ref=row_ref.at[base],
            send_sem=sends.at[3],
            recv_sem=recvc,
            device_id=(f, 1 - r, relay_src),
            device_id_type=MESH,
        ).wait_recv()

    @pl.when(side_target)
    def _():
        pltpu.make_async_remote_copy(
            src_ref=relay_buf,
            dst_ref=row_ref.at[base + 1],
            send_sem=sends.at[4],
            recv_sem=recvf,
            device_id=(f, 1 - r, side_target_src),
            device_id_type=MESH,
        ).wait_recv()

    fan_copy(base + mine).start()
    fan_copy(base + 1 - mine).wait_recv()

    pltpu.make_async_remote_copy(
        src_ref=row_ref.at[sib],
        dst_ref=row_ref.at[sib],
        send_sem=sends.at[0],
        recv_sem=recva,
        device_id=(f, r, sib),
        device_id_type=MESH,
    ).wait_recv()

    @pl.when(crossing)
    def _():
        pltpu.make_async_remote_copy(
            src_ref=row_ref.at[1],
            dst_ref=col_ref.at[1],
            send_sem=sends.at[1],
            recv_sem=recvb.at[1],
            device_id=(f, 1 - r, 2 * k + 1),
            device_id_type=MESH,
        ).wait_recv()

    @pl.when(jnp.logical_not(crossing))
    def _():
        half = pltpu.make_async_copy(row_ref.at[pl.ds(2 * k, 2)], col_ref, local_sem)
        half.start()
        half.wait()

    def wait_send_freq(d, carry):
        freq_copy(d).wait_send()
        return carry

    lax.fori_loop(1, nf, wait_send_freq, 0)
    to_sib.wait_send()
    to_cross.wait_send()
    fan_copy(base + mine).wait_send()

    @pl.when(side_source)
    def _():
        side_copy().wait_send()

    @pl.when(crossing)
    def _():
        relay_copy().wait_send()

    @pl.when(side_relay)
    def _():
        side_relay_copy().wait_send()


def fused_call(samples, gains, taps, table):
    inputs_here, nsamp = samples.shape[1], samples.shape[2]
    channels = table.shape[0] // 2
    frames = nsamp // NFFT
    nf = channels // CH_DEV
    rows = CH_DEV * inputs_here
    width = 2 * SPEC
    ncol = lax.axis_size("col")
    vmem = pltpu.MemorySpace.VMEM
    return pl.pallas_call(
        fused_kernel,
        out_shape=(
            jax.ShapeDtypeStruct((ncol, nf, rows, width), jnp.bfloat16),
            jax.ShapeDtypeStruct((2, nf, rows, width), jnp.bfloat16),
        ),
        in_specs=[pl.BlockSpec(memory_space=pl.ANY)] * 4,
        out_specs=(pl.BlockSpec(memory_space=vmem), pl.BlockSpec(memory_space=vmem)),
        scratch_shapes=[
            pltpu.SMEM((inputs_here,), jnp.float32),
            pltpu.VMEM((TAPS, NFFT), jnp.float32),
            pltpu.VMEM((2, inputs_here, nsamp), jnp.int32),
            pltpu.VMEM((2, frames, inputs_here, NFFT), jnp.float32),
            pltpu.VMEM(table.shape, jnp.bfloat16),
            pltpu.VMEM((2 * NFFT // LANES, SPEC * inputs_here, LANES), jnp.float32),
            pltpu.VMEM((channels * inputs_here, width), jnp.float32),
            pltpu.VMEM((nf, rows, width), jnp.bfloat16),
            pltpu.VMEM((nf, rows, width), jnp.bfloat16),
            pltpu.SemaphoreType.DMA((7,)),
            pltpu.SemaphoreType.DMA((nf,)),
            pltpu.SemaphoreType.DMA((nf,)),
            pltpu.SemaphoreType.DMA,
            pltpu.SemaphoreType.DMA((6,)),
            pltpu.SemaphoreType.DMA,
            pltpu.SemaphoreType.DMA((2,)),
            pltpu.SemaphoreType.DMA,
            pltpu.SemaphoreType.DMA,
            pltpu.SemaphoreType.DMA,
            pltpu.SemaphoreType.DMA,
            pltpu.SemaphoreType.DMA,
        ],
        compiler_params=pltpu.CompilerParams(
            collective_id=0, has_side_effects=True, vmem_limit_bytes=63 * 1024 * 1024
        ),
    )(gains, taps, samples, table)


def local(samples, input_gains, filter_taps):
    nf = lax.axis_size("freq")
    channels = CH_DEV * nf
    inputs_here = samples.shape[1]
    table = dft_table_np(channels)
    row_blk, col_blk = fused_call(samples, input_gains, filter_taps, table)
    return visibilities(row_blk, col_blk)


def vis_kernel(row_ref, col_ref, vr_ref, vi_ref, a_scr, b_scr):
    kk = pl.program_id(0)
    groups = row_ref.shape[2] // CH_DEV
    pair = pl.multiple_of((kk // 2) * 2 * groups, 2 * groups)
    rows = row_ref[:, :, pl.ds(pair, 2 * groups), :].astype(jnp.float32)
    cols = col_ref[:, :, pl.ds(pair, 2 * groups), :].astype(jnp.float32)
    for j in range(2):

        @pl.when(kk % 2 == j)
        def _():
            a = rows[:, :, j * groups : (j + 1) * groups, :]
            a_scr[...] = a.reshape(-1, a.shape[-1]).astype(a_scr.dtype)
            b = cols[:, :, j * groups : (j + 1) * groups, :]
            b = b.reshape(-1, b.shape[-1])
            b_scr[0] = b.astype(b_scr.dtype)
            b_scr[1] = jnp.concatenate([-b[:, SPEC:], b[:, :SPEC]], axis=1).astype(b_scr.dtype)

    a = a_scr[...]
    dims = (((1,), (1,)), ((), ()))
    vr = lax.dot_general(a, b_scr[0], dims, preferred_element_type=jnp.float32)
    vr_ref[0] = (vr * (1.0 / SPEC)).astype(vr_ref.dtype)
    vi = lax.dot_general(a, b_scr[1], dims, preferred_element_type=jnp.float32)
    vi_ref[0] = (vi * (1.0 / SPEC)).astype(vi_ref.dtype)


def visibilities(row_blk, col_blk):
    nrow = row_blk.shape[0] * row_blk.shape[1] * row_blk.shape[2] // CH_DEV
    ncolumn = col_blk.shape[0] * col_blk.shape[1] * col_blk.shape[2] // CH_DEV
    width = row_blk.shape[3]
    out = jax.ShapeDtypeStruct((CH_DEV, nrow, ncolumn), jnp.bfloat16)
    return pl.pallas_call(
        vis_kernel,
        grid=(CH_DEV,),
        out_shape=(out, out),
        in_specs=[
            pl.BlockSpec(row_blk.shape, lambda k: (0, 0, 0, 0)),
            pl.BlockSpec(col_blk.shape, lambda k: (0, 0, 0, 0)),
        ],
        out_specs=(
            pl.BlockSpec((1, nrow, ncolumn), lambda k: (k, 0, 0)),
            pl.BlockSpec((1, nrow, ncolumn), lambda k: (k, 0, 0)),
        ),
        scratch_shapes=[
            pltpu.VMEM((nrow, width), jnp.bfloat16),
            pltpu.VMEM((2, ncolumn, width), jnp.bfloat16),
        ],
        compiler_params=pltpu.CompilerParams(vmem_limit_bytes=63 * 1024 * 1024),
    )(row_blk, col_blk)


def solution(mesh):
    placed = (P(None, ("row", "col", "freq"), None), P(("row", "col", "freq")), P())
    return jax.shard_map(
        local,
        mesh=mesh,
        in_specs=placed,
        out_specs=(P("freq", "row", "col"), P("freq", "row", "col")),
        check_vma=False,
    )
```

```python
import math

import numpy as np

import jax
import jax.numpy as jnp
from jax import lax
from jax.experimental import pallas as pl
from jax.experimental.pallas import tpu as pltpu
from jax.sharding import PartitionSpec as P

NFFT = 1024
TAPS = 4
SPEC = 64
CH_DEV = 4


def dft_table_np(channels):
    position = np.arange(NFFT, dtype=np.int64)
    channel = np.arange(channels, dtype=np.int64)
    phases = (position[:, None] * channel[None, :] % NFFT).astype(np.float64) * (2.0 * math.pi / NFFT)
    scaling = 0.5 / math.sqrt(NFFT)
    cosine = np.cos(phases) * scaling
    sine = np.sin(phases) * scaling
    real_rows = np.stack([cosine, -sine], axis=1)
    imag_rows = np.stack([sine, cosine], axis=1)
    table = np.stack([real_rows, imag_rows], axis=0)
    table = table.transpose(2, 3, 0, 1).reshape(2 * channels, 2 * NFFT)
    return jnp.asarray(table, dtype=jnp.bfloat16)


LANES = 128


def pfb_dft_body(g_hbm, taps_hbm, s_hbm, tab_hbm, o_ref, g_ref, taps_ref, sbuf, vbuf, tab_buf, f_ref, sems, after_start):
    inputs_here, nsamp = s_hbm.shape[1], s_hbm.shape[2]
    frames = nsamp // NFFT
    first = SPEC // 2 + TAPS - 1
    split = first * NFFT
    blocks = NFFT // LANES
    channels = tab_hbm.shape[0] // 2
    parts = []
    for p in range(2):
        head = pltpu.make_async_copy(
            s_hbm.at[p, :, pl.ds(0, split)], sbuf.at[p, :, pl.ds(0, split)], sems.at[2 * p]
        )
        tail = pltpu.make_async_copy(
            s_hbm.at[p, :, pl.ds(split, nsamp - split)],
            sbuf.at[p, :, pl.ds(split, nsamp - split)],
            sems.at[2 * p + 1],
        )
        head.start()
        tail.start()
        parts.append((head, tail))
    tab_cp = pltpu.make_async_copy(tab_hbm, tab_buf, sems.at[4])
    tab_cp.start()
    g_cp = pltpu.make_async_copy(g_hbm, g_ref, sems.at[5])
    g_cp.start()
    taps_cp = pltpu.make_async_copy(taps_hbm, taps_ref, sems.at[6])
    taps_cp.start()
    after_start()
    g_cp.wait()
    taps_cp.wait()

    row = lax.broadcasted_iota(jnp.int32, (inputs_here, NFFT), 0)
    scale = jnp.zeros((inputs_here, NFFT), jnp.float32)
    for i in range(inputs_here):
        scale = jnp.where(row == i, g_ref[i] * 0.25, scale)

    def volts(p, lo, hi):
        def body(j, carry):
            start = pl.multiple_of(j * NFFT, NFFT)
            vbuf[p, j] = sbuf[p, :, pl.ds(start, NFFT)].astype(jnp.float32) * scale
            return carry

        lax.fori_loop(lo, hi, body, 0)

    def filt(p, lo, hi):
        def body(m, carry):
            total = vbuf[p, m] * taps_ref[0:1, :]
            for t in range(1, TAPS):
                total = total + vbuf[p, m + t] * taps_ref[t : t + 1, :]
            rows = pl.ds(pl.multiple_of(m * inputs_here, inputs_here), inputs_here)
            for b in range(blocks):
                f_ref[p * blocks + b, rows, :] = total[:, b * LANES : (b + 1) * LANES]
            return carry

        lax.fori_loop(lo, hi, body, 0)

    for p in range(2):
        head, tail = parts[p]
        head.wait()
        volts(p, 0, first)
        filt(p, 0, SPEC // 2)
        tail.wait()
        volts(p, first, frames)
        filt(p, SPEC // 2, SPEC)

    tab_cp.wait()
    for i in range(inputs_here):
        lhs = jnp.concatenate(
            [f_ref[b, pl.ds(i, SPEC, stride=inputs_here), :] for b in range(2 * blocks)], axis=1
        ).astype(jnp.bfloat16)
        prod = lax.dot_general(
            tab_buf[...], lhs, (((1,), (1,)), ((), ())), preferred_element_type=jnp.float32
        )
        val = jnp.concatenate([prod[:channels], prod[channels:]], axis=1)
        o_ref[pl.ds(i, channels, stride=inputs_here), :] = val


MESH = pl.DeviceIdType.MESH


def fused_kernel(
    g_hbm, taps_hbm, s_hbm, tab_hbm, row_ref, col_ref,
    g_ref, taps_ref, sbuf, vbuf, tab_buf, f_ref, o_scr, spec_ref, relay_buf, pfb_sems,
    send1, recv1, own_sem, sends, recva, recvb, recvc, recvd, recve, recvf, local_sem,
):
    nf = spec_ref.shape[0]
    f = lax.axis_index("freq")
    r = lax.axis_index("row")
    c = lax.axis_index("col")
    k = c % 2
    h = c // 2
    sib = c + 1 - 2 * k
    cross_c = 2 * r + h
    crossing = h != r
    relay_target = jnp.logical_or(c == 1, c == 2)
    fan_target = jnp.logical_not(relay_target)
    relay_dest = 2 - k
    relay_src = 2 * r + 2 - c
    side_source = k == 1
    side_relay = jnp.logical_not(crossing)
    side_target = fan_target
    side_dest = 2 * (1 - r) + h
    side_from = 2 * k + 1
    side_to = 3 - 3 * k
    side_target_src = 2 * (1 - r) + 1 - h
    base = 2 * (1 - h)

    def greet_all():
        barrier = pltpu.get_barrier_semaphore()

        def greet_freq(d, carry):
            pl.semaphore_signal(barrier, inc=1, device_id=((f + d) % nf, r, c), device_id_type=MESH)
            return carry

        lax.fori_loop(1, nf, greet_freq, 0)
        pl.semaphore_signal(barrier, inc=1, device_id=(f, r, sib), device_id_type=MESH)
        pl.semaphore_signal(barrier, inc=1, device_id=(f, 1 - r, cross_c), device_id_type=MESH)

        @pl.when(crossing)
        def _():
            for e in range(2):
                pl.semaphore_signal(barrier, inc=1, device_id=(f, 1 - r, 2 * k + e), device_id_type=MESH)
            pl.semaphore_signal(barrier, inc=1, device_id=(f, 1 - r, relay_dest), device_id_type=MESH)

        @pl.when(relay_target)
        def _():
            pl.semaphore_signal(barrier, inc=1, device_id=(f, 1 - r, relay_src), device_id_type=MESH)

        @pl.when(side_source)
        def _():
            pl.semaphore_signal(barrier, inc=1, device_id=(f, 1 - r, side_dest), device_id_type=MESH)

        @pl.when(side_relay)
        def _():
            pl.semaphore_signal(barrier, inc=1, device_id=(f, 1 - r, side_from), device_id_type=MESH)
            pl.semaphore_signal(barrier, inc=1, device_id=(f, 1 - r, side_to), device_id_type=MESH)

        @pl.when(side_target)
        def _():
            pl.semaphore_signal(barrier, inc=1, device_id=(f, 1 - r, side_target_src), device_id_type=MESH)


    barrier = pltpu.get_barrier_semaphore()
    pfb_dft_body(
        g_hbm, taps_hbm, s_hbm, tab_hbm, o_scr, g_ref, taps_ref, sbuf, vbuf, tab_buf, f_ref,
        pfb_sems, greet_all,
    )
    spec_ref[...] = o_scr[...].astype(spec_ref.dtype).reshape(spec_ref.shape)

    expected = (
        (nf - 1) + 2 + 3 * crossing.astype(jnp.int32) + relay_target.astype(jnp.int32)
        + side_source.astype(jnp.int32) + 2 * side_relay.astype(jnp.int32)
        + side_target.astype(jnp.int32)
    )
    pl.semaphore_wait(barrier, expected)

    own = pltpu.make_async_copy(spec_ref.at[f], row_ref.at[c, f], own_sem)
    own.start()

    def freq_copy(d):
        dest = (f + d) % nf
        return pltpu.make_async_remote_copy(
            src_ref=spec_ref.at[dest],
            dst_ref=row_ref.at[c, f],
            send_sem=send1.at[d],
            recv_sem=recv1.at[f],
            device_id=(dest, r, c),
            device_id_type=MESH,
        )

    def send_freq(d, carry):
        freq_copy(d).start()
        return carry

    lax.fori_loop(1, nf, send_freq, 0)

    def recv_freq(d, carry):
        src = (f + nf - d) % nf
        pltpu.make_async_remote_copy(
            src_ref=spec_ref.at[src],
            dst_ref=row_ref.at[c, src],
            send_sem=send1.at[d],
            recv_sem=recv1.at[src],
            device_id=(src, r, c),
            device_id_type=MESH,
        ).wait_recv()
        return carry

    lax.fori_loop(1, nf, recv_freq, 0)
    own.wait()

    to_sib = pltpu.make_async_remote_copy(
        src_ref=row_ref.at[c],
        dst_ref=row_ref.at[c],
        send_sem=sends.at[0],
        recv_sem=recva,
        device_id=(f, r, sib),
        device_id_type=MESH,
    )
    to_sib.start()
    to_cross = pltpu.make_async_remote_copy(
        src_ref=row_ref.at[c],
        dst_ref=col_ref.at[k],
        send_sem=sends.at[1],
        recv_sem=recvb.at[k],
        device_id=(f, 1 - r, cross_c),
        device_id_type=MESH,
    )
    to_cross.start()

    def side_copy():
        return pltpu.make_async_remote_copy(
            src_ref=row_ref.at[c],
            dst_ref=relay_buf,
            send_sem=sends.at[2],
            recv_sem=recve,
            device_id=(f, 1 - r, side_dest),
            device_id_type=MESH,
        )

    def relay_copy():
        return pltpu.make_async_remote_copy(
            src_ref=col_ref.at[0],
            dst_ref=row_ref.at[2 * k],
            send_sem=sends.at[3],
            recv_sem=recvc,
            device_id=(f, 1 - r, relay_dest),
            device_id_type=MESH,
        )

    def side_relay_copy():
        return pltpu.make_async_remote_copy(
            src_ref=relay_buf,
            dst_ref=row_ref.at[2 * k + 1],
            send_sem=sends.at[4],
            recv_sem=recvf,
            device_id=(f, 1 - r, side_to),
            device_id_type=MESH,
        )

    def fan_copy(slot):
        return pltpu.make_async_remote_copy(
            src_ref=row_ref.at[slot],
            dst_ref=row_ref.at[slot],
            send_sem=sends.at[5],
            recv_sem=recvd,
            device_id=(f, r, sib),
            device_id_type=MESH,
        )

    mine = jnp.where(relay_target, 0, 1)

    @pl.when(side_source)
    def _():
        side_copy().start()

    @pl.when(crossing)
    def _():
        pltpu.make_async_remote_copy(
            src_ref=row_ref.at[0],
            dst_ref=col_ref.at[0],
            send_sem=sends.at[1],
            recv_sem=recvb.at[0],
            device_id=(f, 1 - r, 2 * k),
            device_id_type=MESH,
        ).wait_recv()
        relay_copy().start()

    @pl.when(side_relay)
    def _():
        pltpu.make_async_remote_copy(
            src_ref=row_ref.at[c],
            dst_ref=relay_buf,
            send_sem=sends.at[2],
            recv_sem=recve,
            device_id=(f, 1 - r, side_from),
            device_id_type=MESH,
        ).wait_recv()
        side_relay_copy().start()

    @pl.when(relay_target)
    def _():
        pltpu.make_async_remote_copy(
            src_ref=col_ref.at[0],
            dst_ref=row_ref.at[base],
            send_sem=sends.at[3],
            recv_sem=recvc,
            device_id=(f, 1 - r, relay_src),
            device_id_type=MESH,
        ).wait_recv()

    @pl.when(side_target)
    def _():
        pltpu.make_async_remote_copy(
            src_ref=relay_buf,
            dst_ref=row_ref.at[base + 1],
            send_sem=sends.at[4],
            recv_sem=recvf,
            device_id=(f, 1 - r, side_target_src),
            device_id_type=MESH,
        ).wait_recv()

    fan_copy(base + mine).start()
    fan_copy(base + 1 - mine).wait_recv()

    pltpu.make_async_remote_copy(
        src_ref=row_ref.at[sib],
        dst_ref=row_ref.at[sib],
        send_sem=sends.at[0],
        recv_sem=recva,
        device_id=(f, r, sib),
        device_id_type=MESH,
    ).wait_recv()

    @pl.when(crossing)
    def _():
        pltpu.make_async_remote_copy(
            src_ref=row_ref.at[1],
            dst_ref=col_ref.at[1],
            send_sem=sends.at[1],
            recv_sem=recvb.at[1],
            device_id=(f, 1 - r, 2 * k + 1),
            device_id_type=MESH,
        ).wait_recv()

    @pl.when(jnp.logical_not(crossing))
    def _():
        half = pltpu.make_async_copy(row_ref.at[pl.ds(2 * k, 2)], col_ref, local_sem)
        half.start()
        half.wait()

    def wait_send_freq(d, carry):
        freq_copy(d).wait_send()
        return carry

    lax.fori_loop(1, nf, wait_send_freq, 0)
    to_sib.wait_send()
    to_cross.wait_send()
    fan_copy(base + mine).wait_send()

    @pl.when(side_source)
    def _():
        side_copy().wait_send()

    @pl.when(crossing)
    def _():
        relay_copy().wait_send()

    @pl.when(side_relay)
    def _():
        side_relay_copy().wait_send()


def fused_call(samples, gains, taps, table):
    inputs_here, nsamp = samples.shape[1], samples.shape[2]
    channels = table.shape[0] // 2
    frames = nsamp // NFFT
    nf = channels // CH_DEV
    rows = CH_DEV * inputs_here
    width = 2 * SPEC
    ncol = lax.axis_size("col")
    vmem = pltpu.MemorySpace.VMEM
    return pl.pallas_call(
        fused_kernel,
        out_shape=(
            jax.ShapeDtypeStruct((ncol, nf, rows, width), jnp.bfloat16),
            jax.ShapeDtypeStruct((2, nf, rows, width), jnp.bfloat16),
        ),
        in_specs=[pl.BlockSpec(memory_space=pl.ANY)] * 4,
        out_specs=(pl.BlockSpec(memory_space=vmem), pl.BlockSpec(memory_space=vmem)),
        scratch_shapes=[
            pltpu.SMEM((inputs_here,), jnp.float32),
            pltpu.VMEM((TAPS, NFFT), jnp.float32),
            pltpu.VMEM((2, inputs_here, nsamp), jnp.int32),
            pltpu.VMEM((2, frames, inputs_here, NFFT), jnp.float32),
            pltpu.VMEM(table.shape, jnp.bfloat16),
            pltpu.VMEM((2 * NFFT // LANES, SPEC * inputs_here, LANES), jnp.float32),
            pltpu.VMEM((channels * inputs_here, width), jnp.float32),
            pltpu.VMEM((nf, rows, width), jnp.bfloat16),
            pltpu.VMEM((nf, rows, width), jnp.bfloat16),
            pltpu.SemaphoreType.DMA((7,)),
            pltpu.SemaphoreType.DMA((nf,)),
            pltpu.SemaphoreType.DMA((nf,)),
            pltpu.SemaphoreType.DMA,
            pltpu.SemaphoreType.DMA((6,)),
            pltpu.SemaphoreType.DMA,
            pltpu.SemaphoreType.DMA((2,)),
            pltpu.SemaphoreType.DMA,
            pltpu.SemaphoreType.DMA,
            pltpu.SemaphoreType.DMA,
            pltpu.SemaphoreType.DMA,
            pltpu.SemaphoreType.DMA,
        ],
        compiler_params=pltpu.CompilerParams(
            collective_id=0, has_side_effects=True, vmem_limit_bytes=63 * 1024 * 1024
        ),
    )(gains, taps, samples, table)


def local(samples, input_gains, filter_taps):
    nf = lax.axis_size("freq")
    channels = CH_DEV * nf
    inputs_here = samples.shape[1]
    table = dft_table_np(channels)
    row_blk, col_blk = fused_call(samples, input_gains, filter_taps, table)
    return visibilities(row_blk, col_blk)


def vis_kernel(row_ref, col_ref, vr_ref, vi_ref, a_scr, b_scr):
    kk = pl.program_id(0)
    groups = row_ref.shape[2] // CH_DEV
    pair = pl.multiple_of((kk // 2) * 2 * groups, 2 * groups)
    rows = row_ref[:, :, pl.ds(pair, 2 * groups), :].astype(jnp.float32)
    cols = col_ref[:, :, pl.ds(pair, 2 * groups), :].astype(jnp.float32)
    for j in range(2):

        @pl.when(kk % 2 == j)
        def _():
            a = rows[:, :, j * groups : (j + 1) * groups, :]
            a_scr[...] = (a.reshape(-1, a.shape[-1]) * (1.0 / SPEC)).astype(a_scr.dtype)
            b = cols[:, :, j * groups : (j + 1) * groups, :]
            b = b.reshape(-1, b.shape[-1])
            b_scr[0] = b.astype(b_scr.dtype)
            b_scr[1] = jnp.concatenate([-b[:, SPEC:], b[:, :SPEC]], axis=1).astype(b_scr.dtype)

    a = a_scr[...]
    dims = (((1,), (1,)), ((), ()))
    vr = lax.dot_general(a, b_scr[0], dims, preferred_element_type=jnp.float32)
    vr_ref[0] = vr.astype(vr_ref.dtype)
    vi = lax.dot_general(a, b_scr[1], dims, preferred_element_type=jnp.float32)
    vi_ref[0] = vi.astype(vi_ref.dtype)


def visibilities(row_blk, col_blk):
    nrow = row_blk.shape[0] * row_blk.shape[1] * row_blk.shape[2] // CH_DEV
    ncolumn = col_blk.shape[0] * col_blk.shape[1] * col_blk.shape[2] // CH_DEV
    width = row_blk.shape[3]
    out = jax.ShapeDtypeStruct((CH_DEV, nrow, ncolumn), jnp.bfloat16)
    return pl.pallas_call(
        vis_kernel,
        grid=(CH_DEV,),
        out_shape=(out, out),
        in_specs=[
            pl.BlockSpec(row_blk.shape, lambda k: (0, 0, 0, 0)),
            pl.BlockSpec(col_blk.shape, lambda k: (0, 0, 0, 0)),
        ],
        out_specs=(
            pl.BlockSpec((1, nrow, ncolumn), lambda k: (k, 0, 0)),
            pl.BlockSpec((1, nrow, ncolumn), lambda k: (k, 0, 0)),
        ),
        scratch_shapes=[
            pltpu.VMEM((nrow, width), jnp.bfloat16),
            pltpu.VMEM((2, ncolumn, width), jnp.bfloat16),
        ],
        compiler_params=pltpu.CompilerParams(vmem_limit_bytes=63 * 1024 * 1024),
    )(row_blk, col_blk)


def solution(mesh):
    placed = (P(None, ("row", "col", "freq"), None), P(("row", "col", "freq")), P())
    return jax.shard_map(
        local,
        mesh=mesh,
        in_specs=placed,
        out_specs=(P("freq", "row", "col"), P("freq", "row", "col")),
        check_vma=False,
    )
```

```python
import math

import numpy as np

import jax
import jax.numpy as jnp
from jax import lax
from jax.experimental import pallas as pl
from jax.experimental.pallas import tpu as pltpu
from jax.sharding import PartitionSpec as P

NFFT = 1024
TAPS = 4
SPEC = 64
CH_DEV = 4


def dft_table_np(channels):
    position = np.arange(NFFT, dtype=np.int64)
    channel = np.arange(channels, dtype=np.int64)
    phases = (position[:, None] * channel[None, :] % NFFT).astype(np.float64) * (2.0 * math.pi / NFFT)
    scaling = 0.5 / math.sqrt(NFFT)
    cosine = np.cos(phases) * scaling
    sine = np.sin(phases) * scaling
    real_rows = np.stack([cosine, -sine], axis=1)
    imag_rows = np.stack([sine, cosine], axis=1)
    table = np.stack([real_rows, imag_rows], axis=0)
    table = table.transpose(2, 3, 0, 1).reshape(2 * channels, 2 * NFFT)
    return jnp.asarray(table, dtype=jnp.bfloat16)


LANES = 128


def pfb_dft_body(g_hbm, taps_hbm, s_hbm, tab_hbm, o_ref, g_ref, taps_ref, sbuf, vbuf, tab_buf, f_ref, sems, after_start):
    inputs_here, nsamp = s_hbm.shape[1], s_hbm.shape[2]
    frames = nsamp // NFFT
    first = SPEC // 2 + TAPS - 1
    split = first * NFFT
    blocks = NFFT // LANES
    channels = tab_hbm.shape[0] // 2
    parts = []
    for p in range(2):
        head = pltpu.make_async_copy(
            s_hbm.at[p, :, pl.ds(0, split)], sbuf.at[p, :, pl.ds(0, split)], sems.at[2 * p]
        )
        tail = pltpu.make_async_copy(
            s_hbm.at[p, :, pl.ds(split, nsamp - split)],
            sbuf.at[p, :, pl.ds(split, nsamp - split)],
            sems.at[2 * p + 1],
        )
        head.start()
        tail.start()
        parts.append((head, tail))
    tab_cp = pltpu.make_async_copy(tab_hbm, tab_buf, sems.at[4])
    tab_cp.start()
    g_cp = pltpu.make_async_copy(g_hbm, g_ref, sems.at[5])
    g_cp.start()
    taps_cp = pltpu.make_async_copy(taps_hbm, taps_ref, sems.at[6])
    taps_cp.start()
    after_start()
    g_cp.wait()
    taps_cp.wait()

    row = lax.broadcasted_iota(jnp.int32, (inputs_here, NFFT), 0)
    scale = jnp.zeros((inputs_here, NFFT), jnp.float32)
    for i in range(inputs_here):
        scale = jnp.where(row == i, g_ref[i] * 0.25, scale)

    def volts(p, lo, hi):
        def body(j, carry):
            start = pl.multiple_of(j * NFFT, NFFT)
            vbuf[p, j] = sbuf[p, :, pl.ds(start, NFFT)].astype(jnp.float32) * scale
            return carry

        lax.fori_loop(lo, hi, body, 0)

    coef = [jnp.broadcast_to(taps_ref[t : t + 1, :], (inputs_here, NFFT)) for t in range(TAPS)]

    def filt(p, lo, hi):
        def body(m, carry):
            total = vbuf[p, m] * coef[0]
            for t in range(1, TAPS):
                total = total + vbuf[p, m + t] * coef[t]
            rows = pl.ds(pl.multiple_of(m * inputs_here, inputs_here), inputs_here)
            for b in range(blocks):
                f_ref[p * blocks + b, rows, :] = total[:, b * LANES : (b + 1) * LANES]
            return carry

        lax.fori_loop(lo, hi, body, 0)

    for p in range(2):
        head, tail = parts[p]
        head.wait()
        volts(p, 0, first)
        filt(p, 0, SPEC // 2)
        tail.wait()
        volts(p, first, frames)
        filt(p, SPEC // 2, SPEC)

    tab_cp.wait()
    for i in range(inputs_here):
        lhs = jnp.concatenate(
            [f_ref[b, pl.ds(i, SPEC, stride=inputs_here), :] for b in range(2 * blocks)], axis=1
        ).astype(jnp.bfloat16)
        prod = lax.dot_general(
            tab_buf[...], lhs, (((1,), (1,)), ((), ())), preferred_element_type=jnp.float32
        )
        val = jnp.concatenate([prod[:channels], prod[channels:]], axis=1)
        o_ref[pl.ds(i, channels, stride=inputs_here), :] = val


MESH = pl.DeviceIdType.MESH


def fused_kernel(
    g_hbm, taps_hbm, s_hbm, tab_hbm, row_ref, col_ref,
    g_ref, taps_ref, sbuf, vbuf, tab_buf, f_ref, o_scr, spec_ref, relay_buf, pfb_sems,
    send1, recv1, own_sem, sends, recva, recvb, recvc, recvd, recve, recvf, local_sem,
):
    nf = spec_ref.shape[0]
    f = lax.axis_index("freq")
    r = lax.axis_index("row")
    c = lax.axis_index("col")
    k = c % 2
    h = c // 2
    sib = c + 1 - 2 * k
    cross_c = 2 * r + h
    crossing = h != r
    relay_target = jnp.logical_or(c == 1, c == 2)
    fan_target = jnp.logical_not(relay_target)
    relay_dest = 2 - k
    relay_src = 2 * r + 2 - c
    side_source = k == 1
    side_relay = jnp.logical_not(crossing)
    side_target = fan_target
    side_dest = 2 * (1 - r) + h
    side_from = 2 * k + 1
    side_to = 3 - 3 * k
    side_target_src = 2 * (1 - r) + 1 - h
    base = 2 * (1 - h)

    def greet_all():
        barrier = pltpu.get_barrier_semaphore()

        def greet_freq(d, carry):
            pl.semaphore_signal(barrier, inc=1, device_id=((f + d) % nf, r, c), device_id_type=MESH)
            return carry

        lax.fori_loop(1, nf, greet_freq, 0)
        pl.semaphore_signal(barrier, inc=1, device_id=(f, r, sib), device_id_type=MESH)
        pl.semaphore_signal(barrier, inc=1, device_id=(f, 1 - r, cross_c), device_id_type=MESH)

        @pl.when(crossing)
        def _():
            for e in range(2):
                pl.semaphore_signal(barrier, inc=1, device_id=(f, 1 - r, 2 * k + e), device_id_type=MESH)
            pl.semaphore_signal(barrier, inc=1, device_id=(f, 1 - r, relay_dest), device_id_type=MESH)

        @pl.when(relay_target)
        def _():
            pl.semaphore_signal(barrier, inc=1, device_id=(f, 1 - r, relay_src), device_id_type=MESH)

        @pl.when(side_source)
        def _():
            pl.semaphore_signal(barrier, inc=1, device_id=(f, 1 - r, side_dest), device_id_type=MESH)

        @pl.when(side_relay)
        def _():
            pl.semaphore_signal(barrier, inc=1, device_id=(f, 1 - r, side_from), device_id_type=MESH)
            pl.semaphore_signal(barrier, inc=1, device_id=(f, 1 - r, side_to), device_id_type=MESH)

        @pl.when(side_target)
        def _():
            pl.semaphore_signal(barrier, inc=1, device_id=(f, 1 - r, side_target_src), device_id_type=MESH)


    barrier = pltpu.get_barrier_semaphore()
    pfb_dft_body(
        g_hbm, taps_hbm, s_hbm, tab_hbm, o_scr, g_ref, taps_ref, sbuf, vbuf, tab_buf, f_ref,
        pfb_sems, greet_all,
    )
    spec_ref[...] = o_scr[...].astype(spec_ref.dtype).reshape(spec_ref.shape)

    expected = (
        (nf - 1) + 2 + 3 * crossing.astype(jnp.int32) + relay_target.astype(jnp.int32)
        + side_source.astype(jnp.int32) + 2 * side_relay.astype(jnp.int32)
        + side_target.astype(jnp.int32)
    )
    pl.semaphore_wait(barrier, expected)

    own = pltpu.make_async_copy(spec_ref.at[f], row_ref.at[c, f], own_sem)
    own.start()

    def freq_copy(d):
        dest = (f + d) % nf
        return pltpu.make_async_remote_copy(
            src_ref=spec_ref.at[dest],
            dst_ref=row_ref.at[c, f],
            send_sem=send1.at[d],
            recv_sem=recv1.at[f],
            device_id=(dest, r, c),
            device_id_type=MESH,
        )

    def send_freq(d, carry):
        freq_copy(d).start()
        return carry

    lax.fori_loop(1, nf, send_freq, 0)

    def recv_freq(d, carry):
        src = (f + nf - d) % nf
        pltpu.make_async_remote_copy(
            src_ref=spec_ref.at[src],
            dst_ref=row_ref.at[c, src],
            send_sem=send1.at[d],
            recv_sem=recv1.at[src],
            device_id=(src, r, c),
            device_id_type=MESH,
        ).wait_recv()
        return carry

    lax.fori_loop(1, nf, recv_freq, 0)
    own.wait()

    to_sib = pltpu.make_async_remote_copy(
        src_ref=row_ref.at[c],
        dst_ref=row_ref.at[c],
        send_sem=sends.at[0],
        recv_sem=recva,
        device_id=(f, r, sib),
        device_id_type=MESH,
    )
    to_sib.start()
    to_cross = pltpu.make_async_remote_copy(
        src_ref=row_ref.at[c],
        dst_ref=col_ref.at[k],
        send_sem=sends.at[1],
        recv_sem=recvb.at[k],
        device_id=(f, 1 - r, cross_c),
        device_id_type=MESH,
    )
    to_cross.start()

    def side_copy():
        return pltpu.make_async_remote_copy(
            src_ref=row_ref.at[c],
            dst_ref=relay_buf,
            send_sem=sends.at[2],
            recv_sem=recve,
            device_id=(f, 1 - r, side_dest),
            device_id_type=MESH,
        )

    def relay_copy():
        return pltpu.make_async_remote_copy(
            src_ref=col_ref.at[0],
            dst_ref=row_ref.at[2 * k],
            send_sem=sends.at[3],
            recv_sem=recvc,
            device_id=(f, 1 - r, relay_dest),
            device_id_type=MESH,
        )

    def side_relay_copy():
        return pltpu.make_async_remote_copy(
            src_ref=relay_buf,
            dst_ref=row_ref.at[2 * k + 1],
            send_sem=sends.at[4],
            recv_sem=recvf,
            device_id=(f, 1 - r, side_to),
            device_id_type=MESH,
        )

    def fan_copy(slot):
        return pltpu.make_async_remote_copy(
            src_ref=row_ref.at[slot],
            dst_ref=row_ref.at[slot],
            send_sem=sends.at[5],
            recv_sem=recvd,
            device_id=(f, r, sib),
            device_id_type=MESH,
        )

    mine = jnp.where(relay_target, 0, 1)

    @pl.when(side_source)
    def _():
        side_copy().start()

    @pl.when(crossing)
    def _():
        pltpu.make_async_remote_copy(
            src_ref=row_ref.at[0],
            dst_ref=col_ref.at[0],
            send_sem=sends.at[1],
            recv_sem=recvb.at[0],
            device_id=(f, 1 - r, 2 * k),
            device_id_type=MESH,
        ).wait_recv()
        relay_copy().start()

    @pl.when(side_relay)
    def _():
        pltpu.make_async_remote_copy(
            src_ref=row_ref.at[c],
            dst_ref=relay_buf,
            send_sem=sends.at[2],
            recv_sem=recve,
            device_id=(f, 1 - r, side_from),
            device_id_type=MESH,
        ).wait_recv()
        side_relay_copy().start()

    @pl.when(relay_target)
    def _():
        pltpu.make_async_remote_copy(
            src_ref=col_ref.at[0],
            dst_ref=row_ref.at[base],
            send_sem=sends.at[3],
            recv_sem=recvc,
            device_id=(f, 1 - r, relay_src),
            device_id_type=MESH,
        ).wait_recv()

    @pl.when(side_target)
    def _():
        pltpu.make_async_remote_copy(
            src_ref=relay_buf,
            dst_ref=row_ref.at[base + 1],
            send_sem=sends.at[4],
            recv_sem=recvf,
            device_id=(f, 1 - r, side_target_src),
            device_id_type=MESH,
        ).wait_recv()

    fan_copy(base + mine).start()
    fan_copy(base + 1 - mine).wait_recv()

    pltpu.make_async_remote_copy(
        src_ref=row_ref.at[sib],
        dst_ref=row_ref.at[sib],
        send_sem=sends.at[0],
        recv_sem=recva,
        device_id=(f, r, sib),
        device_id_type=MESH,
    ).wait_recv()

    @pl.when(crossing)
    def _():
        pltpu.make_async_remote_copy(
            src_ref=row_ref.at[1],
            dst_ref=col_ref.at[1],
            send_sem=sends.at[1],
            recv_sem=recvb.at[1],
            device_id=(f, 1 - r, 2 * k + 1),
            device_id_type=MESH,
        ).wait_recv()

    @pl.when(jnp.logical_not(crossing))
    def _():
        half = pltpu.make_async_copy(row_ref.at[pl.ds(2 * k, 2)], col_ref, local_sem)
        half.start()
        half.wait()

    def wait_send_freq(d, carry):
        freq_copy(d).wait_send()
        return carry

    lax.fori_loop(1, nf, wait_send_freq, 0)
    to_sib.wait_send()
    to_cross.wait_send()
    fan_copy(base + mine).wait_send()

    @pl.when(side_source)
    def _():
        side_copy().wait_send()

    @pl.when(crossing)
    def _():
        relay_copy().wait_send()

    @pl.when(side_relay)
    def _():
        side_relay_copy().wait_send()


def fused_call(samples, gains, taps, table):
    inputs_here, nsamp = samples.shape[1], samples.shape[2]
    channels = table.shape[0] // 2
    frames = nsamp // NFFT
    nf = channels // CH_DEV
    rows = CH_DEV * inputs_here
    width = 2 * SPEC
    ncol = lax.axis_size("col")
    vmem = pltpu.MemorySpace.VMEM
    return pl.pallas_call(
        fused_kernel,
        out_shape=(
            jax.ShapeDtypeStruct((ncol, nf, rows, width), jnp.bfloat16),
            jax.ShapeDtypeStruct((2, nf, rows, width), jnp.bfloat16),
        ),
        in_specs=[pl.BlockSpec(memory_space=pl.ANY)] * 4,
        out_specs=(pl.BlockSpec(memory_space=vmem), pl.BlockSpec(memory_space=vmem)),
        scratch_shapes=[
            pltpu.SMEM((inputs_here,), jnp.float32),
            pltpu.VMEM((TAPS, NFFT), jnp.float32),
            pltpu.VMEM((2, inputs_here, nsamp), jnp.int32),
            pltpu.VMEM((2, frames, inputs_here, NFFT), jnp.float32),
            pltpu.VMEM(table.shape, jnp.bfloat16),
            pltpu.VMEM((2 * NFFT // LANES, SPEC * inputs_here, LANES), jnp.float32),
            pltpu.VMEM((channels * inputs_here, width), jnp.float32),
            pltpu.VMEM((nf, rows, width), jnp.bfloat16),
            pltpu.VMEM((nf, rows, width), jnp.bfloat16),
            pltpu.SemaphoreType.DMA((7,)),
            pltpu.SemaphoreType.DMA((nf,)),
            pltpu.SemaphoreType.DMA((nf,)),
            pltpu.SemaphoreType.DMA,
            pltpu.SemaphoreType.DMA((6,)),
            pltpu.SemaphoreType.DMA,
            pltpu.SemaphoreType.DMA((2,)),
            pltpu.SemaphoreType.DMA,
            pltpu.SemaphoreType.DMA,
            pltpu.SemaphoreType.DMA,
            pltpu.SemaphoreType.DMA,
            pltpu.SemaphoreType.DMA,
        ],
        compiler_params=pltpu.CompilerParams(
            collective_id=0, has_side_effects=True, vmem_limit_bytes=63 * 1024 * 1024
        ),
    )(gains, taps, samples, table)


def local(samples, input_gains, filter_taps):
    nf = lax.axis_size("freq")
    channels = CH_DEV * nf
    inputs_here = samples.shape[1]
    table = dft_table_np(channels)
    row_blk, col_blk = fused_call(samples, input_gains, filter_taps, table)
    return visibilities(row_blk, col_blk)


def vis_kernel(row_ref, col_ref, vr_ref, vi_ref, a_scr, b_scr):
    kk = pl.program_id(0)
    groups = row_ref.shape[2] // CH_DEV
    pair = pl.multiple_of((kk // 2) * 2 * groups, 2 * groups)
    rows = row_ref[:, :, pl.ds(pair, 2 * groups), :].astype(jnp.float32)
    cols = col_ref[:, :, pl.ds(pair, 2 * groups), :].astype(jnp.float32)
    for j in range(2):

        @pl.when(kk % 2 == j)
        def _():
            a = rows[:, :, j * groups : (j + 1) * groups, :]
            a_scr[...] = (a.reshape(-1, a.shape[-1]) * (1.0 / SPEC)).astype(a_scr.dtype)
            b = cols[:, :, j * groups : (j + 1) * groups, :]
            b = b.reshape(-1, b.shape[-1])
            b_scr[0] = b.astype(b_scr.dtype)
            b_scr[1] = jnp.concatenate([-b[:, SPEC:], b[:, :SPEC]], axis=1).astype(b_scr.dtype)

    a = a_scr[...]
    dims = (((1,), (1,)), ((), ()))
    vr = lax.dot_general(a, b_scr[0], dims, preferred_element_type=jnp.float32)
    vr_ref[0] = vr.astype(vr_ref.dtype)
    vi = lax.dot_general(a, b_scr[1], dims, preferred_element_type=jnp.float32)
    vi_ref[0] = vi.astype(vi_ref.dtype)


def visibilities(row_blk, col_blk):
    nrow = row_blk.shape[0] * row_blk.shape[1] * row_blk.shape[2] // CH_DEV
    ncolumn = col_blk.shape[0] * col_blk.shape[1] * col_blk.shape[2] // CH_DEV
    width = row_blk.shape[3]
    out = jax.ShapeDtypeStruct((CH_DEV, nrow, ncolumn), jnp.bfloat16)
    return pl.pallas_call(
        vis_kernel,
        grid=(CH_DEV,),
        out_shape=(out, out),
        in_specs=[
            pl.BlockSpec(row_blk.shape, lambda k: (0, 0, 0, 0)),
            pl.BlockSpec(col_blk.shape, lambda k: (0, 0, 0, 0)),
        ],
        out_specs=(
            pl.BlockSpec((1, nrow, ncolumn), lambda k: (k, 0, 0)),
            pl.BlockSpec((1, nrow, ncolumn), lambda k: (k, 0, 0)),
        ),
        scratch_shapes=[
            pltpu.VMEM((nrow, width), jnp.bfloat16),
            pltpu.VMEM((2, ncolumn, width), jnp.bfloat16),
        ],
        compiler_params=pltpu.CompilerParams(vmem_limit_bytes=63 * 1024 * 1024),
    )(row_blk, col_blk)


def solution(mesh):
    placed = (P(None, ("row", "col", "freq"), None), P(("row", "col", "freq")), P())
    return jax.shard_map(
        local,
        mesh=mesh,
        in_specs=placed,
        out_specs=(P("freq", "row", "col"), P("freq", "row", "col")),
        check_vma=False,
    )
```
